32 devices in a mesh: gx: 8 (over y, x, core), gy: 4 (over z).
Axes of the slice: x: 2, y: 2, z: 4, core: 2. Of those that a mesh axis runs over, the one named last changes fastest.
Arguments:
- states: bfloat16 [512, 2048], P('gx'), may hold values from -6 to 6
- attn_gain: bfloat16 [2048], replicated, may hold values from 0.099609375 to 1.8984375
- w_qkv: bfloat16 [2048, 5120], P(None, 'gy'), may hold values from -0.125 to 0.125
- q_gain: bfloat16 [128], replicated, may hold values from 0.099609375 to 1.8984375
- k_gain: bfloat16 [128], replicated, may hold values from 0.099609375 to 1.8984375
- cache_k: bfloat16 [8, 4096, 512], P('gx', 'gy'), may hold values from -400 to 400
- cache_v: bfloat16 [8, 4096, 512], P('gx', 'gy'), may hold values from -6 to 6
- cache_len: int32 [8], P('gx'), may hold values from 256 to 4096, as said below
- tree_mask: int32 [8, 64, 64], P('gx'), may hold values from 0 to 1, as said below
- w_o: bfloat16 [4096, 2048], P(None, 'gy'), may hold values from -0.09375 to 0.09375
- ffn_gain: bfloat16 [2048], P('gy'), may hold values from 0.099609375 to 1.8984375
- routing: int32 [512, 8], replicated, may hold values from 0 to 63, all different within a row; in each aligned block of 64 rows (0 to 63, 64 to 127, ...) at most 12 rows name the same one
- route_weight: float32 [512, 8], replicated, may hold values from 0.05 to 0.5
- w_in: bfloat16 [64, 2048, 1536], P('gx', 'gy'), may hold values from -0.125 to 0.125
- w_down: bfloat16 [64, 768, 2048], P('gx', None, 'gy'), may hold values from -0.21875 to 0.21875
- accept: int32 [8, 8, 64], P('gx'), may hold values from 0 to 1, as said below
Outputs:
- layer_out: bfloat16 [512, 2048], P('gx', 'gy')
- accepted_kv: bfloat16 [8, 8, 1024], P('gx')
The draws below stay inside these ranges and needn't reach their ends.
Inputs may be any that keep to these rules, and one draw needn't show every extreme that they name: `cache_len`: each request's cache holds keys at positions below its length; some request fills all 4096 positions. tree_mask[r, t, u] is 1 exactly when draft token u is t or an ancestor of t in request r's tree; every token's parent has a lower index and token 0 is the root. Row a of accept[r] is the one-hot of the token at depth a on one path from the root of request r's tree; the path is longer than 8 tokens. `routing`: each row names 8 different experts; in each aligned block of 64 rows no expert is named by more than 12 rows.
All inputs are finite; a program needn't handle non-finite values.
Results may differ from the reference program's by a relative error of at most 0.014.
Values may be sent and summed in bfloat16 or wider, within the bound.
A program may use at most 128 MiB of HBM per device.

```python
import math
import jax
import jax.numpy as jnp
import numpy as np
from jax import lax

D = 2048
HEADS = 32
KVH = 4
HD = 128
FF = 768
TOP = 8
TREE = 64
CACHE = 4096
ACC = 8
R_DEV = 1
REQUESTS = 8
TOKENS = 512
EXPERTS = 64
QKV = 5120
MOST = 12
N_GX = 8


def tree_parents(key):
    offsets = jax.random.randint(jax.random.fold_in(key, 7), (REQUESTS, TREE), 1, 4)
    parents = jnp.maximum(jnp.arange(TREE, dtype=jnp.int32)[None, :] - offsets, 0)
    return parents.astype(jnp.int32)


def ancestor_mask(parents):
    columns = jnp.arange(TREE, dtype=jnp.int32)

    def climb(step, state):
        marks, nodes = state
        marks = jnp.maximum(marks, (nodes[:, :, None] == columns[None, None, :]).astype(jnp.int32))
        nodes = jnp.take_along_axis(parents, nodes, axis=1)
        return (marks, nodes)
    start_nodes = jnp.broadcast_to(columns[None, :], (REQUESTS, TREE))
    return lax.fori_loop(0, TREE, climb, (jnp.zeros((REQUESTS, TREE, TREE), jnp.int32), start_nodes))[0]


def draw_tree_mask(key, part):
    return ancestor_mask(tree_parents(key))


def draw_accept(key, part):
    marks = ancestor_mask(tree_parents(key))
    leaves = TREE - 1 - jax.random.randint(jax.random.fold_in(key, 11), (REQUESTS,), 0, TREE // 8 + 1)
    path_row = jnp.take_along_axis(marks, leaves[:, None, None], axis=1)[:, 0, :]
    order = jnp.cumsum(path_row, 1)
    wanted = jnp.arange(ACC, dtype=jnp.int32)[None, :, None] + 1
    onehot = (path_row[:, None, :] == 1) & (order[:, None, :] == wanted)
    return onehot.astype(jnp.int32)


def draw_cache_len(key, part):
    lengths = jax.random.randint(jax.random.fold_in(key, 3), (REQUESTS,), CACHE // 16, CACHE + 1)
    longest = jax.random.randint(jax.random.fold_in(key, 5), (), 0, REQUESTS)
    return jnp.where(jnp.arange(REQUESTS) == longest, CACHE, lengths).astype(jnp.int32)


def draw_cache_k(key, part):
    shape = (REQUESTS, CACHE, KVH * HD)
    values = jax.random.truncated_normal(jax.random.fold_in(key, 26), -6.0, 6.0, shape, jnp.float32)
    return values.astype(jnp.bfloat16)


def shard_levels(key, dims, shards, smallest, largest):
    level = 1.0
    for axis_at, blocks in shards:
        draws = jax.random.uniform(jax.random.fold_in(jax.random.fold_in(key, 6), axis_at), (blocks,), jnp.float32, smallest / len(shards), largest / len(shards))
        level = level * jnp.repeat(jnp.exp(draws), dims[axis_at] // blocks).reshape((-1,) + (1,) * (len(dims) - 1 - axis_at))
    return level


def routed_block(stream_key, own, number, rows, number_of, top, bound, lean):
    ranking = jax.random.permutation(stream_key, number_of)
    crowded, ordinary = portions_of(number_of, rows * top, bound, lean, True), portions_of(number_of, rows * top, bound, lean, False)
    places = jnp.arange(number_of)

    def named(sizes, turn):
        used = int((sizes > 0).sum())
        fixed = max(1, used // 4)
        passed = fixed + (places - fixed + turn * (used - fixed)) % max(1, number_of - fixed)
        return jnp.zeros((number_of,), jnp.int32).at[ranking[jnp.where(places < fixed, places, passed)]].set(jnp.asarray(sizes, jnp.int32))

    sizes = jnp.where(number % 4 == 0, named(crowded, number // 4), named(ordinary, number - number // 4 - 1))
    mixed = jax.random.permutation(jax.random.fold_in(own, 3), number_of)
    giver, sink = mixed[0:number_of // 2 * 2:2], mixed[1:number_of // 2 * 2:2]
    room = jnp.minimum(sizes[giver] - 1, bound - sizes[sink]) // 2
    room = jnp.where((giver == ranking[0]) | (sink == ranking[0]) | (sizes[sink] == 0), 0, jnp.maximum(room, 0))
    passed = jax.random.randint(jax.random.fold_in(own, 4), (number_of // 2,), 0, 1 << 20) % (room + 1)
    sizes = sizes.at[giver].add(-passed).at[sink].add(passed)
    members = jnp.searchsorted(jnp.cumsum(sizes), jnp.arange(rows * top), side="right").astype(jnp.int32)
    listing = members.reshape(top, rows).T
    listing = listing[jax.random.permutation(jax.random.fold_in(own, 1), rows)]
    turn = jax.random.randint(jax.random.fold_in(own, 2), (rows, 1), 0, top)
    return jnp.take_along_axis(listing, (jnp.arange(top)[None, :] + turn) % top, axis=1)


def portions_of(count, total, most, slope, full):
    weights = [(1 << 20) // math.isqrt(rank ** slope) + 1 for rank in range(1, count + 1)]
    largest = most if full else min(most, max(-(-total // count), total * weights[0] // sum(weights)))
    least = 1 if total - largest >= count - 1 else 0
    given, surplus = [largest] + [least] * (count - 1), total - largest - least * (count - 1)
    while surplus > 0:
        movable = [i for i in range(1, count) if given[i] < largest] or [i for i in range(1, count) if given[i] < most]
        pool, budget = sum([weights[i] for i in movable]), surplus
        for i in movable:
            addition = min(most - given[i], max(1, budget * weights[i] // pool), surplus)
            given[i] = given[i] + addition
            surplus = surplus - addition
    return np.array(given)


def bell_draw(rng, shape, scale, limit, split=(), held_as=jnp.bfloat16):
    entries = scale * jax.random.normal(rng, shape, jnp.float32)
    if split:
        entries = entries * shard_levels(rng, shape, split, -0.22, 0.18)
    return jnp.clip(entries, -limit, limit).astype(held_as)


def setup_inputs(seed: int = 0) -> dict:
    splits = jax.random.split(jax.random.key(seed), 17)
    states = bell_draw(splits[0], (TOKENS, D), 1.0, 6.0, ((0, 8),))
    attn_gain = jnp.clip(1.0 + 0.18 * jax.random.normal(splits[1], (D,), jnp.float32), 0.099609375, 1.8984375).astype(jnp.bfloat16)
    w_qkv = bell_draw(splits[2], (D, QKV), D ** -0.5, 0.125, ((1, 4),))
    q_gain = jnp.clip(1.0 + 0.18 * jax.random.normal(splits[3], (HD,), jnp.float32), 0.099609375, 1.8984375).astype(jnp.bfloat16)
    k_gain = jnp.clip(1.0 + 0.18 * jax.random.normal(splits[4], (HD,), jnp.float32), 0.099609375, 1.8984375).astype(jnp.bfloat16)
    cache_k = draw_cache_k(jax.random.fold_in(splits[16], 71), 0)
    cache_v = bell_draw(splits[6], (REQUESTS, CACHE, KVH * HD), 1.0, 6.0, ((0, 8), (1, 4)))
    cache_len = draw_cache_len(jax.random.fold_in(splits[16], 71), 0)
    tree_mask = draw_tree_mask(jax.random.fold_in(splits[16], 71), 0)
    w_o = bell_draw(splits[9], (HEADS * HD, D), (HEADS * HD) ** -0.5, 0.09375, ((1, 4),))
    ffn_gain = jnp.clip(1.0 + 0.18 * jax.random.normal(splits[10], (D,), jnp.float32), 0.099609375, 1.8984375).astype(jnp.bfloat16)
    routing_keys = jax.random.split(jax.random.fold_in(splits[11], 1), TOKENS // (R_DEV * TREE))
    routing_turns = jax.random.permutation(jax.random.fold_in(splits[11], 3), TOKENS // (R_DEV * TREE))
    routing = jax.vmap(lambda own, number: routed_block(jax.random.fold_in(splits[11], 2), own, number, R_DEV * TREE, EXPERTS, TOP, MOST, 2))(routing_keys, routing_turns).reshape((TOKENS, TOP))
    route_weight = jnp.clip(jnp.exp(jax.random.uniform(splits[12], (TOKENS, TOP), jnp.float32, math.log(0.05), math.log(0.5))), 0.05, 0.5)
    w_in = bell_draw(splits[13], (EXPERTS, D, 2 * FF), D ** -0.5, 0.125, ((0, 8), (1, 4)))
    w_down = bell_draw(splits[14], (EXPERTS, FF, D), FF ** -0.5, 0.21875, ((0, 8), (2, 4)))
    accept = draw_accept(jax.random.fold_in(splits[16], 71), 0)
    return dict(states=states, attn_gain=attn_gain, w_qkv=w_qkv, q_gain=q_gain, k_gain=k_gain, cache_k=cache_k, cache_v=cache_v, cache_len=cache_len, tree_mask=tree_mask, w_o=w_o, ffn_gain=ffn_gain, routing=routing, route_weight=route_weight, w_in=w_in, w_down=w_down, accept=accept)


EPS = 1e-06
NEG = -1e+30
THETA_LOG = math.log(1000000.0)

def rms_scale(values, gain):
    return values * lax.rsqrt(lax.optimization_barrier(jnp.mean(values * values, -1, keepdims=True)) + EPS) * gain

def rotate(values, position):
    half = values.shape[-1] // 2
    freqs = jnp.exp(jnp.arange(half, dtype=jnp.float32) * (-2.0 * THETA_LOG / values.shape[-1]))
    angles = position.astype(jnp.float32)[..., None] * freqs
    cosine = jnp.cos(angles)
    sine = jnp.sin(angles)
    lower = values[..., :half]
    upper = values[..., half:]
    return jnp.concatenate([lower * cosine - upper * sine, upper * cosine + lower * sine], -1)

def reference(states, attn_gain, w_qkv, q_gain, k_gain, cache_k, cache_v, cache_len, tree_mask, w_o, ffn_gain, routing, route_weight, w_in, w_down, accept):
    group = HEADS // KVH
    normed = rms_scale(states.astype(jnp.float32), attn_gain.astype(jnp.float32)).astype(jnp.bfloat16)
    qkv = jnp.dot(normed, w_qkv, preferred_element_type=jnp.float32).astype(jnp.bfloat16)
    query = qkv[:, :HEADS * HD].reshape(REQUESTS, TREE, KVH, group, HD)
    keys_new = qkv[:, HEADS * HD:HEADS * HD + KVH * HD].reshape(REQUESTS, TREE, KVH, HD)
    values_new = qkv[:, HEADS * HD + KVH * HD:].reshape(REQUESTS, TREE, KVH, HD)
    depth = lax.optimization_barrier(jnp.sum(tree_mask, -1)) - 1
    position = cache_len[:, None] + depth
    q_rot = rotate(rms_scale(query.astype(jnp.float32), q_gain.astype(jnp.float32)), position[:, :, None, None]).astype(jnp.bfloat16)
    k_rot = rotate(rms_scale(keys_new.astype(jnp.float32), k_gain.astype(jnp.float32)), position[:, :, None]).astype(jnp.bfloat16)
    cached_keys = cache_k.reshape(REQUESTS, CACHE, KVH, HD)
    cached_values = cache_v.reshape(REQUESTS, CACHE, KVH, HD)
    score_scale = HD ** (-0.5)

    def one_request(items):
        q_one, k_one, v_one, ck_one, cv_one, length, mask_one = items
        q_float = q_one.astype(jnp.float32)
        scores_cache = jnp.einsum('tkgd,skd->tkgs', q_float, ck_one.astype(jnp.float32)) * score_scale
        scores_tree = jnp.einsum('tkgd,ukd->tkgu', q_float, k_one.astype(jnp.float32)) * score_scale
        valid = (jnp.arange(CACHE) < length)[None, None, None, :]
        tree_ok = (mask_one == 1)[:, None, None, :]
        scores_cache = jnp.where(valid, scores_cache, NEG)
        scores_tree = jnp.where(tree_ok, scores_tree, NEG)
        row_max = jnp.maximum(lax.optimization_barrier(jnp.max(scores_cache, -1)), lax.optimization_barrier(jnp.max(scores_tree, -1)))
        probs_cache = jnp.where(valid, jnp.exp(scores_cache - row_max[..., None]), 0.0).astype(jnp.bfloat16)
        probs_tree = jnp.where(tree_ok, jnp.exp(scores_tree - row_max[..., None]), 0.0).astype(jnp.bfloat16)
        denom_sum = lax.optimization_barrier(jnp.sum(probs_cache.astype(jnp.float32), -1)) + lax.optimization_barrier(jnp.sum(probs_tree.astype(jnp.float32), -1))
        weighted = jnp.einsum('tkgs,skd->tkgd', probs_cache.astype(jnp.float32), cv_one.astype(jnp.float32))
        weighted = weighted + jnp.einsum('tkgu,ukd->tkgd', probs_tree.astype(jnp.float32), v_one.astype(jnp.float32))
        return (weighted / denom_sum[..., None]).astype(jnp.bfloat16).reshape(TREE, HEADS * HD)
    attn = lax.map(one_request, (q_rot, k_rot, values_new, cached_keys, cached_values, cache_len, tree_mask))
    attn = attn.reshape(TOKENS, HEADS * HD)
    resid = (states.astype(jnp.float32) + jnp.dot(attn, w_o, preferred_element_type=jnp.float32)).astype(jnp.bfloat16)
    resid_float = resid.astype(jnp.float32)
    inverse = lax.rsqrt(lax.optimization_barrier(jnp.mean(resid_float * resid_float, -1)) + EPS)
    scaled = (resid_float * ffn_gain.astype(jnp.float32)).astype(jnp.bfloat16)
    padded = jnp.concatenate([scaled, jnp.zeros((1, D), jnp.bfloat16)], 0)
    inverse_pad = jnp.concatenate([inverse, jnp.zeros((1,), jnp.float32)], 0)

    def one_expert(moe_sum, expert_id):
        matched = routing == expert_id
        weight_col = lax.optimization_barrier(jnp.sum(jnp.where(matched, route_weight, 0.0), -1))
        weight_pad = jnp.concatenate([weight_col, jnp.zeros((1,), jnp.float32)], 0)
        slot_idx = jnp.nonzero(jnp.any(matched, -1), size=N_GX * MOST, fill_value=TOKENS)[0].astype(jnp.int32)
        gate_up = jnp.dot(padded[slot_idx], w_in[expert_id], preferred_element_type=jnp.float32)
        row_scale = inverse_pad[slot_idx][:, None]
        hidden = (jax.nn.silu(gate_up[:, :FF] * row_scale) * (gate_up[:, FF:] * row_scale)).astype(jnp.bfloat16)
        out_rows = jnp.dot(hidden, w_down[expert_id], preferred_element_type=jnp.float32)
        return (moe_sum.at[slot_idx].add(out_rows * weight_pad[slot_idx][:, None], mode='drop'), None)
    moe_total = lax.scan(one_expert, jnp.zeros((TOKENS, D), jnp.float32), jnp.arange(EXPERTS, dtype=jnp.int32))[0]
    layer_out = (resid_float + moe_total).astype(jnp.bfloat16)
    kv_new = jnp.concatenate([k_rot.reshape(REQUESTS, TREE, KVH * HD), values_new.reshape(REQUESTS, TREE, KVH * HD)], -1)
    accepted_kv = jnp.einsum('rat,rtc->rac', accept.astype(jnp.float32), kv_new.astype(jnp.float32)).astype(jnp.bfloat16)
    return (layer_out, accepted_kv)
```

```python
import math

import jax
import jax.numpy as jnp
from jax import lax
from jax.experimental import pallas as pl
from jax.experimental.pallas import tpu as pltpu
from jax.sharding import PartitionSpec as P

EPS = 1e-06
NEG = -1e30
THETA_LOG = math.log(1000000.0)


MESH = pl.DeviceIdType.MESH


def exchange(arrays, axis, scatter, cid):
    count = lax.axis_size(axis)
    number = len(arrays)

    def kernel(*refs):
        ins, outs = refs[:number], refs[number : 2 * number]
        send, recv, local = refs[2 * number :]
        me = lax.axis_index(axis)
        barrier = pltpu.get_barrier_semaphore()
        for d in range(1, count):
            pl.semaphore_signal(
                barrier, inc=1, device_id={axis: lax.rem(me + d, count)}, device_id_type=MESH
            )
        pl.semaphore_wait(barrier, count - 1)
        copies = []
        for d in range(1, count):
            peer = lax.rem(me + d, count)
            for i in range(number):
                copy = pltpu.make_async_remote_copy(
                    src_ref=ins[i].at[peer] if scatter else ins[i],
                    dst_ref=outs[i].at[me],
                    send_sem=send.at[i, d],
                    recv_sem=recv.at[i, d],
                    device_id={axis: peer},
                    device_id_type=MESH,
                )
                copy.start()
                copies.append(copy)
        own = []
        for i in range(number):
            copy = pltpu.make_async_copy(
                ins[i].at[me] if scatter else ins[i], outs[i].at[me], local.at[i]
            )
            copy.start()
            own.append(copy)
        for copy in own + copies:
            copy.wait()

    outs = [
        jax.ShapeDtypeStruct(x.shape if scatter else (count,) + x.shape, x.dtype) for x in arrays
    ]
    return pl.pallas_call(
        kernel,
        out_shape=outs,
        in_specs=[pl.BlockSpec(memory_space=pltpu.VMEM)] * number,
        out_specs=[pl.BlockSpec(memory_space=pltpu.VMEM)] * number,
        scratch_shapes=[
            pltpu.SemaphoreType.DMA((number, count)),
            pltpu.SemaphoreType.DMA((number, count)),
            pltpu.SemaphoreType.DMA((number,)),
        ],
        compiler_params=pltpu.CompilerParams(collective_id=cid, has_side_effects=True),
        name="exchange_%d" % cid,
    )(*arrays)


def expert_layer(rows, squares, w_in, w_down, slot_weight, pick_back, resid, model_width, cid):
    axis = "gy"
    count = lax.axis_size(axis)
    peers = lax.axis_size("gx")
    experts, slots, depth = rows.shape
    tokens, cols = resid.shape
    wide = w_in.shape[2]
    units = wide // 2
    half = experts // 2
    piece = 16
    sub = slots // piece
    chunks = half * sub
    hop = 2
    far = hop * (count - 1)

    def kernel(
        x_ref, sq_ref, weight_ref, pick_ref, resid_ref, w_hbm, d_hbm, out_ref,
        hid_ref, wbuf, dbuf, part, rbuf, sqbuf, inv_ref, obuf, pbuf, ret,
        wsem, dsem, rs_s, rs_r, h_s, h_r, sq_s, sq_r, g_s, g_r,
    ):
        me = lax.axis_index(axis)
        prev = lax.rem(me + count - 1, count)
        nxt = lax.rem(me + 1, count)
        at_low = me == 0
        at_high = me == count - 1

        def load(e):
            return pltpu.make_async_copy(w_hbm.at[e], wbuf.at[e], wsem.at[e])

        def load_down(e):
            return pltpu.make_async_copy(d_hbm.at[e], dbuf.at[e], dsem.at[e])

        row = lax.axis_index("gx")
        for s in range(half):
            load(half + s).start()
            load(s).start()
        for s in range(half):
            load_down(half + s).start()
            load_down(s).start()
        barrier = pltpu.get_barrier_semaphore()
        for d in range(1, count):
            pl.semaphore_signal(
                barrier, inc=1, device_id={axis: lax.rem(me + d, count)}, device_id_type=MESH
            )
        for d in range(1, peers):
            pl.semaphore_signal(
                barrier, inc=1, device_id={"gx": lax.rem(row + d, peers)}, device_id_type=MESH
            )

        def multiply(h, s):
            e = h * half + s
            load(e).wait()
            value = jnp.dot(x_ref[e], wbuf[e], preferred_element_type=jnp.float32)
            for j in range(sub):
                part[h, s * sub + j] = value[j * piece : (j + 1) * piece].astype(jnp.bfloat16)

        multiply(1, 0)
        multiply(0, 0)
        pl.semaphore_wait(barrier, count + peers - 2)

        def sq_copy(d):
            return pltpu.make_async_remote_copy(
                src_ref=sq_ref,
                dst_ref=sqbuf.at[d],
                send_sem=sq_s.at[d],
                recv_sem=sq_r.at[d],
                device_id={axis: lax.rem(me + d, count)},
                device_id_type=MESH,
            )

        for d in range(1, count):
            sq_copy(d).start()

        def finish_squares():
            total = sq_ref[...]
            for d in range(1, count):
                sq_copy(d).wait()
                total = total + sqbuf[d]
            inv_ref[...] = lax.rsqrt(total / model_width + EPS)

        diagonal = lax.broadcasted_iota(jnp.int32, (piece, 128), 0) == lax.broadcasted_iota(
            jnp.int32, (piece, 128), 1
        )

        def rs_copy(h, c):
            return pltpu.make_async_remote_copy(
                src_ref=part.at[h, c],
                dst_ref=rbuf.at[h, c],
                send_sem=rs_s.at[h, c],
                recv_sem=rs_r.at[h, c],
                device_id={axis: nxt if h else prev},
                device_id_type=MESH,
            )

        def hid_copy(h, c):
            return pltpu.make_async_remote_copy(
                src_ref=hid_ref.at[h, c],
                dst_ref=hid_ref.at[h, c],
                send_sem=h_s.at[h, c],
                recv_sem=h_r.at[h, c],
                device_id={axis: prev if h else nxt},
                device_id_type=MESH,
            )

        def ends(h):
            return (at_low, at_high) if h else (at_high, at_low)

        def reduce_chunk(h, c):
            first, last = ends(h)

            @pl.when(jnp.logical_not(first))
            def _():
                rs_copy(h, c).wait_recv()

            @pl.when(jnp.logical_not(jnp.logical_or(first, last)))
            def _():
                part[h, c] = (
                    part[h, c].astype(jnp.float32) + rbuf[h, c].astype(jnp.float32)
                ).astype(jnp.bfloat16)

            @pl.when(jnp.logical_not(last))
            def _():
                rs_copy(h, c).start()

            @pl.when(last)
            def _():
                row = inv_ref[pl.ds(h * chunks + c, 1), :]
                inverse = jnp.sum(jnp.where(diagonal, row, 0.0), 1, keepdims=True)
                summed = part[h, c].astype(jnp.float32) + rbuf[h, c].astype(jnp.float32)
                gate = summed[:, :units] * inverse
                up = summed[:, units:] * inverse
                hid_ref[h, c] = (gate / (1.0 + jnp.exp(-gate)) * up).astype(jnp.bfloat16)
                hid_copy(h, c).start()

        def return_chunk(h, c):
            first, last = ends(h)

            @pl.when(jnp.logical_not(last))
            def _():
                hid_copy(h, c).wait_recv()

            @pl.when(jnp.logical_not(jnp.logical_or(first, last)))
            def _():
                hid_copy(h, c).start()

        def project(h, s):
            e = h * half + s
            load_down(e).wait()
            value = hid_ref[h, pl.ds(s * sub, sub)].reshape(slots, units)
            value = jnp.dot(value, dbuf[e], preferred_element_type=jnp.float32)
            obuf[e] = (value * weight_ref[e]).astype(jnp.bfloat16)

        def step(t, carry):
            for h, place in ((1, 1), (0, sub // 2 + 1)):

                @pl.when(jnp.logical_and(t < chunks - sub, lax.rem(t, sub) == place))
                def _():
                    multiply(h, lax.div(t, sub) + 1)

            @pl.when(t == far - 1)
            def _():
                finish_squares()

            for h in (1, 0):
                way = hop * (me if h else count - 1 - me)
                c = t - way

                @pl.when(jnp.logical_and(c >= 0, c < chunks))
                def _():
                    reduce_chunk(h, c)

            for h in (1, 0):
                way = hop * (me if h else count - 1 - me)
                b = t - 2 * far + way

                @pl.when(jnp.logical_and(b >= 0, b < chunks))
                def _():
                    return_chunk(h, b)

                    @pl.when(lax.rem(b, sub) == sub - 1)
                    def _():
                        project(h, lax.div(b, sub))

            return carry

        lax.fori_loop(0, chunks + 2 * far, step, 0)

        def finish(c, carry):
            for h in (1, 0):
                first, last = ends(h)

                @pl.when(jnp.logical_not(last))
                def _():
                    rs_copy(h, c).wait_send()

                @pl.when(jnp.logical_not(first))
                def _():
                    hid_copy(h, c).wait_send()

            return carry

        summed = lax.dot_general(
            pick_ref[...],
            obuf[...].reshape(experts * slots, cols),
            (((0,), (0,)), ((), ())),
            preferred_element_type=jnp.float32,
        )
        for p in range(peers):
            pbuf[p] = summed[p * tokens : (p + 1) * tokens].astype(jnp.bfloat16)

        def back_copy(d):
            peer = lax.rem(row + d, peers)
            return pltpu.make_async_remote_copy(
                src_ref=pbuf.at[peer],
                dst_ref=ret.at[d],
                send_sem=g_s.at[d],
                recv_sem=g_r.at[d],
                device_id={"gx": peer},
                device_id_type=MESH,
            )

        for d in range(1, peers):
            back_copy(d).start()
        moe = pbuf[row].astype(jnp.float32)
        lax.fori_loop(0, chunks, finish, 0)
        for d in range(1, peers):
            back_copy(d).wait_recv()
            moe = moe + ret[d].astype(jnp.float32)
        out_ref[...] = (resid_ref[...].astype(jnp.float32) + moe).astype(jnp.bfloat16)
        for d in range(1, peers):
            back_copy(d).wait_send()

    vmem = pl.BlockSpec(memory_space=pltpu.VMEM)
    hbm = pl.BlockSpec(memory_space=pl.ANY)
    dma = pltpu.SemaphoreType.DMA
    return pl.pallas_call(
        kernel,
        out_shape=jax.ShapeDtypeStruct((tokens, cols), jnp.bfloat16),
        in_specs=[vmem] * 5 + [hbm, hbm],
        out_specs=vmem,
        scratch_shapes=[
            pltpu.VMEM((2, chunks, piece, units), jnp.bfloat16),
            pltpu.VMEM((experts, depth, wide), jnp.bfloat16),
            pltpu.VMEM((experts, units, cols), jnp.bfloat16),
            pltpu.VMEM((2, chunks, piece, wide), jnp.bfloat16),
            pltpu.VMEM((2, chunks, piece, wide), jnp.bfloat16),
            pltpu.VMEM((count, 2 * chunks, 128), jnp.float32),
            pltpu.VMEM((2 * chunks, 128), jnp.float32),
            pltpu.VMEM((experts, slots, cols), jnp.bfloat16),
            pltpu.VMEM((peers, tokens, cols), jnp.bfloat16),
            pltpu.VMEM((peers, tokens, cols), jnp.bfloat16),
            dma((experts,)),
            dma((experts,)),
            dma((2, chunks)),
            dma((2, chunks)),
            dma((2, chunks)),
            dma((2, chunks)),
            dma((count,)),
            dma((count,)),
            dma((peers,)),
            dma((peers,)),
        ],
        compiler_params=pltpu.CompilerParams(
            collective_id=cid, has_side_effects=True, vmem_limit_bytes=52 * 1024 * 1024
        ),
        name="expert_layer",
    )(rows, squares, slot_weight, pick_back, resid, w_in, w_down)


def attention_block(
    qkv, q_gain, k_gain, cosine, sine, cache_k, cache_v, limit, tree_mask, states_here, w_o, cid
):
    blocks = lax.axis_size("gy")
    rows_gx = lax.axis_size("gx")
    tokens = qkv.shape[0]
    span, kv_cols = cache_k.shape
    dim = q_gain.shape[1]
    kv_heads = kv_cols // dim
    heads = qkv.shape[1] // dim - 2 * kv_heads
    group = heads // kv_heads
    per_block = heads // blocks
    blocks_here = blocks // kv_heads
    width = per_block * dim
    cols = w_o.shape[1]
    scale = dim ** (-0.5)

    def kernel(
        limit_ref, q_ref, qg_ref, kg_ref, cos_ref, sin_ref, k_ref, v_ref, mask_ref, st_ref, wo_hbm,
        h_ref, rot_ref,
        acc_out, stat_out, acc_in, stat_in, attn, wo,
        wo_sem, a_s, a_r, s_s, s_r, t_s, t_r, h_s, h_r,
    ):
        me = lax.axis_index("gy")
        row = lax.axis_index("gx")
        load = pltpu.make_async_copy(wo_hbm, wo, wo_sem)
        load.start()
        barrier = pltpu.get_barrier_semaphore()
        for axis, here, count in (("gy", me, blocks), ("gx", row, rows_gx)):
            for d in range(1, count):
                pl.semaphore_signal(
                    barrier, inc=1, device_id={axis: lax.rem(here + d, count)}, device_id_type=MESH
                )
        pl.semaphore_wait(barrier, blocks + rows_gx - 2)

        def send(src, dst, send_sem, recv_sem, axis, peer):
            return pltpu.make_async_remote_copy(
                src_ref=src,
                dst_ref=dst,
                send_sem=send_sem,
                recv_sem=recv_sem,
                device_id={axis: peer},
                device_id_type=MESH,
            )

        def part_copies(block, source):
            return (
                send(acc_out.at[block], acc_in.at[source], a_s.at[block], a_r.at[source], "gy", block),
                send(stat_out.at[block], stat_in.at[source], s_s.at[block], s_r.at[source], "gy", block),
            )

        cos = cos_ref[...]
        sin = sin_ref[...]

        def turn(value, gain):
            value = value.astype(jnp.float32)
            value = value * lax.rsqrt(jnp.mean(value * value, -1, keepdims=True) + EPS) * gain
            return (value * cos + pltpu.roll(value, dim // 2, 1) * sin).astype(jnp.bfloat16)

        q_gain_row = qg_ref[...].astype(jnp.float32)
        k_gain_row = kg_ref[...].astype(jnp.float32)
        contract = (((1,), (1,)), ((), ()))
        diagonal = lax.broadcasted_iota(jnp.int32, (tokens, 128), 0) == lax.broadcasted_iota(
            jnp.int32, (tokens, 128), 1
        )

        def one_head(i, carry):
            g = lax.rem(lax.div(me, blocks_here) + 1 + i, kv_heads)

            def lanes(first, size):
                return pl.ds(pl.multiple_of(first, 128), size)

            query = jnp.concatenate(
                [
                    turn(q_ref[:, lanes((g * group + j) * dim, dim)], q_gain_row)
                    for j in range(group)
                ],
                0,
            )
            keys = turn(q_ref[:, lanes((heads + g) * dim, dim)], k_gain_row)
            values = q_ref[:, lanes((heads + kv_heads + g) * dim, dim)]
            rot_ref[:, lanes(g * dim, dim)] = keys
            tree = (
                lax.dot_general(query, keys, contract, preferred_element_type=jnp.float32) * scale
            )
            mask = jnp.concatenate([mask_ref[...]] * group, 0)
            tree_ok = jnp.logical_and(mask == 1, me == 0)
            tree = jnp.where(tree_ok, tree, NEG)
            score = (
                lax.dot_general(
                    query,
                    k_ref[:, lanes(g * dim, dim)],
                    contract,
                    preferred_element_type=jnp.float32,
                )
                * scale
            )
            valid = lax.broadcasted_iota(jnp.int32, score.shape, 1) < limit_ref[0]
            score = jnp.where(valid, score, NEG)
            top = jnp.maximum(jnp.max(score, 1, keepdims=True), jnp.max(tree, 1, keepdims=True))
            prob = jnp.where(valid, jnp.exp(score - top), 0.0).astype(jnp.bfloat16)
            prob_tree = jnp.where(tree_ok, jnp.exp(tree - top), 0.0).astype(jnp.bfloat16)
            total = jnp.sum(prob.astype(jnp.float32), 1, keepdims=True) + jnp.sum(
                prob_tree.astype(jnp.float32), 1, keepdims=True
            )
            acc = jnp.dot(prob, v_ref[:, lanes(g * dim, dim)], preferred_element_type=jnp.float32)
            acc = acc + jnp.dot(prob_tree, values, preferred_element_type=jnp.float32)
            acc = acc.astype(jnp.bfloat16)
            for b in range(blocks_here):
                block = g * blocks_here + b
                for place in range(per_block):
                    j = b * per_block + place
                    rows = slice(j * tokens, (j + 1) * tokens)
                    acc_out[block, :, place * dim : (place + 1) * dim] = acc[rows]
                    for k, column in enumerate((top, total)):
                        stat_out[block, k * per_block + place : k * per_block + place + 1, :] = (
                            jnp.sum(jnp.where(diagonal, column[rows], 0.0), 0, keepdims=True)
                        )

                @pl.when(block != me)
                def _():
                    for copy in part_copies(block, me):
                        copy.start()

            return carry

        lax.fori_loop(0, kv_heads, one_head, 0)

        acc_in[me] = acc_out[me]
        stat_in[me] = stat_out[me]
        for d in range(1, blocks):
            source = lax.rem(me + d, blocks)
            for copy in part_copies(source, source):
                copy.wait_recv()
        tops = [stat_in[j, :per_block, :] for j in range(blocks)]
        best = tops[0]
        for j in range(1, blocks):
            best = jnp.maximum(best, tops[j])
        factors = [jnp.exp(tops[j] - best) for j in range(blocks)]
        denom = stat_in[0, per_block:, :] * factors[0]
        for j in range(1, blocks):
            denom = denom + stat_in[j, per_block:, :] * factors[j]
        for place in range(per_block):
            joined = jnp.zeros((tokens, dim), jnp.float32)
            for j in range(blocks):
                line = (factors[j] / denom)[place : place + 1, :]
                column = jnp.sum(jnp.where(diagonal, line, 0.0), 1, keepdims=True)
                joined = joined + column * acc_in[
                    j, :, place * dim : (place + 1) * dim
                ].astype(jnp.float32)
            attn[me, :, place * dim : (place + 1) * dim] = joined.astype(jnp.bfloat16)

        def attn_copy(d, source):
            return send(
                attn.at[source], attn.at[source], t_s.at[d], t_r.at[d], "gy", lax.rem(me + d, blocks)
            )

        for d in range(1, blocks):
            attn_copy(d, me).start()
        load.wait()

        def project(source):
            return jnp.dot(
                attn[source],
                wo[pl.ds(pl.multiple_of(source * width, width), width), :],
                preferred_element_type=jnp.float32,
            )

        total = st_ref[...].astype(jnp.float32) + project(me)
        for d in range(1, blocks):
            source = lax.rem(me + blocks - d, blocks)
            attn_copy(d, source).wait_recv()
            total = total + project(source)
        h_ref[row] = total.astype(jnp.bfloat16)

        def h_copy(d, source):
            return send(
                h_ref.at[source], h_ref.at[source], h_s.at[d], h_r.at[d], "gx",
                lax.rem(row + d, rows_gx),
            )

        for d in range(1, rows_gx):
            h_copy(d, row).start()
        for d in range(1, blocks):
            block = lax.rem(me + d, blocks)
            for copy in part_copies(block, me):
                copy.wait_send()
            attn_copy(d, me).wait_send()
        for d in range(1, rows_gx):
            h_copy(d, lax.rem(row + rows_gx - d, rows_gx)).wait_recv()
            h_copy(d, row).wait_send()

    vmem = pl.BlockSpec(memory_space=pltpu.VMEM)
    dma = pltpu.SemaphoreType.DMA
    return pl.pallas_call(
        kernel,
        out_shape=[
            jax.ShapeDtypeStruct((rows_gx, tokens, cols), jnp.bfloat16),
            jax.ShapeDtypeStruct((tokens, kv_cols), jnp.bfloat16),
        ],
        in_specs=[pl.BlockSpec(memory_space=pltpu.SMEM)]
        + [vmem] * 9
        + [pl.BlockSpec(memory_space=pl.ANY)],
        out_specs=[vmem, vmem],
        scratch_shapes=[
            pltpu.VMEM((blocks, tokens, width), jnp.bfloat16),
            pltpu.VMEM((blocks, 2 * per_block, 128), jnp.float32),
            pltpu.VMEM((blocks, tokens, width), jnp.bfloat16),
            pltpu.VMEM((blocks, 2 * per_block, 128), jnp.float32),
            pltpu.VMEM((blocks, tokens, width), jnp.bfloat16),
            pltpu.VMEM(w_o.shape, jnp.bfloat16),
            dma,
            dma((blocks,)),
            dma((blocks,)),
            dma((blocks,)),
            dma((blocks,)),
            dma((blocks,)),
            dma((blocks,)),
            dma((rows_gx,)),
            dma((rows_gx,)),
        ],
        compiler_params=pltpu.CompilerParams(
            collective_id=cid, has_side_effects=True, vmem_limit_bytes=48 * 1024 * 1024
        ),
        name="attention_block",
    )(
        limit, qkv, q_gain, k_gain, cosine, sine, cache_k, cache_v, tree_mask, states_here, w_o
    )


def attention_line(
    states, attn_gain, w_qkv, q_gain, k_gain, cache_k, cache_v, cache_len, tree_mask, w_o, accept, cid
):
    count = lax.axis_size("gy")
    rows_gx = lax.axis_size("gx")
    tokens, model = states.shape
    span, kv_cols = cache_k.shape
    dim = q_gain.shape[1]
    kv_heads = kv_cols // dim
    own = w_qkv.shape[1] // dim
    heads = own * count - 2 * kv_heads
    group = heads // kv_heads
    cols = w_o.shape[1]
    chunks = own // 2
    part = group // 2
    steps = heads // part
    rows = part * tokens
    lane = 128
    accepted = accept.shape[0]
    last = count - 1
    factor = dim ** (-0.5) / math.log(2.0)

    def kernel(
        len_ref, st_ref, ag_ref, qg_ref, kg_ref, mask_ref, acc_ref, wq_hbm, k_hbm, v_hbm, wo_hbm,
        h_ref, akv_ref,
        normed, wq, qall, kext, vext, wo, bias, tree_bias,
        own_acc, own_stat, end_out, end_in, stat_in, mid_out, mid_in, mstat_out, mstat_in,
        attn, total, akv,
        wq_sem, k_sem, v_sem, wo_sem, q_s, q_r, e_s, e_r, es_s, es_r, m_s, m_r, ms_s, ms_r,
        f_s, f_r, a_s, a_r, h_s, h_r,
    ):
        me = lax.axis_index("gy")
        row = lax.axis_index("gx")
        is_last = me == last
        is_end = jnp.logical_or(me == 0, is_last)
        is_mid = jnp.logical_not(is_end)
        low = me < 2
        mid_of = jnp.where(low, 1, 2)
        end_of = jnp.where(low, 0, last)
        other_mid = 3 - mid_of

        def send(src, dst, send_sem, recv_sem, axis, peer):
            return pltpu.make_async_remote_copy(
                src_ref=src,
                dst_ref=dst,
                send_sem=send_sem,
                recv_sem=recv_sem,
                device_id={axis: peer},
                device_id_type=MESH,
            )

        def chunk_at(i):
            return jnp.where(is_last, i, chunks - 1 - i)

        def load_w(c):
            return pltpu.make_async_copy(
                wq_hbm.at[:, pl.ds(pl.multiple_of(c * 2 * dim, 2 * dim), 2 * dim)],
                wq.at[c],
                wq_sem.at[c],
            )

        def load_k(g):
            return pltpu.make_async_copy(
                k_hbm.at[:, g * dim : (g + 1) * dim], kext.at[g, 0:span, :], k_sem.at[g]
            )

        def load_v(g):
            return pltpu.make_async_copy(
                v_hbm.at[:, g * dim : (g + 1) * dim], vext.at[g, 0:span, 0:dim], v_sem.at[g]
            )

        load_o = pltpu.make_async_copy(wo_hbm, wo, wo_sem)
        for i in range(chunks):
            load_w(chunk_at(i)).start()
        for g in range(kv_heads - 1, -1, -1):
            load_k(g).start()
            load_v(g).start()
        load_o.start()
        barrier = pltpu.get_barrier_semaphore()
        for axis, here, number in (("gy", me, count), ("gx", row, rows_gx)):
            for d in range(1, number):
                pl.semaphore_signal(
                    barrier, inc=1, device_id={axis: lax.rem(here + d, number)}, device_id_type=MESH
                )

        value = st_ref[...].astype(jnp.float32)
        value = value * lax.rsqrt(jnp.mean(value * value, -1, keepdims=True) + EPS)
        normed[...] = (value * ag_ref[...].astype(jnp.float32)).astype(jnp.bfloat16)
        mask = mask_ref[...]
        position = len_ref[0] + jnp.sum(mask, -1, keepdims=True) - 1
        place = lax.broadcasted_iota(jnp.int32, (tokens, dim), 1)
        half = lax.rem(place, dim // 2).astype(jnp.float32)
        angle = position.astype(jnp.float32) * jnp.exp(half * (-2.0 * THETA_LOG / dim))
        cos = jnp.cos(angle)
        sin = jnp.sin(angle)
        sin = jnp.where(place < dim // 2, -sin, sin)
        limit = len_ref[0] - me * span
        spot = lax.broadcasted_iota(jnp.int32, (1, span), 1)
        bias[...] = jnp.where(spot < limit, 0.0, NEG)
        allowed = jnp.logical_and(mask == 1, is_last)
        tree_bias[...] = jnp.full((tokens, lane), NEG, jnp.float32)
        tree_bias[:, 0:tokens] = jnp.where(allowed, 0.0, NEG)
        for g in range(kv_heads):
            kext[g, span : span + lane, :] = jnp.zeros((lane, dim), jnp.bfloat16)
            vext[g, span : span + lane, 0:dim] = jnp.zeros((lane, dim), jnp.bfloat16)
            vext[g, :, dim : 2 * dim] = jnp.ones((span + lane, dim), jnp.bfloat16)
        total[...] = st_ref[:, pl.ds(pl.multiple_of(me * cols, 128), cols)].astype(jnp.float32)
        q_gain_row = qg_ref[...].astype(jnp.float32)
        k_gain_row = kg_ref[...].astype(jnp.float32)

        def q_copy(k, c, peer):
            block = qall.at[pl.ds(2 * k, 2)]
            return send(block, block, q_s.at[peer, c], q_r.at[k], "gy", peer)

        pl.semaphore_wait(barrier, count + rows_gx - 2)

        def project_in(i, carry):
            c = chunk_at(i)
            load_w(c).wait()
            value = jnp.dot(normed[...], wq[c], preferred_element_type=jnp.float32)
            value = value.astype(jnp.bfloat16)
            k = me * chunks + c
            for j in range(2):
                head = 2 * k + j
                raw = value[:, j * dim : (j + 1) * dim]
                turned = raw.astype(jnp.float32)
                gain = jnp.where(head < heads, q_gain_row, k_gain_row)
                scale = lax.rsqrt(jnp.mean(turned * turned, -1, keepdims=True) + EPS)
                turned = turned * scale * gain
                turned = (turned * cos + pltpu.roll(turned, dim // 2, 1) * sin).astype(jnp.bfloat16)
                qall[head] = jnp.where(head < heads + kv_heads, turned, raw)
            for peer in range(count - 1, -1, -1):

                @pl.when(jnp.logical_and(me != peer, 2 * k < heads))
                def _():
                    q_copy(k, c, peer).start()

            return carry

        lax.fori_loop(0, chunks, project_in, 0)

        def akv_copy(d, peer):
            return send(akv, akv, a_s.at[d], a_r, "gy", peer)

        @pl.when(is_last)
        def _():
            pick = acc_ref[...].astype(jnp.bfloat16)
            for i in range(2 * kv_heads):
                akv[:, i * dim : (i + 1) * dim] = jnp.dot(
                    pick, qall[heads + i], preferred_element_type=jnp.float32
                ).astype(jnp.bfloat16)
            for d in range(last):
                akv_copy(d, d).start()
            for g in range(kv_heads):
                kext[g, span : span + tokens, :] = qall[heads + g]
                vext[g, span : span + tokens, 0:dim] = qall[heads + kv_heads + g]

        diagonal = lax.broadcasted_iota(jnp.int32, (tokens, lane), 0) == lax.broadcasted_iota(
            jnp.int32, (tokens, lane), 1
        )

        def as_row(column):
            return jnp.sum(jnp.where(diagonal, column, 0.0), 0, keepdims=True)

        def as_column(line):
            return jnp.sum(jnp.where(diagonal, line, 0.0), 1, keepdims=True)

        contract = (((1,), (1,)), ((), ()))

        def end_copy(s):
            return (
                send(end_out.at[s], end_in.at[s], e_s.at[s], e_r.at[s], "gy", mid_of),
                send(own_stat.at[s], stat_in.at[s], es_s.at[s], es_r.at[s], "gy", mid_of),
            )

        def mid_copy(s):
            return (
                send(mid_out.at[s], mid_in.at[s], m_s.at[s], m_r.at[s], "gy", other_mid),
                send(mstat_out.at[s], mstat_in.at[s], ms_s.at[s], ms_r.at[s], "gy", other_mid),
            )

        def block_of(s):
            return steps - 1 - s

        def final_copy(s):
            place = attn.at[pl.ds(block_of(s) * part, part)]
            return send(place, place, f_s.at[s], f_r.at[s], "gy", end_of)

        def attend(s):
            b = block_of(s)
            for n in range(part // 2):
                k = b * (part // 2) + n
                source = lax.div(k, chunks)

                @pl.when(source != me)
                def _():
                    q_copy(k, 0, source).wait_recv()

            g = lax.div(b, 2)
            query = qall[pl.ds(b * part, part)].reshape(rows, dim)
            score = lax.dot_general(query, kext[g], contract, preferred_element_type=jnp.float32)
            cached = score[:, :span] + bias[...]
            tree = score[:, span:] + jnp.concatenate([tree_bias[...]] * part, 0)
            top = jnp.maximum(jnp.max(cached, 1, keepdims=True), jnp.max(tree, 1, keepdims=True))
            top = jnp.maximum(top, 0.5 * NEG)
            prob = jnp.concatenate(
                [
                    jnp.exp2((cached - top) * factor).astype(jnp.bfloat16),
                    jnp.exp2((tree - top) * factor).astype(jnp.bfloat16),
                ],
                1,
            )
            out = jnp.dot(prob, vext[g], preferred_element_type=jnp.float32)
            for j in range(part):
                here = slice(j * tokens, (j + 1) * tokens)
                own_stat[s, j : j + 1, :] = as_row(top[here])
                own_stat[s, part + j : part + j + 1, :] = as_row(out[here, dim:])

            @pl.when(is_end)
            def _():
                end_out[s] = out[:, :dim].astype(jnp.bfloat16)
                for copy in end_copy(s):
                    copy.start()

            @pl.when(is_mid)
            def _():
                own_acc[s] = out[:, :dim]

        def join(s):
            for copy in end_copy(s):
                copy.wait_recv()
            a, b = own_stat[s, :part, :], stat_in[s, :part, :]
            top = jnp.maximum(a, b)
            fa, fb = jnp.exp2((a - top) * factor), jnp.exp2((b - top) * factor)
            mstat_out[s, :part, :] = top
            mstat_out[s, part:, :] = own_stat[s, part:, :] * fa + stat_in[s, part:, :] * fb
            for j in range(part):
                here = slice(j * tokens, (j + 1) * tokens)
                value = own_acc[s, here, :] * as_column(fa[j : j + 1])
                value = value + end_in[s, here, :].astype(jnp.float32) * as_column(fb[j : j + 1])
                own_acc[s, here, :] = value
                mid_out[s, here, :] = value.astype(jnp.bfloat16)
            for copy in mid_copy(s):
                copy.start()

        def project_out(s):
            b = block_of(s)
            value = jnp.concatenate([attn[b * part + j] for j in range(part)], 1)
            weight = wo[pl.ds(pl.multiple_of(b * part * dim, part * dim), part * dim), :]
            total[...] += jnp.dot(value, weight, preferred_element_type=jnp.float32)

        def settle(s):
            for copy in mid_copy(s):
                copy.wait_recv()
            a, b = mstat_out[s, :part, :], mstat_in[s, :part, :]
            top = jnp.maximum(a, b)
            fa, fb = jnp.exp2((a - top) * factor), jnp.exp2((b - top) * factor)
            denom = mstat_out[s, part:, :] * fa + mstat_in[s, part:, :] * fb
            fa, fb = fa / denom, fb / denom
            for j in range(part):
                here = slice(j * tokens, (j + 1) * tokens)
                value = own_acc[s, here, :] * as_column(fa[j : j + 1])
                value = value + mid_in[s, here, :].astype(jnp.float32) * as_column(fb[j : j + 1])
                attn[block_of(s) * part + j] = value.astype(jnp.bfloat16)
            final_copy(s).start()
            project_out(s)

        for g in range(kv_heads):
            load_k(g).wait()
            load_v(g).wait()

        def step(t, carry):
            @pl.when(t < steps)
            def _():
                attend(t)

            @pl.when(t == 2)
            def _():
                load_o.wait()

            @pl.when(jnp.logical_and(is_mid, jnp.logical_and(t >= 1, t <= steps)))
            def _():
                join(t - 1)

            @pl.when(jnp.logical_and(is_mid, jnp.logical_and(t >= 2, t <= steps + 1)))
            def _():
                settle(t - 2)

            @pl.when(jnp.logical_and(is_end, t >= 3))
            def _():
                final_copy(t - 3).wait_recv()
                project_out(t - 3)

            return carry

        lax.fori_loop(0, steps + 3, step, 0)
        h_ref[row] = total[...].astype(jnp.bfloat16)

        def h_copy(d, source):
            return send(
                h_ref.at[source], h_ref.at[source], h_s.at[d], h_r.at[d], "gx",
                lax.rem(row + d, rows_gx),
            )

        for d in range(1, rows_gx):
            h_copy(d, row).start()

        @pl.when(is_last)
        def _():
            for d in range(last):
                akv_copy(d, d).wait_send()

        @pl.when(jnp.logical_not(is_last))
        def _():
            akv_copy(0, last).wait_recv()

        akv_ref[...] = akv[0:accepted, :]

        def sent(c, carry):
            k = me * chunks + c
            for peer in range(count):

                @pl.when(jnp.logical_and(me != peer, 2 * k < heads))
                def _():
                    q_copy(k, c, peer).wait_send()

            return carry

        lax.fori_loop(0, chunks, sent, 0)

        def done(s, carry):
            @pl.when(is_end)
            def _():
                for copy in end_copy(s):
                    copy.wait_send()

            @pl.when(is_mid)
            def _():
                for copy in mid_copy(s):
                    copy.wait_send()
                final_copy(s).wait_send()

            return carry

        lax.fori_loop(0, steps, done, 0)
        for d in range(1, rows_gx):
            h_copy(d, lax.rem(row + rows_gx - d, rows_gx)).wait_recv()
            h_copy(d, row).wait_send()

    pad = -accepted % 16
    vmem = pl.BlockSpec(memory_space=pltpu.VMEM)
    hbm = pl.BlockSpec(memory_space=pl.ANY)
    dma = pltpu.SemaphoreType.DMA
    stat = pltpu.VMEM((steps, 2 * part, lane), jnp.float32)
    piece = pltpu.VMEM((steps, rows, dim), jnp.bfloat16)
    return pl.pallas_call(
        kernel,
        out_shape=[
            jax.ShapeDtypeStruct((rows_gx, tokens, cols), jnp.bfloat16),
            jax.ShapeDtypeStruct((accepted, 2 * kv_cols), jnp.bfloat16),
        ],
        in_specs=[pl.BlockSpec(memory_space=pltpu.SMEM)] + [vmem] * 6 + [hbm] * 4,
        out_specs=[vmem, vmem],
        scratch_shapes=[
            pltpu.VMEM((tokens, model), jnp.bfloat16),
            pltpu.VMEM((chunks, model, 2 * dim), jnp.bfloat16),
            pltpu.VMEM((own * count, tokens, dim), jnp.bfloat16),
            pltpu.VMEM((kv_heads, span + lane, dim), jnp.bfloat16),
            pltpu.VMEM((kv_heads, span + lane, 2 * dim), jnp.bfloat16),
            pltpu.VMEM(w_o.shape, jnp.bfloat16),
            pltpu.VMEM((1, span), jnp.float32),
            pltpu.VMEM((tokens, lane), jnp.float32),
            pltpu.VMEM((steps, rows, dim), jnp.float32),
            stat,
            piece,
            piece,
            stat,
            piece,
            piece,
            stat,
            stat,
            pltpu.VMEM((heads, tokens, dim), jnp.bfloat16),
            pltpu.VMEM((tokens, cols), jnp.float32),
            pltpu.VMEM((accepted + pad, 2 * kv_cols), jnp.bfloat16),
            dma((chunks,)),
            dma((kv_heads,)),
            dma((kv_heads,)),
            dma,
            dma((count, chunks)),
            dma((count * chunks,)),
        ]
        + [dma((steps,))] * 10
        + [dma((last,)), dma, dma((rows_gx,)), dma((rows_gx,))],
        compiler_params=pltpu.CompilerParams(
            collective_id=cid, has_side_effects=True, vmem_limit_bytes=40 * 1024 * 1024
        ),
        name="attention_line",
    )(
        cache_len, states, attn_gain, q_gain, k_gain, tree_mask,
        jnp.pad(accept, ((0, pad), (0, 0))), w_qkv, cache_k, cache_v, w_o,
    )


def rms_scale(values, gain):
    return values * lax.rsqrt(jnp.mean(values * values, -1, keepdims=True) + EPS) * gain


def angles_of(position, dim):
    freqs = jnp.exp(jnp.arange(dim // 2, dtype=jnp.float32) * (-2.0 * THETA_LOG / dim))
    angles = position.astype(jnp.float32)[..., None] * freqs
    cosine = jnp.cos(angles)
    sine = jnp.sin(angles)
    return jnp.concatenate([cosine, cosine], -1), jnp.concatenate([-sine, sine], -1)


def body(
    states,
    attn_gain,
    w_qkv,
    q_gain,
    k_gain,
    cache_k,
    cache_v,
    cache_len,
    tree_mask,
    w_o,
    ffn_gain,
    routing,
    route_weight,
    w_in,
    w_down,
    accept,
):
    tok_rows, model_width = states.shape
    head_dim = q_gain.shape[0]
    kv_cols = cache_k.shape[2]
    heads_all = w_o.shape[0] // head_dim
    cache_span = cache_k.shape[1]
    cols_here = w_o.shape[1]
    col_index = lax.axis_index("gy")
    row_index = lax.axis_index("gx")
    count_gx = lax.axis_size("gx")
    count_gy = lax.axis_size("gy")
    own_heads = w_qkv.shape[1] // head_dim
    kv_heads = kv_cols // head_dim
    on_line = (
        count_gy == 4
        and w_qkv.shape[1] % (2 * head_dim) == 0
        and own_heads >= 2 * kv_heads
        and (own_heads - 2 * kv_heads) % 2 == 0
        and heads_all % (4 * kv_heads) == 0
        and tok_rows % 16 == 0
        and tok_rows <= 128
    )
    if on_line:
        gathered, accepted_kv = attention_line(
            states,
            attn_gain[None],
            w_qkv,
            q_gain[None],
            k_gain[None],
            cache_k[0],
            cache_v[0],
            cache_len,
            tree_mask[0],
            w_o,
            accept[0],
            0,
        )
        accepted_kv = accepted_kv[None]
    else:
        normed = rms_scale(states.astype(jnp.float32), attn_gain.astype(jnp.float32)).astype(
            jnp.bfloat16
        )
        qkv_part = jnp.dot(normed, w_qkv, preferred_element_type=jnp.float32).astype(jnp.bfloat16)
        (qkv_blocks,) = exchange([qkv_part], "gy", False, 0)
        qkv_whole = jnp.swapaxes(qkv_blocks, 0, 1).reshape(tok_rows, -1)
        q_cols = heads_all * head_dim
        depth = jnp.sum(tree_mask, -1) - 1
        cosine, sine = angles_of((cache_len[:, None] + depth)[0], head_dim)
        states_here = lax.dynamic_slice_in_dim(states, col_index * cols_here, cols_here, 1)
        gathered, k_rot = attention_block(
            qkv_whole,
            q_gain[None],
            k_gain[None],
            cosine,
            sine,
            cache_k[0],
            cache_v[0],
            cache_len - col_index * cache_span,
            tree_mask[0],
            states_here,
            w_o,
            1,
        )
        kv_new = jnp.concatenate([k_rot, qkv_whole[:, q_cols + kv_cols :]], -1)[None]
        accepted_kv = jnp.einsum(
            "rat,rtc->rac", accept.astype(jnp.bfloat16), kv_new, preferred_element_type=jnp.float32
        ).astype(jnp.bfloat16)
    resid = lax.dynamic_index_in_dim(gathered, row_index, 0, False)
    exp_here = w_in.shape[0]
    expert_count = exp_here * count_gx
    top_k = routing.shape[1]
    most_rows = 3 * tok_rows * top_k // (2 * expert_count)
    hidden_units = w_down.shape[1]
    gain_float = ffn_gain.astype(jnp.float32)
    tokens = routing.shape[0]
    slots = count_gx * most_rows
    own_experts = row_index * exp_here + jnp.arange(exp_here, dtype=jnp.int32)
    matched = routing[:, None, :] == own_experts[None, :, None]
    hits = jnp.any(matched, -1)
    weights = jnp.sum(jnp.where(matched, route_weight[:, None, :], 0.0), -1)
    order = jnp.arange(tok_rows, dtype=jnp.int32)
    earlier = (order[:, None] > order[None, :]).astype(jnp.bfloat16)
    rank = jnp.einsum(
        "tu,bue->bte",
        earlier,
        hits.astype(jnp.bfloat16).reshape(count_gx, tok_rows, exp_here),
        preferred_element_type=jnp.float32,
    ).astype(jnp.int32)
    first_slot = jnp.arange(count_gx, dtype=jnp.int32)[:, None, None] * most_rows
    slot_of = jnp.where(hits, (rank + first_slot).reshape(tokens, exp_here), -1)
    pick = slot_of.T[:, None, :] == jnp.arange(slots, dtype=jnp.int32)[None, :, None]
    pick_matrix = pick.astype(jnp.bfloat16)
    slot_weight = jnp.sum(jnp.where(pick, weights.T[:, None, :], 0.0), -1)
    gathered = gathered.reshape(tokens, cols_here).astype(jnp.float32)
    token_squares = jnp.sum(gathered * gathered, -1)
    slot_squares = jnp.sum(jnp.where(pick, token_squares, 0.0), -1)
    piece = 16
    slot_squares = jnp.pad(slot_squares.reshape(-1, piece), ((0, 0), (0, 128 - piece)))
    scaled = (gathered * gain_float).astype(jnp.bfloat16)
    rows = jnp.einsum(
        "est,td->esd", pick_matrix, scaled, preferred_element_type=jnp.float32
    ).astype(jnp.bfloat16)
    layer_out = expert_layer(
        rows,
        slot_squares,
        w_in,
        w_down,
        slot_weight[..., None],
        pick_matrix.reshape(exp_here * slots, tokens),
        resid,
        model_width,
        4,
    )
    return (layer_out, accepted_kv)


def solution(mesh):
    in_specs = (
        P("gx", None),
        P(),
        P(None, "gy"),
        P(),
        P(),
        P("gx", "gy", None),
        P("gx", "gy", None),
        P("gx"),
        P("gx", None, None),
        P(None, "gy"),
        P("gy"),
        P(),
        P(),
        P("gx", "gy", None),
        P("gx", None, "gy"),
        P("gx", None, None),
    )
    out_specs = (P("gx", "gy"), P("gx", None, None))
    return jax.shard_map(body, mesh=mesh, in_specs=in_specs, out_specs=out_specs, check_vma=False)
```

```python
import math

import jax
import jax.numpy as jnp
from jax import lax
from jax.experimental import pallas as pl
from jax.experimental.pallas import tpu as pltpu
from jax.sharding import PartitionSpec as P

EPS = 1e-06
NEG = -1e30
THETA_LOG = math.log(1000000.0)


MESH = pl.DeviceIdType.MESH


def exchange(arrays, axis, scatter, cid):
    count = lax.axis_size(axis)
    number = len(arrays)

    def kernel(*refs):
        ins, outs = refs[:number], refs[number : 2 * number]
        send, recv, local = refs[2 * number :]
        me = lax.axis_index(axis)
        barrier = pltpu.get_barrier_semaphore()
        for d in range(1, count):
            pl.semaphore_signal(
                barrier, inc=1, device_id={axis: lax.rem(me + d, count)}, device_id_type=MESH
            )
        pl.semaphore_wait(barrier, count - 1)
        copies = []
        for d in range(1, count):
            peer = lax.rem(me + d, count)
            for i in range(number):
                copy = pltpu.make_async_remote_copy(
                    src_ref=ins[i].at[peer] if scatter else ins[i],
                    dst_ref=outs[i].at[me],
                    send_sem=send.at[i, d],
                    recv_sem=recv.at[i, d],
                    device_id={axis: peer},
                    device_id_type=MESH,
                )
                copy.start()
                copies.append(copy)
        own = []
        for i in range(number):
            copy = pltpu.make_async_copy(
                ins[i].at[me] if scatter else ins[i], outs[i].at[me], local.at[i]
            )
            copy.start()
            own.append(copy)
        for copy in own + copies:
            copy.wait()

    outs = [
        jax.ShapeDtypeStruct(x.shape if scatter else (count,) + x.shape, x.dtype) for x in arrays
    ]
    return pl.pallas_call(
        kernel,
        out_shape=outs,
        in_specs=[pl.BlockSpec(memory_space=pltpu.VMEM)] * number,
        out_specs=[pl.BlockSpec(memory_space=pltpu.VMEM)] * number,
        scratch_shapes=[
            pltpu.SemaphoreType.DMA((number, count)),
            pltpu.SemaphoreType.DMA((number, count)),
            pltpu.SemaphoreType.DMA((number,)),
        ],
        compiler_params=pltpu.CompilerParams(collective_id=cid, has_side_effects=True),
        name="exchange_%d" % cid,
    )(*arrays)


def expert_layer(rows, squares, w_in, w_down, slot_weight, pick_back, resid, model_width, cid):
    axis = "gy"
    count = lax.axis_size(axis)
    peers = lax.axis_size("gx")
    experts, slots, depth = rows.shape
    tokens, cols = resid.shape
    wide = w_in.shape[2]
    units = wide // 2
    half = experts // 2
    piece = 16
    sub = slots // piece
    chunks = half * sub
    hop = 2
    far = hop * (count - 1)

    def kernel(
        x_ref, sq_ref, weight_ref, pick_ref, resid_ref, w_hbm, d_hbm, out_ref,
        hid_ref, wbuf, dbuf, part, rbuf, sqbuf, inv_ref, obuf, pbuf, ret,
        wsem, dsem, rs_s, rs_r, h_s, h_r, sq_s, sq_r, g_s, g_r,
    ):
        me = lax.axis_index(axis)
        prev = lax.rem(me + count - 1, count)
        nxt = lax.rem(me + 1, count)
        at_low = me == 0
        at_high = me == count - 1

        def load(e):
            return pltpu.make_async_copy(w_hbm.at[e], wbuf.at[e], wsem.at[e])

        def load_down(e):
            return pltpu.make_async_copy(d_hbm.at[e], dbuf.at[e], dsem.at[e])

        row = lax.axis_index("gx")
        for s in range(half):
            load(half + s).start()
            load(s).start()
        for s in range(half):
            load_down(half + s).start()
            load_down(s).start()
        barrier = pltpu.get_barrier_semaphore()
        for d in range(1, count):
            pl.semaphore_signal(
                barrier, inc=1, device_id={axis: lax.rem(me + d, count)}, device_id_type=MESH
            )
        for d in range(1, peers):
            pl.semaphore_signal(
                barrier, inc=1, device_id={"gx": lax.rem(row + d, peers)}, device_id_type=MESH
            )

        def multiply(h, s):
            e = h * half + s
            load(e).wait()
            value = jnp.dot(x_ref[e], wbuf[e], preferred_element_type=jnp.float32)
            for j in range(sub):
                part[h, s * sub + j] = value[j * piece : (j + 1) * piece].astype(jnp.bfloat16)

        multiply(1, 0)
        multiply(0, 0)
        pl.semaphore_wait(barrier, count + peers - 2)

        def sq_copy(d):
            return pltpu.make_async_remote_copy(
                src_ref=sq_ref,
                dst_ref=sqbuf.at[d],
                send_sem=sq_s.at[d],
                recv_sem=sq_r.at[d],
                device_id={axis: lax.rem(me + d, count)},
                device_id_type=MESH,
            )

        for d in range(1, count):
            sq_copy(d).start()

        def finish_squares():
            total = sq_ref[...]
            for d in range(1, count):
                sq_copy(d).wait()
                total = total + sqbuf[d]
            inv_ref[...] = lax.rsqrt(total / model_width + EPS)

        diagonal = lax.broadcasted_iota(jnp.int32, (piece, 128), 0) == lax.broadcasted_iota(
            jnp.int32, (piece, 128), 1
        )

        def rs_copy(h, c):
            return pltpu.make_async_remote_copy(
                src_ref=part.at[h, c],
                dst_ref=rbuf.at[h, c],
                send_sem=rs_s.at[h, c],
                recv_sem=rs_r.at[h, c],
                device_id={axis: nxt if h else prev},
                device_id_type=MESH,
            )

        def hid_copy(h, c):
            return pltpu.make_async_remote_copy(
                src_ref=hid_ref.at[h, c],
                dst_ref=hid_ref.at[h, c],
                send_sem=h_s.at[h, c],
                recv_sem=h_r.at[h, c],
                device_id={axis: prev if h else nxt},
                device_id_type=MESH,
            )

        def ends(h):
            return (at_low, at_high) if h else (at_high, at_low)

        def reduce_chunk(h, c):
            first, last = ends(h)

            @pl.when(jnp.logical_not(first))
            def _():
                rs_copy(h, c).wait_recv()

            @pl.when(jnp.logical_not(jnp.logical_or(first, last)))
            def _():
                part[h, c] = (
                    part[h, c].astype(jnp.float32) + rbuf[h, c].astype(jnp.float32)
                ).astype(jnp.bfloat16)

            @pl.when(jnp.logical_not(last))
            def _():
                rs_copy(h, c).start()

            @pl.when(last)
            def _():
                row = inv_ref[pl.ds(h * chunks + c, 1), :]
                inverse = jnp.sum(jnp.where(diagonal, row, 0.0), 1, keepdims=True)
                summed = part[h, c].astype(jnp.float32) + rbuf[h, c].astype(jnp.float32)
                gate = summed[:, :units] * inverse
                up = summed[:, units:] * inverse
                hid_ref[h, c] = (gate / (1.0 + jnp.exp(-gate)) * up).astype(jnp.bfloat16)
                hid_copy(h, c).start()

        def return_chunk(h, c):
            first, last = ends(h)

            @pl.when(jnp.logical_not(last))
            def _():
                hid_copy(h, c).wait_recv()

            @pl.when(jnp.logical_not(jnp.logical_or(first, last)))
            def _():
                hid_copy(h, c).start()

        def project(h, s):
            e = h * half + s
            load_down(e).wait()
            value = hid_ref[h, pl.ds(s * sub, sub)].reshape(slots, units)
            value = jnp.dot(value, dbuf[e], preferred_element_type=jnp.float32)
            obuf[e] = (value * weight_ref[e]).astype(jnp.bfloat16)

        def step(t, carry):
            for h, place in ((1, 1), (0, sub // 2 + 1)):

                @pl.when(jnp.logical_and(t < chunks - sub, lax.rem(t, sub) == place))
                def _():
                    multiply(h, lax.div(t, sub) + 1)

            @pl.when(t == far - 1)
            def _():
                finish_squares()

            for h in (1, 0):
                way = hop * (me if h else count - 1 - me)
                c = t - way

                @pl.when(jnp.logical_and(c >= 0, c < chunks))
                def _():
                    reduce_chunk(h, c)

            for h in (1, 0):
                way = hop * (me if h else count - 1 - me)
                b = t - 2 * far + way

                @pl.when(jnp.logical_and(b >= 0, b < chunks))
                def _():
                    return_chunk(h, b)

                    @pl.when(lax.rem(b, sub) == sub - 1)
                    def _():
                        project(h, lax.div(b, sub))

            return carry

        lax.fori_loop(0, chunks + 2 * far, step, 0)

        def finish(c, carry):
            for h in (1, 0):
                first, last = ends(h)

                @pl.when(jnp.logical_not(last))
                def _():
                    rs_copy(h, c).wait_send()

                @pl.when(jnp.logical_not(first))
                def _():
                    hid_copy(h, c).wait_send()

            return carry

        summed = lax.dot_general(
            pick_ref[...],
            obuf[...].reshape(experts * slots, cols),
            (((0,), (0,)), ((), ())),
            preferred_element_type=jnp.float32,
        )
        for p in range(peers):
            pbuf[p] = summed[p * tokens : (p + 1) * tokens].astype(jnp.bfloat16)

        def back_copy(d):
            peer = lax.rem(row + d, peers)
            return pltpu.make_async_remote_copy(
                src_ref=pbuf.at[peer],
                dst_ref=ret.at[d],
                send_sem=g_s.at[d],
                recv_sem=g_r.at[d],
                device_id={"gx": peer},
                device_id_type=MESH,
            )

        for d in range(1, peers):
            back_copy(d).start()
        moe = pbuf[row].astype(jnp.float32)
        lax.fori_loop(0, chunks, finish, 0)
        for d in range(1, peers):
            back_copy(d).wait_recv()
            moe = moe + ret[d].astype(jnp.float32)
        out_ref[...] = (resid_ref[...].astype(jnp.float32) + moe).astype(jnp.bfloat16)
        for d in range(1, peers):
            back_copy(d).wait_send()

    vmem = pl.BlockSpec(memory_space=pltpu.VMEM)
    hbm = pl.BlockSpec(memory_space=pl.ANY)
    dma = pltpu.SemaphoreType.DMA
    return pl.pallas_call(
        kernel,
        out_shape=jax.ShapeDtypeStruct((tokens, cols), jnp.bfloat16),
        in_specs=[vmem] * 5 + [hbm, hbm],
        out_specs=vmem,
        scratch_shapes=[
            pltpu.VMEM((2, chunks, piece, units), jnp.bfloat16),
            pltpu.VMEM((experts, depth, wide), jnp.bfloat16),
            pltpu.VMEM((experts, units, cols), jnp.bfloat16),
            pltpu.VMEM((2, chunks, piece, wide), jnp.bfloat16),
            pltpu.VMEM((2, chunks, piece, wide), jnp.bfloat16),
            pltpu.VMEM((count, 2 * chunks, 128), jnp.float32),
            pltpu.VMEM((2 * chunks, 128), jnp.float32),
            pltpu.VMEM((experts, slots, cols), jnp.bfloat16),
            pltpu.VMEM((peers, tokens, cols), jnp.bfloat16),
            pltpu.VMEM((peers, tokens, cols), jnp.bfloat16),
            dma((experts,)),
            dma((experts,)),
            dma((2, chunks)),
            dma((2, chunks)),
            dma((2, chunks)),
            dma((2, chunks)),
            dma((count,)),
            dma((count,)),
            dma((peers,)),
            dma((peers,)),
        ],
        compiler_params=pltpu.CompilerParams(
            collective_id=cid, has_side_effects=True, vmem_limit_bytes=52 * 1024 * 1024
        ),
        name="expert_layer",
    )(rows, squares, slot_weight, pick_back, resid, w_in, w_down)


def attention_block(
    qkv, q_gain, k_gain, cosine, sine, cache_k, cache_v, limit, tree_mask, states_here, w_o, cid
):
    blocks = lax.axis_size("gy")
    rows_gx = lax.axis_size("gx")
    tokens = qkv.shape[0]
    span, kv_cols = cache_k.shape
    dim = q_gain.shape[1]
    kv_heads = kv_cols // dim
    heads = qkv.shape[1] // dim - 2 * kv_heads
    group = heads // kv_heads
    per_block = heads // blocks
    blocks_here = blocks // kv_heads
    width = per_block * dim
    cols = w_o.shape[1]
    scale = dim ** (-0.5)

    def kernel(
        limit_ref, q_ref, qg_ref, kg_ref, cos_ref, sin_ref, k_ref, v_ref, mask_ref, st_ref, wo_hbm,
        h_ref, rot_ref,
        acc_out, stat_out, acc_in, stat_in, attn, wo,
        wo_sem, a_s, a_r, s_s, s_r, t_s, t_r, h_s, h_r,
    ):
        me = lax.axis_index("gy")
        row = lax.axis_index("gx")
        load = pltpu.make_async_copy(wo_hbm, wo, wo_sem)
        load.start()
        barrier = pltpu.get_barrier_semaphore()
        for axis, here, count in (("gy", me, blocks), ("gx", row, rows_gx)):
            for d in range(1, count):
                pl.semaphore_signal(
                    barrier, inc=1, device_id={axis: lax.rem(here + d, count)}, device_id_type=MESH
                )
        pl.semaphore_wait(barrier, blocks + rows_gx - 2)

        def send(src, dst, send_sem, recv_sem, axis, peer):
            return pltpu.make_async_remote_copy(
                src_ref=src,
                dst_ref=dst,
                send_sem=send_sem,
                recv_sem=recv_sem,
                device_id={axis: peer},
                device_id_type=MESH,
            )

        def part_copies(block, source):
            return (
                send(acc_out.at[block], acc_in.at[source], a_s.at[block], a_r.at[source], "gy", block),
                send(stat_out.at[block], stat_in.at[source], s_s.at[block], s_r.at[source], "gy", block),
            )

        cos = cos_ref[...]
        sin = sin_ref[...]

        def turn(value, gain):
            value = value.astype(jnp.float32)
            value = value * lax.rsqrt(jnp.mean(value * value, -1, keepdims=True) + EPS) * gain
            return (value * cos + pltpu.roll(value, dim // 2, 1) * sin).astype(jnp.bfloat16)

        q_gain_row = qg_ref[...].astype(jnp.float32)
        k_gain_row = kg_ref[...].astype(jnp.float32)
        contract = (((1,), (1,)), ((), ()))
        diagonal = lax.broadcasted_iota(jnp.int32, (tokens, 128), 0) == lax.broadcasted_iota(
            jnp.int32, (tokens, 128), 1
        )

        def one_head(i, carry):
            g = lax.rem(lax.div(me, blocks_here) + 1 + i, kv_heads)

            def lanes(first, size):
                return pl.ds(pl.multiple_of(first, 128), size)

            query = jnp.concatenate(
                [
                    turn(q_ref[:, lanes((g * group + j) * dim, dim)], q_gain_row)
                    for j in range(group)
                ],
                0,
            )
            keys = turn(q_ref[:, lanes((heads + g) * dim, dim)], k_gain_row)
            values = q_ref[:, lanes((heads + kv_heads + g) * dim, dim)]
            rot_ref[:, lanes(g * dim, dim)] = keys
            tree = (
                lax.dot_general(query, keys, contract, preferred_element_type=jnp.float32) * scale
            )
            mask = jnp.concatenate([mask_ref[...]] * group, 0)
            tree_ok = jnp.logical_and(mask == 1, me == 0)
            tree = jnp.where(tree_ok, tree, NEG)
            score = (
                lax.dot_general(
                    query,
                    k_ref[:, lanes(g * dim, dim)],
                    contract,
                    preferred_element_type=jnp.float32,
                )
                * scale
            )
            valid = lax.broadcasted_iota(jnp.int32, score.shape, 1) < limit_ref[0]
            score = jnp.where(valid, score, NEG)
            top = jnp.maximum(jnp.max(score, 1, keepdims=True), jnp.max(tree, 1, keepdims=True))
            prob = jnp.where(valid, jnp.exp(score - top), 0.0).astype(jnp.bfloat16)
            prob_tree = jnp.where(tree_ok, jnp.exp(tree - top), 0.0).astype(jnp.bfloat16)
            total = jnp.sum(prob.astype(jnp.float32), 1, keepdims=True) + jnp.sum(
                prob_tree.astype(jnp.float32), 1, keepdims=True
            )
            acc = jnp.dot(prob, v_ref[:, lanes(g * dim, dim)], preferred_element_type=jnp.float32)
            acc = acc + jnp.dot(prob_tree, values, preferred_element_type=jnp.float32)
            acc = acc.astype(jnp.bfloat16)
            for b in range(blocks_here):
                block = g * blocks_here + b
                for place in range(per_block):
                    j = b * per_block + place
                    rows = slice(j * tokens, (j + 1) * tokens)
                    acc_out[block, :, place * dim : (place + 1) * dim] = acc[rows]
                    for k, column in enumerate((top, total)):
                        stat_out[block, k * per_block + place : k * per_block + place + 1, :] = (
                            jnp.sum(jnp.where(diagonal, column[rows], 0.0), 0, keepdims=True)
                        )

                @pl.when(block != me)
                def _():
                    for copy in part_copies(block, me):
                        copy.start()

            return carry

        lax.fori_loop(0, kv_heads, one_head, 0)

        acc_in[me] = acc_out[me]
        stat_in[me] = stat_out[me]
        for d in range(1, blocks):
            source = lax.rem(me + d, blocks)
            for copy in part_copies(source, source):
                copy.wait_recv()
        tops = [stat_in[j, :per_block, :] for j in range(blocks)]
        best = tops[0]
        for j in range(1, blocks):
            best = jnp.maximum(best, tops[j])
        factors = [jnp.exp(tops[j] - best) for j in range(blocks)]
        denom = stat_in[0, per_block:, :] * factors[0]
        for j in range(1, blocks):
            denom = denom + stat_in[j, per_block:, :] * factors[j]
        for place in range(per_block):
            joined = jnp.zeros((tokens, dim), jnp.float32)
            for j in range(blocks):
                line = (factors[j] / denom)[place : place + 1, :]
                column = jnp.sum(jnp.where(diagonal, line, 0.0), 1, keepdims=True)
                joined = joined + column * acc_in[
                    j, :, place * dim : (place + 1) * dim
                ].astype(jnp.float32)
            attn[me, :, place * dim : (place + 1) * dim] = joined.astype(jnp.bfloat16)

        def attn_copy(d, source):
            return send(
                attn.at[source], attn.at[source], t_s.at[d], t_r.at[d], "gy", lax.rem(me + d, blocks)
            )

        for d in range(1, blocks):
            attn_copy(d, me).start()
        load.wait()

        def project(source):
            return jnp.dot(
                attn[source],
                wo[pl.ds(pl.multiple_of(source * width, width), width), :],
                preferred_element_type=jnp.float32,
            )

        total = st_ref[...].astype(jnp.float32) + project(me)
        for d in range(1, blocks):
            source = lax.rem(me + blocks - d, blocks)
            attn_copy(d, source).wait_recv()
            total = total + project(source)
        h_ref[row] = total.astype(jnp.bfloat16)

        def h_copy(d, source):
            return send(
                h_ref.at[source], h_ref.at[source], h_s.at[d], h_r.at[d], "gx",
                lax.rem(row + d, rows_gx),
            )

        for d in range(1, rows_gx):
            h_copy(d, row).start()
        for d in range(1, blocks):
            block = lax.rem(me + d, blocks)
            for copy in part_copies(block, me):
                copy.wait_send()
            attn_copy(d, me).wait_send()
        for d in range(1, rows_gx):
            h_copy(d, lax.rem(row + rows_gx - d, rows_gx)).wait_recv()
            h_copy(d, row).wait_send()

    vmem = pl.BlockSpec(memory_space=pltpu.VMEM)
    dma = pltpu.SemaphoreType.DMA
    return pl.pallas_call(
        kernel,
        out_shape=[
            jax.ShapeDtypeStruct((rows_gx, tokens, cols), jnp.bfloat16),
            jax.ShapeDtypeStruct((tokens, kv_cols), jnp.bfloat16),
        ],
        in_specs=[pl.BlockSpec(memory_space=pltpu.SMEM)]
        + [vmem] * 9
        + [pl.BlockSpec(memory_space=pl.ANY)],
        out_specs=[vmem, vmem],
        scratch_shapes=[
            pltpu.VMEM((blocks, tokens, width), jnp.bfloat16),
            pltpu.VMEM((blocks, 2 * per_block, 128), jnp.float32),
            pltpu.VMEM((blocks, tokens, width), jnp.bfloat16),
            pltpu.VMEM((blocks, 2 * per_block, 128), jnp.float32),
            pltpu.VMEM((blocks, tokens, width), jnp.bfloat16),
            pltpu.VMEM(w_o.shape, jnp.bfloat16),
            dma,
            dma((blocks,)),
            dma((blocks,)),
            dma((blocks,)),
            dma((blocks,)),
            dma((blocks,)),
            dma((blocks,)),
            dma((rows_gx,)),
            dma((rows_gx,)),
        ],
        compiler_params=pltpu.CompilerParams(
            collective_id=cid, has_side_effects=True, vmem_limit_bytes=48 * 1024 * 1024
        ),
        name="attention_block",
    )(
        limit, qkv, q_gain, k_gain, cosine, sine, cache_k, cache_v, tree_mask, states_here, w_o
    )


def layer_line(
    states, attn_gain, w_qkv, q_gain, k_gain, cache_k, cache_v, cache_len, tree_mask, w_o, accept,
    ffn_gain, routing, route_weight, w_in, w_down, cid
):
    count = lax.axis_size("gy")
    rows_gx = lax.axis_size("gx")
    tokens, model = states.shape
    span, kv_cols = cache_k.shape
    dim = q_gain.shape[1]
    kv_heads = kv_cols // dim
    own = w_qkv.shape[1] // dim
    heads = own * count - 2 * kv_heads
    group = heads // kv_heads
    cols = w_o.shape[1]
    chunks = own // 2
    part = group // 2
    steps = heads // part
    rows = part * tokens
    lane = 128
    accepted = accept.shape[0]
    last = count - 1
    factor = dim ** (-0.5) / math.log(2.0)
    top_k, everyone = routing.shape
    experts, depth, wide = w_in.shape
    units = wide // 2
    most_rows = 3 * tokens * top_k // (2 * experts * rows_gx)
    slots = rows_gx * most_rows
    split = experts // 2
    grain = 16
    sub = slots // grain
    strips = split * sub
    hop = 2
    far = hop * last

    def kernel(
        len_ref, st_ref, ag_ref, qg_ref, kg_ref, mask_ref, acc_ref, fg_ref, rt_ref, rw_ref,
        wq_hbm, k_hbm, v_hbm, wo_hbm, w_hbm, d_hbm,
        out_ref, akv_ref,
        normed, wq, qall, kext, vext, wo, bias, tree_bias,
        own_acc, own_stat, end_out, end_in, stat_in, mid_out, mid_in, mstat_out, mstat_in,
        attn, total, akv,
        wq_sem, k_sem, v_sem, wo_sem, q_s, q_r, e_s, e_r, es_s, es_r, m_s, m_r, ms_s, ms_r,
        f_s, f_r, a_s, a_r, h_s, h_r,
        h_all, scaled, pick, wcol, sq_out, sq_in, inv_row, hid, wbuf, dbuf, part_sum, rbuf, obuf, pbuf, ret,
        w_sem, d_sem, sq_s, sq_r, rs_s, rs_r, hid_s, hid_r, g_s, g_r,
    ):
        me = lax.axis_index("gy")
        row = lax.axis_index("gx")
        is_last = me == last
        is_end = jnp.logical_or(me == 0, is_last)
        is_mid = jnp.logical_not(is_end)
        low = me < 2
        mid_of = jnp.where(low, 1, 2)
        end_of = jnp.where(low, 0, last)
        other_mid = 3 - mid_of

        def send(src, dst, send_sem, recv_sem, axis, peer):
            return pltpu.make_async_remote_copy(
                src_ref=src,
                dst_ref=dst,
                send_sem=send_sem,
                recv_sem=recv_sem,
                device_id={axis: peer},
                device_id_type=MESH,
            )

        def chunk_at(i):
            return jnp.where(is_last, i, chunks - 1 - i)

        def load_w(c):
            return pltpu.make_async_copy(
                wq_hbm.at[:, pl.ds(pl.multiple_of(c * 2 * dim, 2 * dim), 2 * dim)],
                wq.at[c],
                wq_sem.at[c],
            )

        def load_k(g):
            return pltpu.make_async_copy(
                k_hbm.at[:, g * dim : (g + 1) * dim], kext.at[g, 0:span, :], k_sem.at[g]
            )

        def load_v(g):
            return pltpu.make_async_copy(
                v_hbm.at[:, g * dim : (g + 1) * dim], vext.at[g, 0:span, 0:dim], v_sem.at[g]
            )

        load_o = pltpu.make_async_copy(wo_hbm, wo, wo_sem)
        for i in range(chunks):
            load_w(chunk_at(i)).start()
        for g in range(kv_heads - 1, -1, -1):
            load_k(g).start()
            load_v(g).start()
        load_o.start()
        barrier = pltpu.get_barrier_semaphore()
        for axis, here, number in (("gy", me, count), ("gx", row, rows_gx)):
            for d in range(1, number):
                pl.semaphore_signal(
                    barrier, inc=1, device_id={axis: lax.rem(here + d, number)}, device_id_type=MESH
                )

        value = st_ref[...].astype(jnp.float32)
        value = value * lax.rsqrt(jnp.mean(value * value, -1, keepdims=True) + EPS)
        normed[...] = (value * ag_ref[...].astype(jnp.float32)).astype(jnp.bfloat16)
        mask = mask_ref[...]
        position = len_ref[0] + jnp.sum(mask, -1, keepdims=True) - 1
        place = lax.broadcasted_iota(jnp.int32, (tokens, dim), 1)
        half = lax.rem(place, dim // 2).astype(jnp.float32)
        angle = position.astype(jnp.float32) * jnp.exp(half * (-2.0 * THETA_LOG / dim))
        cos = jnp.cos(angle)
        sin = jnp.sin(angle)
        sin = jnp.where(place < dim // 2, -sin, sin)
        limit = len_ref[0] - me * span
        spot = lax.broadcasted_iota(jnp.int32, (1, span), 1)
        bias[...] = jnp.where(spot < limit, 0.0, NEG)
        allowed = jnp.logical_and(mask == 1, is_last)
        tree_bias[...] = jnp.full((tokens, lane), NEG, jnp.float32)
        tree_bias[:, 0:tokens] = jnp.where(allowed, 0.0, NEG)
        for g in range(kv_heads):
            kext[g, span : span + lane, :] = jnp.zeros((lane, dim), jnp.bfloat16)
            vext[g, span : span + lane, 0:dim] = jnp.zeros((lane, dim), jnp.bfloat16)
            vext[g, :, dim : 2 * dim] = jnp.ones((span + lane, dim), jnp.bfloat16)
        total[...] = st_ref[:, pl.ds(pl.multiple_of(me * cols, 128), cols)].astype(jnp.float32)
        q_gain_row = qg_ref[...].astype(jnp.float32)
        k_gain_row = kg_ref[...].astype(jnp.float32)

        def q_copy(k, c, peer):
            block = qall.at[pl.ds(2 * k, 2)]
            return send(block, block, q_s.at[peer, c], q_r.at[k], "gy", peer)

        pl.semaphore_wait(barrier, count + rows_gx - 2)

        def project_in(i, carry):
            c = chunk_at(i)
            load_w(c).wait()
            value = jnp.dot(normed[...], wq[c], preferred_element_type=jnp.float32)
            value = value.astype(jnp.bfloat16)
            k = me * chunks + c
            for j in range(2):
                head = 2 * k + j
                raw = value[:, j * dim : (j + 1) * dim]
                turned = raw.astype(jnp.float32)
                gain = jnp.where(head < heads, q_gain_row, k_gain_row)
                scale = lax.rsqrt(jnp.mean(turned * turned, -1, keepdims=True) + EPS)
                turned = turned * scale * gain
                turned = (turned * cos + pltpu.roll(turned, dim // 2, 1) * sin).astype(jnp.bfloat16)
                qall[head] = jnp.where(head < heads + kv_heads, turned, raw)
            for peer in range(count - 1, -1, -1):

                @pl.when(jnp.logical_and(me != peer, 2 * k < heads))
                def _():
                    q_copy(k, c, peer).start()

            return carry

        lax.fori_loop(0, chunks, project_in, 0)

        def load_in(e):
            return pltpu.make_async_copy(w_hbm.at[e], wbuf.at[e], w_sem.at[e])

        def load_down(e):
            return pltpu.make_async_copy(d_hbm.at[e], dbuf.at[e], d_sem.at[e])

        for e in range(split):
            load_in(split + e).start()
            load_in(e).start()
        for e in range(split):
            load_down(split + e).start()
            load_down(e).start()

        names = rt_ref[...]
        shares = rw_ref[...]
        hits, weights = [], []
        for e in range(experts):
            matched = names == row * experts + e
            hits.append(jnp.sum(jnp.where(matched, 1.0, 0.0), 0, keepdims=True))
            weights.append(jnp.sum(jnp.where(matched, shares, 0.0), 0, keepdims=True))
        hit = jnp.concatenate(hits, 0)
        before = lax.broadcasted_iota(jnp.int32, (lane, lane), 0)
        after = lax.broadcasted_iota(jnp.int32, (lane, lane), 1)
        same = lax.div(before, tokens) == lax.div(after, tokens)
        earlier = jnp.where(jnp.logical_and(before < after, same), 1.0, 0.0).astype(jnp.bfloat16)
        rank = jnp.concatenate(
            [
                jnp.dot(
                    hit[:, i : i + lane].astype(jnp.bfloat16),
                    earlier,
                    preferred_element_type=jnp.float32,
                )
                for i in range(0, everyone, lane)
            ],
            1,
        )
        block_no = lax.div(lax.broadcasted_iota(jnp.int32, (experts, everyone), 1), tokens)
        slot_of = jnp.where(hit > 0.5, rank + (block_no * most_rows).astype(jnp.float32), -1.0)
        slot_no = lax.broadcasted_iota(jnp.int32, (slots, everyone), 0).astype(jnp.float32)
        for e in range(experts):
            chosen = slot_no == slot_of[e : e + 1]
            pick[e] = jnp.where(chosen, 1.0, 0.0).astype(jnp.bfloat16)
            column = jnp.sum(jnp.where(chosen, weights[e], 0.0), 1, keepdims=True)
            wcol[e] = jnp.broadcast_to(column, (slots, lane))

        def akv_copy(d, peer):
            return send(akv, akv, a_s.at[d], a_r, "gy", peer)

        @pl.when(is_last)
        def _():
            pick = acc_ref[...].astype(jnp.bfloat16)
            akv[...] = jnp.zeros(akv.shape, jnp.bfloat16)
            for i in range(2 * kv_heads):
                akv[0:accepted, i * dim : (i + 1) * dim] = jnp.dot(
                    pick, qall[heads + i], preferred_element_type=jnp.float32
                ).astype(jnp.bfloat16)
            for d in range(last):
                akv_copy(d, d).start()
            for g in range(kv_heads):
                kext[g, span : span + tokens, :] = qall[heads + g]
                vext[g, span : span + tokens, 0:dim] = qall[heads + kv_heads + g]

        diagonal = lax.broadcasted_iota(jnp.int32, (tokens, lane), 0) == lax.broadcasted_iota(
            jnp.int32, (tokens, lane), 1
        )

        def as_row(column):
            return jnp.sum(jnp.where(diagonal, column, 0.0), 0, keepdims=True)

        def as_column(line):
            return jnp.sum(jnp.where(diagonal, line, 0.0), 1, keepdims=True)

        contract = (((1,), (1,)), ((), ()))

        def end_copy(s):
            return (
                send(end_out.at[s], end_in.at[s], e_s.at[s], e_r.at[s], "gy", mid_of),
                send(own_stat.at[s], stat_in.at[s], es_s.at[s], es_r.at[s], "gy", mid_of),
            )

        def mid_copy(s):
            return (
                send(mid_out.at[s], mid_in.at[s], m_s.at[s], m_r.at[s], "gy", other_mid),
                send(mstat_out.at[s], mstat_in.at[s], ms_s.at[s], ms_r.at[s], "gy", other_mid),
            )

        def block_of(s):
            return steps - 1 - s

        def final_copy(s):
            place = attn.at[pl.ds(block_of(s) * part, part)]
            return send(place, place, f_s.at[s], f_r.at[s], "gy", end_of)

        def attend(s):
            b = block_of(s)
            for n in range(part // 2):
                k = b * (part // 2) + n
                source = lax.div(k, chunks)

                @pl.when(source != me)
                def _():
                    q_copy(k, 0, source).wait_recv()

            g = lax.div(b, 2)
            query = qall[pl.ds(b * part, part)].reshape(rows, dim)
            score = lax.dot_general(query, kext[g], contract, preferred_element_type=jnp.float32)
            cached = score[:, :span] + bias[...]
            tree = score[:, span:] + jnp.concatenate([tree_bias[...]] * part, 0)
            top = jnp.maximum(jnp.max(cached, 1, keepdims=True), jnp.max(tree, 1, keepdims=True))
            top = jnp.maximum(top, 0.5 * NEG)
            prob = jnp.concatenate(
                [
                    jnp.exp2((cached - top) * factor).astype(jnp.bfloat16),
                    jnp.exp2((tree - top) * factor).astype(jnp.bfloat16),
                ],
                1,
            )
            out = jnp.dot(prob, vext[g], preferred_element_type=jnp.float32)
            for j in range(part):
                here = slice(j * tokens, (j + 1) * tokens)
                own_stat[s, j : j + 1, :] = as_row(top[here])
                own_stat[s, part + j : part + j + 1, :] = as_row(out[here, dim:])

            @pl.when(is_end)
            def _():
                end_out[s] = out[:, :dim].astype(jnp.bfloat16)
                for copy in end_copy(s):
                    copy.start()

            @pl.when(is_mid)
            def _():
                own_acc[s] = out[:, :dim]

        def join(s):
            for copy in end_copy(s):
                copy.wait_recv()
            a, b = own_stat[s, :part, :], stat_in[s, :part, :]
            top = jnp.maximum(a, b)
            fa, fb = jnp.exp2((a - top) * factor), jnp.exp2((b - top) * factor)
            mstat_out[s, :part, :] = top
            mstat_out[s, part:, :] = own_stat[s, part:, :] * fa + stat_in[s, part:, :] * fb
            for j in range(part):
                here = slice(j * tokens, (j + 1) * tokens)
                value = own_acc[s, here, :] * as_column(fa[j : j + 1])
                value = value + end_in[s, here, :].astype(jnp.float32) * as_column(fb[j : j + 1])
                own_acc[s, here, :] = value
                mid_out[s, here, :] = value.astype(jnp.bfloat16)
            for copy in mid_copy(s):
                copy.start()

        def project_out(s):
            b = block_of(s)
            value = jnp.concatenate([attn[b * part + j] for j in range(part)], 1)
            weight = wo[pl.ds(pl.multiple_of(b * part * dim, part * dim), part * dim), :]
            total[...] += jnp.dot(value, weight, preferred_element_type=jnp.float32)

        def settle(s):
            for copy in mid_copy(s):
                copy.wait_recv()
            a, b = mstat_out[s, :part, :], mstat_in[s, :part, :]
            top = jnp.maximum(a, b)
            fa, fb = jnp.exp2((a - top) * factor), jnp.exp2((b - top) * factor)
            denom = mstat_out[s, part:, :] * fa + mstat_in[s, part:, :] * fb
            fa, fb = fa / denom, fb / denom
            for j in range(part):
                here = slice(j * tokens, (j + 1) * tokens)
                value = own_acc[s, here, :] * as_column(fa[j : j + 1])
                value = value + mid_in[s, here, :].astype(jnp.float32) * as_column(fb[j : j + 1])
                attn[block_of(s) * part + j] = value.astype(jnp.bfloat16)
            final_copy(s).start()
            project_out(s)

        for g in range(kv_heads):
            load_k(g).wait()
            load_v(g).wait()

        def step(t, carry):
            @pl.when(t < steps)
            def _():
                attend(t)

            @pl.when(t == 2)
            def _():
                load_o.wait()

            @pl.when(jnp.logical_and(is_mid, jnp.logical_and(t >= 1, t <= steps)))
            def _():
                join(t - 1)

            @pl.when(jnp.logical_and(is_mid, jnp.logical_and(t >= 2, t <= steps + 1)))
            def _():
                settle(t - 2)

            @pl.when(jnp.logical_and(is_end, t >= 3))
            def _():
                final_copy(t - 3).wait_recv()
                project_out(t - 3)

            return carry

        lax.fori_loop(0, steps + 3, step, 0)
        h_all[row] = total[...].astype(jnp.bfloat16)

        def h_copy(d, source):
            return send(
                h_all.at[source], h_all.at[source], h_s.at[d], h_r.at[d], "gx",
                lax.rem(row + d, rows_gx),
            )

        for d in range(1, rows_gx):
            h_copy(d, row).start()

        @pl.when(is_last)
        def _():
            for d in range(last):
                akv_copy(d, d).wait_send()

        @pl.when(jnp.logical_not(is_last))
        def _():
            akv_copy(0, last).wait_recv()

        akv_ref[...] = akv[0:accepted, :]

        def sent(c, carry):
            k = me * chunks + c
            for peer in range(count):

                @pl.when(jnp.logical_and(me != peer, 2 * k < heads))
                def _():
                    q_copy(k, c, peer).wait_send()

            return carry

        def done(s, carry):
            @pl.when(is_end)
            def _():
                for copy in end_copy(s):
                    copy.wait_send()

            @pl.when(is_mid)
            def _():
                for copy in mid_copy(s):
                    copy.wait_send()
                final_copy(s).wait_send()

            return carry

        gain = fg_ref[...].astype(jnp.float32)
        for d in range(rows_gx):
            source = lax.rem(row + rows_gx - d, rows_gx)
            if d:
                h_copy(d, source).wait_recv()
            value = h_all[source].astype(jnp.float32)
            scaled[source] = (value * gain).astype(jnp.bfloat16)
        square_of = lax.broadcasted_iota(jnp.int32, (lane, lane), 0) == lax.broadcasted_iota(
            jnp.int32, (lane, lane), 1
        )

        def multiply(h, s):
            e = h * split + s
            load_in(e).wait()
            value = jnp.dot(
                pick[e], scaled[...].reshape(everyone, cols), preferred_element_type=jnp.float32
            ).astype(jnp.bfloat16)
            value = jnp.dot(value, wbuf[e], preferred_element_type=jnp.float32)
            for j in range(sub):
                part_sum[h, s * sub + j] = value[j * grain : (j + 1) * grain].astype(jnp.bfloat16)

        multiply(1, 0)
        multiply(0, 0)
        sq_out[...] = jnp.zeros(sq_out.shape, jnp.float32)
        for i in range(everyone // lane):
            value = h_all[pl.ds(i * (lane // tokens), lane // tokens)].reshape(lane, cols)
            value = value.astype(jnp.float32)
            column = jnp.sum(value * value, 1, keepdims=True)
            line = jnp.sum(jnp.where(square_of, column, 0.0), 0, keepdims=True)
            sq_out[0:1, i * lane : (i + 1) * lane] = line

        def sq_copy(d):
            return send(
                sq_out, sq_in.at[d], sq_s.at[d], sq_r.at[d], "gy", lax.rem(me + d, count)
            )

        for d in range(1, count):
            sq_copy(d).start()

        def finish_squares():
            whole = sq_out[0:1, :]
            for d in range(1, count):
                sq_copy(d).wait()
                whole = whole + sq_in[d, 0:1, :]
            inv_row[...] = lax.rsqrt(whole / model + EPS)

        prev = lax.rem(me + count - 1, count)
        nxt = lax.rem(me + 1, count)
        at_low = me == 0
        at_high = is_last

        def rs_copy(h, c):
            return send(
                part_sum.at[h, c], rbuf.at[h, c], rs_s.at[h, c], rs_r.at[h, c], "gy",
                nxt if h else prev,
            )

        def hid_copy(h, c):
            return send(
                hid.at[h, c], hid.at[h, c], hid_s.at[h, c], hid_r.at[h, c], "gy",
                prev if h else nxt,
            )

        def ends(h):
            return (at_low, at_high) if h else (at_high, at_low)

        def reduce_strip(h, c):
            first, final = ends(h)

            @pl.when(jnp.logical_not(first))
            def _():
                rs_copy(h, c).wait_recv()

            @pl.when(jnp.logical_not(jnp.logical_or(first, final)))
            def _():
                part_sum[h, c] = (
                    part_sum[h, c].astype(jnp.float32) + rbuf[h, c].astype(jnp.float32)
                ).astype(jnp.bfloat16)

            @pl.when(jnp.logical_not(final))
            def _():
                rs_copy(h, c).start()

            @pl.when(final)
            def _():
                e = h * split + lax.div(c, sub)
                at = pl.multiple_of(lax.rem(c, sub) * grain, grain)
                chosen = pick[e, pl.ds(at, grain), :].astype(jnp.float32)
                inverse = jnp.sum(chosen * inv_row[...], 1, keepdims=True)
                summed = part_sum[h, c].astype(jnp.float32) + rbuf[h, c].astype(jnp.float32)
                gate = summed[:, :units] * inverse
                up = summed[:, units:] * inverse
                hid[h, c] = (gate / (1.0 + jnp.exp(-gate)) * up).astype(jnp.bfloat16)
                hid_copy(h, c).start()

        def return_strip(h, c):
            first, final = ends(h)

            @pl.when(jnp.logical_not(final))
            def _():
                hid_copy(h, c).wait_recv()

            @pl.when(jnp.logical_not(jnp.logical_or(first, final)))
            def _():
                hid_copy(h, c).start()

        def project_down(h, s):
            e = h * split + s
            load_down(e).wait()
            value = hid[h, pl.ds(s * sub, sub)].reshape(slots, units)
            value = jnp.dot(value, dbuf[e], preferred_element_type=jnp.float32)
            obuf[e] = (value * wcol[e, :, 0:1]).astype(jnp.bfloat16)

        def moe_step(t, carry):
            for h, place in ((1, 1), (0, sub // 2 + 1)):

                @pl.when(jnp.logical_and(t < strips - sub, lax.rem(t, sub) == place))
                def _():
                    multiply(h, lax.div(t, sub) + 1)

            @pl.when(t == far - 1)
            def _():
                finish_squares()

            for h in (1, 0):
                way = hop * (me if h else last - me)
                c = t - way

                @pl.when(jnp.logical_and(c >= 0, c < strips))
                def _():
                    reduce_strip(h, c)

            for h in (1, 0):
                way = hop * (me if h else last - me)
                b = t - 2 * far + way

                @pl.when(jnp.logical_and(b >= 0, b < strips))
                def _():
                    return_strip(h, b)

                    @pl.when(lax.rem(b, sub) == sub - 1)
                    def _():
                        project_down(h, lax.div(b, sub))

            return carry

        lax.fori_loop(0, strips + 2 * far, moe_step, 0)

        def finish(c, carry):
            for h in (1, 0):
                first, final = ends(h)

                @pl.when(jnp.logical_not(final))
                def _():
                    rs_copy(h, c).wait_send()

                @pl.when(jnp.logical_not(first))
                def _():
                    hid_copy(h, c).wait_send()

            return carry

        summed = lax.dot_general(
            pick[...].reshape(experts * slots, everyone),
            obuf[...].reshape(experts * slots, cols),
            (((0,), (0,)), ((), ())),
            preferred_element_type=jnp.float32,
        )
        for p in range(rows_gx):
            pbuf[p] = summed[p * tokens : (p + 1) * tokens].astype(jnp.bfloat16)

        def back_copy(d):
            peer = lax.rem(row + d, rows_gx)
            return send(pbuf.at[peer], ret.at[d], g_s.at[d], g_r.at[d], "gx", peer)

        for d in range(1, rows_gx):
            back_copy(d).start()
        moe = pbuf[row].astype(jnp.float32)
        lax.fori_loop(0, chunks, sent, 0)
        lax.fori_loop(0, steps, done, 0)
        lax.fori_loop(0, strips, finish, 0)
        for d in range(1, rows_gx):
            h_copy(d, row).wait_send()
        for d in range(1, rows_gx):
            back_copy(d).wait_recv()
            moe = moe + ret[d].astype(jnp.float32)
        out_ref[...] = (h_all[row].astype(jnp.float32) + moe).astype(jnp.bfloat16)
        for d in range(1, rows_gx):
            back_copy(d).wait_send()

    pad = -accepted % 16
    vmem = pl.BlockSpec(memory_space=pltpu.VMEM)
    hbm = pl.BlockSpec(memory_space=pl.ANY)
    dma = pltpu.SemaphoreType.DMA
    stat = pltpu.VMEM((steps, 2 * part, lane), jnp.float32)
    piece = pltpu.VMEM((steps, rows, dim), jnp.bfloat16)
    return pl.pallas_call(
        kernel,
        out_shape=[
            jax.ShapeDtypeStruct((tokens, cols), jnp.bfloat16),
            jax.ShapeDtypeStruct((accepted, 2 * kv_cols), jnp.bfloat16),
        ],
        in_specs=[pl.BlockSpec(memory_space=pltpu.SMEM)] + [vmem] * 9 + [hbm] * 6,
        out_specs=[vmem, vmem],
        scratch_shapes=[
            pltpu.VMEM((tokens, model), jnp.bfloat16),
            pltpu.VMEM((chunks, model, 2 * dim), jnp.bfloat16),
            pltpu.VMEM((own * count, tokens, dim), jnp.bfloat16),
            pltpu.VMEM((kv_heads, span + lane, dim), jnp.bfloat16),
            pltpu.VMEM((kv_heads, span + lane, 2 * dim), jnp.bfloat16),
            pltpu.VMEM(w_o.shape, jnp.bfloat16),
            pltpu.VMEM((1, span), jnp.float32),
            pltpu.VMEM((tokens, lane), jnp.float32),
            pltpu.VMEM((steps, rows, dim), jnp.float32),
            stat,
            piece,
            piece,
            stat,
            piece,
            piece,
            stat,
            stat,
            pltpu.VMEM((heads, tokens, dim), jnp.bfloat16),
            pltpu.VMEM((tokens, cols), jnp.float32),
            pltpu.VMEM((accepted + pad, 2 * kv_cols), jnp.bfloat16),
            dma((chunks,)),
            dma((kv_heads,)),
            dma((kv_heads,)),
            dma,
            dma((count, chunks)),
            dma((count * chunks,)),
        ]
        + [dma((steps,))] * 10
        + [dma((last,)), dma, dma((rows_gx,)), dma((rows_gx,))]
        + [
            pltpu.VMEM((rows_gx, tokens, cols), jnp.bfloat16),
            pltpu.VMEM((rows_gx, tokens, cols), jnp.bfloat16),
            pltpu.VMEM((experts, slots, everyone), jnp.bfloat16),
            pltpu.VMEM((experts, slots, lane), jnp.float32),
            pltpu.VMEM((8, everyone), jnp.float32),
            pltpu.VMEM((count, 8, everyone), jnp.float32),
            pltpu.VMEM((1, everyone), jnp.float32),
            pltpu.VMEM((2, strips, grain, units), jnp.bfloat16),
            pltpu.VMEM((experts, depth, wide), jnp.bfloat16),
            pltpu.VMEM((experts, units, cols), jnp.bfloat16),
            pltpu.VMEM((2, strips, grain, wide), jnp.bfloat16),
            pltpu.VMEM((2, strips, grain, wide), jnp.bfloat16),
            pltpu.VMEM((experts, slots, cols), jnp.bfloat16),
            pltpu.VMEM((rows_gx, tokens, cols), jnp.bfloat16),
            pltpu.VMEM((rows_gx, tokens, cols), jnp.bfloat16),
            dma((experts,)),
            dma((experts,)),
            dma((count,)),
            dma((count,)),
            dma((2, strips)),
            dma((2, strips)),
            dma((2, strips)),
            dma((2, strips)),
            dma((rows_gx,)),
            dma((rows_gx,)),
        ],
        compiler_params=pltpu.CompilerParams(
            collective_id=cid, has_side_effects=True, vmem_limit_bytes=62 * 1024 * 1024
        ),
        name="layer_line",
    )(
        cache_len, states, attn_gain, q_gain, k_gain, tree_mask,
        accept, ffn_gain, routing, route_weight, w_qkv, cache_k, cache_v, w_o, w_in, w_down,
    )


def rms_scale(values, gain):
    return values * lax.rsqrt(jnp.mean(values * values, -1, keepdims=True) + EPS) * gain


def angles_of(position, dim):
    freqs = jnp.exp(jnp.arange(dim // 2, dtype=jnp.float32) * (-2.0 * THETA_LOG / dim))
    angles = position.astype(jnp.float32)[..., None] * freqs
    cosine = jnp.cos(angles)
    sine = jnp.sin(angles)
    return jnp.concatenate([cosine, cosine], -1), jnp.concatenate([-sine, sine], -1)


def body(
    states,
    attn_gain,
    w_qkv,
    q_gain,
    k_gain,
    cache_k,
    cache_v,
    cache_len,
    tree_mask,
    w_o,
    ffn_gain,
    routing,
    route_weight,
    w_in,
    w_down,
    accept,
):
    tok_rows, model_width = states.shape
    head_dim = q_gain.shape[0]
    kv_cols = cache_k.shape[2]
    heads_all = w_o.shape[0] // head_dim
    cache_span = cache_k.shape[1]
    cols_here = w_o.shape[1]
    col_index = lax.axis_index("gy")
    row_index = lax.axis_index("gx")
    count_gx = lax.axis_size("gx")
    count_gy = lax.axis_size("gy")
    own_heads = w_qkv.shape[1] // head_dim
    kv_heads = kv_cols // head_dim
    on_line = (
        count_gy == 4
        and w_qkv.shape[1] % (2 * head_dim) == 0
        and own_heads >= 2 * kv_heads
        and (own_heads - 2 * kv_heads) % 2 == 0
        and heads_all % (4 * kv_heads) == 0
        and tok_rows % 16 == 0
        and 128 % tok_rows == 0
        and routing.shape[0] % 128 == 0
        and w_in.shape[1] == w_o.shape[1]
        and (3 * routing.shape[0] * routing.shape[1] // (2 * w_in.shape[0] * lax.axis_size("gx"))) % 16 == 0
    )
    if on_line:
        layer_out, accepted_kv = layer_line(
            states,
            attn_gain[None],
            w_qkv,
            q_gain[None],
            k_gain[None],
            cache_k[0],
            cache_v[0],
            cache_len,
            tree_mask[0],
            w_o,
            accept[0],
            ffn_gain[None],
            routing.T,
            route_weight.T,
            w_in,
            w_down,
            0,
        )
        return (layer_out, accepted_kv[None])
    normed = rms_scale(states.astype(jnp.float32), attn_gain.astype(jnp.float32)).astype(
        jnp.bfloat16
    )
    qkv_part = jnp.dot(normed, w_qkv, preferred_element_type=jnp.float32).astype(jnp.bfloat16)
    (qkv_blocks,) = exchange([qkv_part], "gy", False, 0)
    qkv_whole = jnp.swapaxes(qkv_blocks, 0, 1).reshape(tok_rows, -1)
    q_cols = heads_all * head_dim
    depth = jnp.sum(tree_mask, -1) - 1
    cosine, sine = angles_of((cache_len[:, None] + depth)[0], head_dim)
    states_here = lax.dynamic_slice_in_dim(states, col_index * cols_here, cols_here, 1)
    gathered, k_rot = attention_block(
        qkv_whole,
        q_gain[None],
        k_gain[None],
        cosine,
        sine,
        cache_k[0],
        cache_v[0],
        cache_len - col_index * cache_span,
        tree_mask[0],
        states_here,
        w_o,
        1,
    )
    kv_new = jnp.concatenate([k_rot, qkv_whole[:, q_cols + kv_cols :]], -1)[None]
    accepted_kv = jnp.einsum(
        "rat,rtc->rac", accept.astype(jnp.bfloat16), kv_new, preferred_element_type=jnp.float32
    ).astype(jnp.bfloat16)
    resid = lax.dynamic_index_in_dim(gathered, row_index, 0, False)
    exp_here = w_in.shape[0]
    expert_count = exp_here * count_gx
    top_k = routing.shape[1]
    most_rows = 3 * tok_rows * top_k // (2 * expert_count)
    hidden_units = w_down.shape[1]
    gain_float = ffn_gain.astype(jnp.float32)
    tokens = routing.shape[0]
    slots = count_gx * most_rows
    own_experts = row_index * exp_here + jnp.arange(exp_here, dtype=jnp.int32)
    matched = routing[:, None, :] == own_experts[None, :, None]
    hits = jnp.any(matched, -1)
    weights = jnp.sum(jnp.where(matched, route_weight[:, None, :], 0.0), -1)
    order = jnp.arange(tok_rows, dtype=jnp.int32)
    earlier = (order[:, None] > order[None, :]).astype(jnp.bfloat16)
    rank = jnp.einsum(
        "tu,bue->bte",
        earlier,
        hits.astype(jnp.bfloat16).reshape(count_gx, tok_rows, exp_here),
        preferred_element_type=jnp.float32,
    ).astype(jnp.int32)
    first_slot = jnp.arange(count_gx, dtype=jnp.int32)[:, None, None] * most_rows
    slot_of = jnp.where(hits, (rank + first_slot).reshape(tokens, exp_here), -1)
    pick = slot_of.T[:, None, :] == jnp.arange(slots, dtype=jnp.int32)[None, :, None]
    pick_matrix = pick.astype(jnp.bfloat16)
    slot_weight = jnp.sum(jnp.where(pick, weights.T[:, None, :], 0.0), -1)
    gathered = gathered.reshape(tokens, cols_here).astype(jnp.float32)
    token_squares = jnp.sum(gathered * gathered, -1)
    slot_squares = jnp.sum(jnp.where(pick, token_squares, 0.0), -1)
    piece = 16
    slot_squares = jnp.pad(slot_squares.reshape(-1, piece), ((0, 0), (0, 128 - piece)))
    scaled = (gathered * gain_float).astype(jnp.bfloat16)
    rows = jnp.einsum(
        "est,td->esd", pick_matrix, scaled, preferred_element_type=jnp.float32
    ).astype(jnp.bfloat16)
    layer_out = expert_layer(
        rows,
        slot_squares,
        w_in,
        w_down,
        slot_weight[..., None],
        pick_matrix.reshape(exp_here * slots, tokens),
        resid,
        model_width,
        4,
    )
    return (layer_out, accepted_kv)


def solution(mesh):
    in_specs = (
        P("gx", None),
        P(),
        P(None, "gy"),
        P(),
        P(),
        P("gx", "gy", None),
        P("gx", "gy", None),
        P("gx"),
        P("gx", None, None),
        P(None, "gy"),
        P("gy"),
        P(),
        P(),
        P("gx", "gy", None),
        P("gx", None, "gy"),
        P("gx", None, None),
    )
    out_specs = (P("gx", "gy"), P("gx", None, None))
    return jax.shard_map(body, mesh=mesh, in_specs=in_specs, out_specs=out_specs, check_vma=False)
```

```python
import math

import jax
import jax.numpy as jnp
from jax import lax
from jax.experimental import pallas as pl
from jax.experimental.pallas import tpu as pltpu
from jax.sharding import PartitionSpec as P

EPS = 1e-06
NEG = -1e30
THETA_LOG = math.log(1000000.0)


MESH = pl.DeviceIdType.MESH


def exchange(arrays, axis, scatter, cid):
    count = lax.axis_size(axis)
    number = len(arrays)

    def kernel(*refs):
        ins, outs = refs[:number], refs[number : 2 * number]
        send, recv, local = refs[2 * number :]
        me = lax.axis_index(axis)
        barrier = pltpu.get_barrier_semaphore()
        for d in range(1, count):
            pl.semaphore_signal(
                barrier, inc=1, device_id={axis: lax.rem(me + d, count)}, device_id_type=MESH
            )
        pl.semaphore_wait(barrier, count - 1)
        copies = []
        for d in range(1, count):
            peer = lax.rem(me + d, count)
            for i in range(number):
                copy = pltpu.make_async_remote_copy(
                    src_ref=ins[i].at[peer] if scatter else ins[i],
                    dst_ref=outs[i].at[me],
                    send_sem=send.at[i, d],
                    recv_sem=recv.at[i, d],
                    device_id={axis: peer},
                    device_id_type=MESH,
                )
                copy.start()
                copies.append(copy)
        own = []
        for i in range(number):
            copy = pltpu.make_async_copy(
                ins[i].at[me] if scatter else ins[i], outs[i].at[me], local.at[i]
            )
            copy.start()
            own.append(copy)
        for copy in own + copies:
            copy.wait()

    outs = [
        jax.ShapeDtypeStruct(x.shape if scatter else (count,) + x.shape, x.dtype) for x in arrays
    ]
    return pl.pallas_call(
        kernel,
        out_shape=outs,
        in_specs=[pl.BlockSpec(memory_space=pltpu.VMEM)] * number,
        out_specs=[pl.BlockSpec(memory_space=pltpu.VMEM)] * number,
        scratch_shapes=[
            pltpu.SemaphoreType.DMA((number, count)),
            pltpu.SemaphoreType.DMA((number, count)),
            pltpu.SemaphoreType.DMA((number,)),
        ],
        compiler_params=pltpu.CompilerParams(collective_id=cid, has_side_effects=True),
        name="exchange_%d" % cid,
    )(*arrays)


def expert_layer(rows, squares, w_in, w_down, slot_weight, pick_back, resid, model_width, cid):
    axis = "gy"
    count = lax.axis_size(axis)
    peers = lax.axis_size("gx")
    experts, slots, depth = rows.shape
    tokens, cols = resid.shape
    wide = w_in.shape[2]
    units = wide // 2
    half = experts // 2
    piece = 16
    sub = slots // piece
    chunks = half * sub
    hop = 2
    far = hop * (count - 1)

    def kernel(
        x_ref, sq_ref, weight_ref, pick_ref, resid_ref, w_hbm, d_hbm, out_ref,
        hid_ref, wbuf, dbuf, part, rbuf, sqbuf, inv_ref, obuf, pbuf, ret,
        wsem, dsem, rs_s, rs_r, h_s, h_r, sq_s, sq_r, g_s, g_r,
    ):
        me = lax.axis_index(axis)
        prev = lax.rem(me + count - 1, count)
        nxt = lax.rem(me + 1, count)
        at_low = me == 0
        at_high = me == count - 1

        def load(e):
            return pltpu.make_async_copy(w_hbm.at[e], wbuf.at[e], wsem.at[e])

        def load_down(e):
            return pltpu.make_async_copy(d_hbm.at[e], dbuf.at[e], dsem.at[e])

        row = lax.axis_index("gx")
        for s in range(half):
            load(half + s).start()
            load(s).start()
        for s in range(half):
            load_down(half + s).start()
            load_down(s).start()
        barrier = pltpu.get_barrier_semaphore()
        for d in range(1, count):
            pl.semaphore_signal(
                barrier, inc=1, device_id={axis: lax.rem(me + d, count)}, device_id_type=MESH
            )
        for d in range(1, peers):
            pl.semaphore_signal(
                barrier, inc=1, device_id={"gx": lax.rem(row + d, peers)}, device_id_type=MESH
            )

        def multiply(h, s):
            e = h * half + s
            load(e).wait()
            value = jnp.dot(x_ref[e], wbuf[e], preferred_element_type=jnp.float32)
            for j in range(sub):
                part[h, s * sub + j] = value[j * piece : (j + 1) * piece].astype(jnp.bfloat16)

        multiply(1, 0)
        multiply(0, 0)
        pl.semaphore_wait(barrier, count + peers - 2)

        def sq_copy(d):
            return pltpu.make_async_remote_copy(
                src_ref=sq_ref,
                dst_ref=sqbuf.at[d],
                send_sem=sq_s.at[d],
                recv_sem=sq_r.at[d],
                device_id={axis: lax.rem(me + d, count)},
                device_id_type=MESH,
            )

        for d in range(1, count):
            sq_copy(d).start()

        def finish_squares():
            total = sq_ref[...]
            for d in range(1, count):
                sq_copy(d).wait()
                total = total + sqbuf[d]
            inv_ref[...] = lax.rsqrt(total / model_width + EPS)

        diagonal = lax.broadcasted_iota(jnp.int32, (piece, 128), 0) == lax.broadcasted_iota(
            jnp.int32, (piece, 128), 1
        )

        def rs_copy(h, c):
            return pltpu.make_async_remote_copy(
                src_ref=part.at[h, c],
                dst_ref=rbuf.at[h, c],
                send_sem=rs_s.at[h, c],
                recv_sem=rs_r.at[h, c],
                device_id={axis: nxt if h else prev},
                device_id_type=MESH,
            )

        def hid_copy(h, c):
            return pltpu.make_async_remote_copy(
                src_ref=hid_ref.at[h, c],
                dst_ref=hid_ref.at[h, c],
                send_sem=h_s.at[h, c],
                recv_sem=h_r.at[h, c],
                device_id={axis: prev if h else nxt},
                device_id_type=MESH,
            )

        def ends(h):
            return (at_low, at_high) if h else (at_high, at_low)

        def reduce_chunk(h, c):
            first, last = ends(h)

            @pl.when(jnp.logical_not(first))
            def _():
                rs_copy(h, c).wait_recv()

            @pl.when(jnp.logical_not(jnp.logical_or(first, last)))
            def _():
                part[h, c] = (
                    part[h, c].astype(jnp.float32) + rbuf[h, c].astype(jnp.float32)
                ).astype(jnp.bfloat16)

            @pl.when(jnp.logical_not(last))
            def _():
                rs_copy(h, c).start()

            @pl.when(last)
            def _():
                row = inv_ref[pl.ds(h * chunks + c, 1), :]
                inverse = jnp.sum(jnp.where(diagonal, row, 0.0), 1, keepdims=True)
                summed = part[h, c].astype(jnp.float32) + rbuf[h, c].astype(jnp.float32)
                gate = summed[:, :units] * inverse
                up = summed[:, units:] * inverse
                hid_ref[h, c] = (gate / (1.0 + jnp.exp(-gate)) * up).astype(jnp.bfloat16)
                hid_copy(h, c).start()

        def return_chunk(h, c):
            first, last = ends(h)

            @pl.when(jnp.logical_not(last))
            def _():
                hid_copy(h, c).wait_recv()

            @pl.when(jnp.logical_not(jnp.logical_or(first, last)))
            def _():
                hid_copy(h, c).start()

        def project(h, s):
            e = h * half + s
            load_down(e).wait()
            value = hid_ref[h, pl.ds(s * sub, sub)].reshape(slots, units)
            value = jnp.dot(value, dbuf[e], preferred_element_type=jnp.float32)
            obuf[e] = (value * weight_ref[e]).astype(jnp.bfloat16)

        def step(t, carry):
            for h, place in ((1, 1), (0, sub // 2 + 1)):

                @pl.when(jnp.logical_and(t < chunks - sub, lax.rem(t, sub) == place))
                def _():
                    multiply(h, lax.div(t, sub) + 1)

            @pl.when(t == far - 1)
            def _():
                finish_squares()

            for h in (1, 0):
                way = hop * (me if h else count - 1 - me)
                c = t - way

                @pl.when(jnp.logical_and(c >= 0, c < chunks))
                def _():
                    reduce_chunk(h, c)

            for h in (1, 0):
                way = hop * (me if h else count - 1 - me)
                b = t - 2 * far + way

                @pl.when(jnp.logical_and(b >= 0, b < chunks))
                def _():
                    return_chunk(h, b)

                    @pl.when(lax.rem(b, sub) == sub - 1)
                    def _():
                        project(h, lax.div(b, sub))

            return carry

        lax.fori_loop(0, chunks + 2 * far, step, 0)

        def finish(c, carry):
            for h in (1, 0):
                first, last = ends(h)

                @pl.when(jnp.logical_not(last))
                def _():
                    rs_copy(h, c).wait_send()

                @pl.when(jnp.logical_not(first))
                def _():
                    hid_copy(h, c).wait_send()

            return carry

        summed = lax.dot_general(
            pick_ref[...],
            obuf[...].reshape(experts * slots, cols),
            (((0,), (0,)), ((), ())),
            preferred_element_type=jnp.float32,
        )
        for p in range(peers):
            pbuf[p] = summed[p * tokens : (p + 1) * tokens].astype(jnp.bfloat16)

        def back_copy(d):
            peer = lax.rem(row + d, peers)
            return pltpu.make_async_remote_copy(
                src_ref=pbuf.at[peer],
                dst_ref=ret.at[d],
                send_sem=g_s.at[d],
                recv_sem=g_r.at[d],
                device_id={"gx": peer},
                device_id_type=MESH,
            )

        for d in range(1, peers):
            back_copy(d).start()
        moe = pbuf[row].astype(jnp.float32)
        lax.fori_loop(0, chunks, finish, 0)
        for d in range(1, peers):
            back_copy(d).wait_recv()
            moe = moe + ret[d].astype(jnp.float32)
        out_ref[...] = (resid_ref[...].astype(jnp.float32) + moe).astype(jnp.bfloat16)
        for d in range(1, peers):
            back_copy(d).wait_send()

    vmem = pl.BlockSpec(memory_space=pltpu.VMEM)
    hbm = pl.BlockSpec(memory_space=pl.ANY)
    dma = pltpu.SemaphoreType.DMA
    return pl.pallas_call(
        kernel,
        out_shape=jax.ShapeDtypeStruct((tokens, cols), jnp.bfloat16),
        in_specs=[vmem] * 5 + [hbm, hbm],
        out_specs=vmem,
        scratch_shapes=[
            pltpu.VMEM((2, chunks, piece, units), jnp.bfloat16),
            pltpu.VMEM((experts, depth, wide), jnp.bfloat16),
            pltpu.VMEM((experts, units, cols), jnp.bfloat16),
            pltpu.VMEM((2, chunks, piece, wide), jnp.bfloat16),
            pltpu.VMEM((2, chunks, piece, wide), jnp.bfloat16),
            pltpu.VMEM((count, 2 * chunks, 128), jnp.float32),
            pltpu.VMEM((2 * chunks, 128), jnp.float32),
            pltpu.VMEM((experts, slots, cols), jnp.bfloat16),
            pltpu.VMEM((peers, tokens, cols), jnp.bfloat16),
            pltpu.VMEM((peers, tokens, cols), jnp.bfloat16),
            dma((experts,)),
            dma((experts,)),
            dma((2, chunks)),
            dma((2, chunks)),
            dma((2, chunks)),
            dma((2, chunks)),
            dma((count,)),
            dma((count,)),
            dma((peers,)),
            dma((peers,)),
        ],
        compiler_params=pltpu.CompilerParams(
            collective_id=cid, has_side_effects=True, vmem_limit_bytes=52 * 1024 * 1024
        ),
        name="expert_layer",
    )(rows, squares, slot_weight, pick_back, resid, w_in, w_down)


def attention_block(
    qkv, q_gain, k_gain, cosine, sine, cache_k, cache_v, limit, tree_mask, states_here, w_o, cid
):
    blocks = lax.axis_size("gy")
    rows_gx = lax.axis_size("gx")
    tokens = qkv.shape[0]
    span, kv_cols = cache_k.shape
    dim = q_gain.shape[1]
    kv_heads = kv_cols // dim
    heads = qkv.shape[1] // dim - 2 * kv_heads
    group = heads // kv_heads
    per_block = heads // blocks
    blocks_here = blocks // kv_heads
    width = per_block * dim
    cols = w_o.shape[1]
    scale = dim ** (-0.5)

    def kernel(
        limit_ref, q_ref, qg_ref, kg_ref, cos_ref, sin_ref, k_ref, v_ref, mask_ref, st_ref, wo_hbm,
        h_ref, rot_ref,
        acc_out, stat_out, acc_in, stat_in, attn, wo,
        wo_sem, a_s, a_r, s_s, s_r, t_s, t_r, h_s, h_r,
    ):
        me = lax.axis_index("gy")
        row = lax.axis_index("gx")
        load = pltpu.make_async_copy(wo_hbm, wo, wo_sem)
        load.start()
        barrier = pltpu.get_barrier_semaphore()
        for axis, here, count in (("gy", me, blocks), ("gx", row, rows_gx)):
            for d in range(1, count):
                pl.semaphore_signal(
                    barrier, inc=1, device_id={axis: lax.rem(here + d, count)}, device_id_type=MESH
                )
        pl.semaphore_wait(barrier, blocks + rows_gx - 2)

        def send(src, dst, send_sem, recv_sem, axis, peer):
            return pltpu.make_async_remote_copy(
                src_ref=src,
                dst_ref=dst,
                send_sem=send_sem,
                recv_sem=recv_sem,
                device_id={axis: peer},
                device_id_type=MESH,
            )

        def part_copies(block, source):
            return (
                send(acc_out.at[block], acc_in.at[source], a_s.at[block], a_r.at[source], "gy", block),
                send(stat_out.at[block], stat_in.at[source], s_s.at[block], s_r.at[source], "gy", block),
            )

        cos = cos_ref[...]
        sin = sin_ref[...]

        def turn(value, gain):
            value = value.astype(jnp.float32)
            value = value * lax.rsqrt(jnp.mean(value * value, -1, keepdims=True) + EPS) * gain
            return (value * cos + pltpu.roll(value, dim // 2, 1) * sin).astype(jnp.bfloat16)

        q_gain_row = qg_ref[...].astype(jnp.float32)
        k_gain_row = kg_ref[...].astype(jnp.float32)
        contract = (((1,), (1,)), ((), ()))
        diagonal = lax.broadcasted_iota(jnp.int32, (tokens, 128), 0) == lax.broadcasted_iota(
            jnp.int32, (tokens, 128), 1
        )

        def one_head(i, carry):
            g = lax.rem(lax.div(me, blocks_here) + 1 + i, kv_heads)

            def lanes(first, size):
                return pl.ds(pl.multiple_of(first, 128), size)

            query = jnp.concatenate(
                [
                    turn(q_ref[:, lanes((g * group + j) * dim, dim)], q_gain_row)
                    for j in range(group)
                ],
                0,
            )
            keys = turn(q_ref[:, lanes((heads + g) * dim, dim)], k_gain_row)
            values = q_ref[:, lanes((heads + kv_heads + g) * dim, dim)]
            rot_ref[:, lanes(g * dim, dim)] = keys
            tree = (
                lax.dot_general(query, keys, contract, preferred_element_type=jnp.float32) * scale
            )
            mask = jnp.concatenate([mask_ref[...]] * group, 0)
            tree_ok = jnp.logical_and(mask == 1, me == 0)
            tree = jnp.where(tree_ok, tree, NEG)
            score = (
                lax.dot_general(
                    query,
                    k_ref[:, lanes(g * dim, dim)],
                    contract,
                    preferred_element_type=jnp.float32,
                )
                * scale
            )
            valid = lax.broadcasted_iota(jnp.int32, score.shape, 1) < limit_ref[0]
            score = jnp.where(valid, score, NEG)
            top = jnp.maximum(jnp.max(score, 1, keepdims=True), jnp.max(tree, 1, keepdims=True))
            prob = jnp.where(valid, jnp.exp(score - top), 0.0).astype(jnp.bfloat16)
            prob_tree = jnp.where(tree_ok, jnp.exp(tree - top), 0.0).astype(jnp.bfloat16)
            total = jnp.sum(prob.astype(jnp.float32), 1, keepdims=True) + jnp.sum(
                prob_tree.astype(jnp.float32), 1, keepdims=True
            )
            acc = jnp.dot(prob, v_ref[:, lanes(g * dim, dim)], preferred_element_type=jnp.float32)
            acc = acc + jnp.dot(prob_tree, values, preferred_element_type=jnp.float32)
            acc = acc.astype(jnp.bfloat16)
            for b in range(blocks_here):
                block = g * blocks_here + b
                for place in range(per_block):
                    j = b * per_block + place
                    rows = slice(j * tokens, (j + 1) * tokens)
                    acc_out[block, :, place * dim : (place + 1) * dim] = acc[rows]
                    for k, column in enumerate((top, total)):
                        stat_out[block, k * per_block + place : k * per_block + place + 1, :] = (
                            jnp.sum(jnp.where(diagonal, column[rows], 0.0), 0, keepdims=True)
                        )

                @pl.when(block != me)
                def _():
                    for copy in part_copies(block, me):
                        copy.start()

            return carry

        lax.fori_loop(0, kv_heads, one_head, 0)

        acc_in[me] = acc_out[me]
        stat_in[me] = stat_out[me]
        for d in range(1, blocks):
            source = lax.rem(me + d, blocks)
            for copy in part_copies(source, source):
                copy.wait_recv()
        tops = [stat_in[j, :per_block, :] for j in range(blocks)]
        best = tops[0]
        for j in range(1, blocks):
            best = jnp.maximum(best, tops[j])
        factors = [jnp.exp(tops[j] - best) for j in range(blocks)]
        denom = stat_in[0, per_block:, :] * factors[0]
        for j in range(1, blocks):
            denom = denom + stat_in[j, per_block:, :] * factors[j]
        for place in range(per_block):
            joined = jnp.zeros((tokens, dim), jnp.float32)
            for j in range(blocks):
                line = (factors[j] / denom)[place : place + 1, :]
                column = jnp.sum(jnp.where(diagonal, line, 0.0), 1, keepdims=True)
                joined = joined + column * acc_in[
                    j, :, place * dim : (place + 1) * dim
                ].astype(jnp.float32)
            attn[me, :, place * dim : (place + 1) * dim] = joined.astype(jnp.bfloat16)

        def attn_copy(d, source):
            return send(
                attn.at[source], attn.at[source], t_s.at[d], t_r.at[d], "gy", lax.rem(me + d, blocks)
            )

        for d in range(1, blocks):
            attn_copy(d, me).start()
        load.wait()

        def project(source):
            return jnp.dot(
                attn[source],
                wo[pl.ds(pl.multiple_of(source * width, width), width), :],
                preferred_element_type=jnp.float32,
            )

        total = st_ref[...].astype(jnp.float32) + project(me)
        for d in range(1, blocks):
            source = lax.rem(me + blocks - d, blocks)
            attn_copy(d, source).wait_recv()
            total = total + project(source)
        h_ref[row] = total.astype(jnp.bfloat16)

        def h_copy(d, source):
            return send(
                h_ref.at[source], h_ref.at[source], h_s.at[d], h_r.at[d], "gx",
                lax.rem(row + d, rows_gx),
            )

        for d in range(1, rows_gx):
            h_copy(d, row).start()
        for d in range(1, blocks):
            block = lax.rem(me + d, blocks)
            for copy in part_copies(block, me):
                copy.wait_send()
            attn_copy(d, me).wait_send()
        for d in range(1, rows_gx):
            h_copy(d, lax.rem(row + rows_gx - d, rows_gx)).wait_recv()
            h_copy(d, row).wait_send()

    vmem = pl.BlockSpec(memory_space=pltpu.VMEM)
    dma = pltpu.SemaphoreType.DMA
    return pl.pallas_call(
        kernel,
        out_shape=[
            jax.ShapeDtypeStruct((rows_gx, tokens, cols), jnp.bfloat16),
            jax.ShapeDtypeStruct((tokens, kv_cols), jnp.bfloat16),
        ],
        in_specs=[pl.BlockSpec(memory_space=pltpu.SMEM)]
        + [vmem] * 9
        + [pl.BlockSpec(memory_space=pl.ANY)],
        out_specs=[vmem, vmem],
        scratch_shapes=[
            pltpu.VMEM((blocks, tokens, width), jnp.bfloat16),
            pltpu.VMEM((blocks, 2 * per_block, 128), jnp.float32),
            pltpu.VMEM((blocks, tokens, width), jnp.bfloat16),
            pltpu.VMEM((blocks, 2 * per_block, 128), jnp.float32),
            pltpu.VMEM((blocks, tokens, width), jnp.bfloat16),
            pltpu.VMEM(w_o.shape, jnp.bfloat16),
            dma,
            dma((blocks,)),
            dma((blocks,)),
            dma((blocks,)),
            dma((blocks,)),
            dma((blocks,)),
            dma((blocks,)),
            dma((rows_gx,)),
            dma((rows_gx,)),
        ],
        compiler_params=pltpu.CompilerParams(
            collective_id=cid, has_side_effects=True, vmem_limit_bytes=48 * 1024 * 1024
        ),
        name="attention_block",
    )(
        limit, qkv, q_gain, k_gain, cosine, sine, cache_k, cache_v, tree_mask, states_here, w_o
    )


def layer_line(
    states, attn_gain, w_qkv, q_gain, k_gain, cache_k, cache_v, cache_len, tree_mask, w_o, accept,
    ffn_gain, routing, route_weight, w_in, w_down, cid
):
    count = lax.axis_size("gy")
    rows_gx = lax.axis_size("gx")
    tokens, model = states.shape
    span, kv_cols = cache_k.shape
    dim = q_gain.shape[1]
    kv_heads = kv_cols // dim
    own = w_qkv.shape[1] // dim
    heads = own * count - 2 * kv_heads
    group = heads // kv_heads
    cols = w_o.shape[1]
    chunks = own // 2
    part = group // 2
    steps = heads // part
    first_relay = 2
    lag = 3
    rows = part * tokens
    lane = 128
    accepted = accept.shape[0]
    last = count - 1
    factor = dim ** (-0.5) / math.log(2.0)
    top_k, everyone = routing.shape
    experts, depth, wide = w_in.shape
    units = wide // 2
    most_rows = 3 * tokens * top_k // (2 * experts * rows_gx)
    slots = rows_gx * most_rows
    split = experts // 2
    grain = 16
    sub = slots // grain
    strips = split * sub
    hop = 4
    far = hop * last

    def kernel(
        len_ref, st_ref, ag_ref, qg_ref, kg_ref, mask_ref, acc_ref, fg_ref, rt_ref, rw_ref,
        wq_hbm, k_hbm, v_hbm, wo_hbm, w_hbm, d_hbm,
        out_ref, akv_ref,
        normed, wq, qall, kext, vext, wo, bias, tree_bias,
        own_acc, own_stat, end_out, end_in, stat_in, mid_out, mid_in, mstat_out, mstat_in,
        attn, total, akv,
        wq_sem, k_sem, v_sem, wo_sem, q_s, q_r, e_s, e_r, es_s, es_r, m_s, m_r, ms_s, ms_r,
        f_s, f_r, a_s, a_r, h_s, h_r,
        h_all, scaled, pick, wcol, sq_out, sq_in, inv_row, hid, wbuf, dbuf, part_sum, rbuf, obuf, pbuf, ret,
        w_sem, d_sem, sq_s, sq_r, rs_s, rs_r, hid_s, hid_r, g_s, g_r,
    ):
        me = lax.axis_index("gy")
        row = lax.axis_index("gx")
        is_last = me == last
        is_end = jnp.logical_or(me == 0, is_last)
        is_mid = jnp.logical_not(is_end)
        low = me < 2
        mid_of = jnp.where(low, 1, 2)
        end_of = jnp.where(low, 0, last)
        other_mid = 3 - mid_of

        def send(src, dst, send_sem, recv_sem, axis, peer):
            return pltpu.make_async_remote_copy(
                src_ref=src,
                dst_ref=dst,
                send_sem=send_sem,
                recv_sem=recv_sem,
                device_id={axis: peer},
                device_id_type=MESH,
            )

        def chunk_at(i):
            return jnp.where(is_last, i, chunks - 1 - i)

        def load_w(c):
            return pltpu.make_async_copy(
                wq_hbm.at[:, pl.ds(pl.multiple_of(c * 2 * dim, 2 * dim), 2 * dim)],
                wq.at[c],
                wq_sem.at[c],
            )

        def load_k(g):
            return pltpu.make_async_copy(
                k_hbm.at[:, g * dim : (g + 1) * dim], kext.at[g, 0:span, :], k_sem.at[g]
            )

        def load_v(g):
            return pltpu.make_async_copy(
                v_hbm.at[:, g * dim : (g + 1) * dim], vext.at[g, 0:span, 0:dim], v_sem.at[g]
            )

        load_o = pltpu.make_async_copy(wo_hbm, wo, wo_sem)
        for i in range(chunks):
            load_w(chunk_at(i)).start()
        for g in range(kv_heads - 1, -1, -1):
            load_k(g).start()
            load_v(g).start()
        load_o.start()
        barrier = pltpu.get_barrier_semaphore()
        for axis, here, number in (("gy", me, count), ("gx", row, rows_gx)):
            for d in range(1, number):
                pl.semaphore_signal(
                    barrier, inc=1, device_id={axis: lax.rem(here + d, number)}, device_id_type=MESH
                )

        value = st_ref[...].astype(jnp.float32)
        value = value * lax.rsqrt(jnp.mean(value * value, -1, keepdims=True) + EPS)
        normed[...] = (value * ag_ref[...].reshape(1, model).astype(jnp.float32)).astype(jnp.bfloat16)
        mask = mask_ref[...]
        position = len_ref[0] + jnp.sum(mask, -1, keepdims=True) - 1
        place = lax.broadcasted_iota(jnp.int32, (tokens, dim), 1)
        half = lax.rem(place, dim // 2).astype(jnp.float32)
        angle = position.astype(jnp.float32) * jnp.exp(half * (-2.0 * THETA_LOG / dim))
        cos = jnp.cos(angle)
        sin = jnp.sin(angle)
        sin = jnp.where(place < dim // 2, -sin, sin)
        limit = len_ref[0] - me * span
        spot = lax.broadcasted_iota(jnp.int32, (1, span), 1)
        bias[...] = jnp.where(spot < limit, 0.0, NEG)
        allowed = jnp.logical_and(mask == 1, is_last)
        tree_bias[...] = jnp.full((tokens, lane), NEG, jnp.float32)
        tree_bias[:, 0:tokens] = jnp.where(allowed, 0.0, NEG)
        for g in range(kv_heads):
            kext[g, span : span + lane, :] = jnp.zeros((lane, dim), jnp.bfloat16)
            vext[g, span : span + lane, 0:dim] = jnp.zeros((lane, dim), jnp.bfloat16)
            vext[g, :, dim : 2 * dim] = jnp.ones((span + lane, dim), jnp.bfloat16)
        total[...] = st_ref[:, pl.ds(pl.multiple_of(me * cols, 128), cols)].astype(jnp.float32)
        q_gain_row = qg_ref[...].astype(jnp.float32)
        k_gain_row = kg_ref[...].astype(jnp.float32)

        def q_copy(k, c, peer):
            block = qall.at[pl.ds(2 * k, 2)]
            return send(block, block, q_s.at[peer, c], q_r.at[k], "gy", peer)

        relay = me == last - 1

        def direct(k, peer):
            far_pair = jnp.logical_and(me == 0, peer == last)
            there = jnp.logical_and(me != peer, jnp.logical_not(far_pair))
            return jnp.logical_and(there, 2 * k < heads)

        def relay_copy(k):
            return q_copy(k, chunks + k, last)

        pl.semaphore_wait(barrier, count + rows_gx - 2)

        def project_in(i, carry):
            c = chunk_at(i)
            load_w(c).wait()
            value = jnp.dot(normed[...], wq[c], preferred_element_type=jnp.float32)
            value = value.astype(jnp.bfloat16)
            k = me * chunks + c
            for j in range(2):
                head = 2 * k + j
                raw = value[:, j * dim : (j + 1) * dim]
                turned = raw.astype(jnp.float32)
                gain = jnp.where(head < heads, q_gain_row, k_gain_row)
                scale = lax.rsqrt(jnp.mean(turned * turned, -1, keepdims=True) + EPS)
                turned = turned * scale * gain
                turned = (turned * cos + pltpu.roll(turned, dim // 2, 1) * sin).astype(jnp.bfloat16)
                qall[head] = jnp.where(head < heads + kv_heads, turned, raw)
            for peer in range(count - 1, -1, -1):

                @pl.when(direct(k, peer))
                def _():
                    q_copy(k, c, peer).start()

            return carry

        lax.fori_loop(0, chunks, project_in, 0)

        def load_in(e):
            return pltpu.make_async_copy(w_hbm.at[e], wbuf.at[e], w_sem.at[e])

        def load_down(e):
            return pltpu.make_async_copy(d_hbm.at[e], dbuf.at[e], d_sem.at[e])

        for e in range(split):
            load_in(split + e).start()
            load_in(e).start()
        for e in range(split):
            load_down(split + e).start()
            load_down(e).start()

        names = rt_ref[...]
        shares = rw_ref[...]
        hits, weights = [], []
        for e in range(experts):
            matched = names == row * experts + e
            hits.append(jnp.sum(jnp.where(matched, 1.0, 0.0), 0, keepdims=True))
            weights.append(jnp.sum(jnp.where(matched, shares, 0.0), 0, keepdims=True))
        hit = jnp.concatenate(hits, 0)
        before = lax.broadcasted_iota(jnp.int32, (lane, lane), 0)
        after = lax.broadcasted_iota(jnp.int32, (lane, lane), 1)
        same = lax.div(before, tokens) == lax.div(after, tokens)
        earlier = jnp.where(jnp.logical_and(before < after, same), 1.0, 0.0).astype(jnp.bfloat16)
        rank = jnp.concatenate(
            [
                jnp.dot(
                    hit[:, i : i + lane].astype(jnp.bfloat16),
                    earlier,
                    preferred_element_type=jnp.float32,
                )
                for i in range(0, everyone, lane)
            ],
            1,
        )
        block_no = lax.div(lax.broadcasted_iota(jnp.int32, (experts, everyone), 1), tokens)
        slot_of = jnp.where(hit > 0.5, rank + (block_no * most_rows).astype(jnp.float32), -1.0)
        slot_no = lax.broadcasted_iota(jnp.int32, (slots, everyone), 0).astype(jnp.float32)
        for e in range(experts):
            chosen = slot_no == slot_of[e : e + 1]
            pick[e] = jnp.where(chosen, 1.0, 0.0).astype(jnp.bfloat16)
            column = jnp.sum(jnp.where(chosen, weights[e], 0.0), 1, keepdims=True)
            wcol[e] = jnp.broadcast_to(column, (slots, lane))

        def akv_copy(d, peer):
            return send(akv, akv, a_s.at[d], a_r, "gy", peer)

        @pl.when(is_last)
        def _():
            pick = acc_ref[...].astype(jnp.bfloat16)
            akv[...] = jnp.zeros(akv.shape, jnp.bfloat16)
            for i in range(2 * kv_heads):
                akv[0:accepted, i * dim : (i + 1) * dim] = jnp.dot(
                    pick, qall[heads + i], preferred_element_type=jnp.float32
                ).astype(jnp.bfloat16)
            for d in range(last):
                akv_copy(d, d).start()
            for g in range(kv_heads):
                kext[g, span : span + tokens, :] = qall[heads + g]
                vext[g, span : span + tokens, 0:dim] = qall[heads + kv_heads + g]

        diagonal = lax.broadcasted_iota(jnp.int32, (tokens, lane), 0) == lax.broadcasted_iota(
            jnp.int32, (tokens, lane), 1
        )

        def as_row(column):
            return jnp.sum(jnp.where(diagonal, column, 0.0), 0, keepdims=True)

        def as_column(line):
            return jnp.sum(jnp.where(diagonal, line, 0.0), 1, keepdims=True)

        contract = (((1,), (1,)), ((), ()))

        def end_copy(s):
            return (
                send(end_out.at[s], end_in.at[s], e_s.at[s], e_r.at[s], "gy", mid_of),
                send(own_stat.at[s], stat_in.at[s], es_s.at[s], es_r.at[s], "gy", mid_of),
            )

        def mid_copy(s):
            return (
                send(mid_out.at[s], mid_in.at[s], m_s.at[s], m_r.at[s], "gy", other_mid),
                send(mstat_out.at[s], mstat_in.at[s], ms_s.at[s], ms_r.at[s], "gy", other_mid),
            )

        def block_of(s):
            return steps - 1 - s

        def final_copy(s):
            place = attn.at[pl.ds(block_of(s) * part, part)]
            return send(place, place, f_s.at[s], f_r.at[s], "gy", end_of)

        def attend(s):
            b = block_of(s)
            for n in range(part // 2):
                k = b * (part // 2) + n
                source = lax.div(k, chunks)
                relayed = jnp.logical_and(relay, source == 0)

                @pl.when(jnp.logical_and(source != me, jnp.logical_not(relayed)))
                def _():
                    q_copy(k, 0, source).wait_recv()

            g = lax.div(b, 2)
            query = qall[pl.ds(b * part, part)].reshape(rows, dim)
            score = lax.dot_general(query, kext[g], contract, preferred_element_type=jnp.float32)
            cached = score[:, :span] + bias[...]
            tree = score[:, span:] + jnp.concatenate([tree_bias[...]] * part, 0)
            top = jnp.maximum(jnp.max(cached, 1, keepdims=True), jnp.max(tree, 1, keepdims=True))
            top = jnp.maximum(top, 0.5 * NEG)
            prob = jnp.concatenate(
                [
                    jnp.exp2((cached - top) * factor).astype(jnp.bfloat16),
                    jnp.exp2((tree - top) * factor).astype(jnp.bfloat16),
                ],
                1,
            )
            out = jnp.dot(prob, vext[g], preferred_element_type=jnp.float32)
            for j in range(part):
                here = slice(j * tokens, (j + 1) * tokens)
                own_stat[s, j : j + 1, :] = as_row(top[here])
                own_stat[s, part + j : part + j + 1, :] = as_row(out[here, dim:])

            @pl.when(is_end)
            def _():
                end_out[s] = out[:, :dim].astype(jnp.bfloat16)
                for copy in end_copy(s):
                    copy.start()

            @pl.when(is_mid)
            def _():
                own_acc[s] = out[:, :dim]

        def join(s):
            for copy in end_copy(s):
                copy.wait_recv()
            a, b = own_stat[s, :part, :], stat_in[s, :part, :]
            top = jnp.maximum(a, b)
            fa, fb = jnp.exp2((a - top) * factor), jnp.exp2((b - top) * factor)
            mstat_out[s, :part, :] = top
            mstat_out[s, part:, :] = own_stat[s, part:, :] * fa + stat_in[s, part:, :] * fb
            for j in range(part):
                here = slice(j * tokens, (j + 1) * tokens)
                value = own_acc[s, here, :] * as_column(fa[j : j + 1])
                value = value + end_in[s, here, :].astype(jnp.float32) * as_column(fb[j : j + 1])
                own_acc[s, here, :] = value
                mid_out[s, here, :] = value.astype(jnp.bfloat16)
            for copy in mid_copy(s):
                copy.start()

        def project_out(s):
            b = block_of(s)
            value = jnp.concatenate([attn[b * part + j] for j in range(part)], 1)
            weight = wo[pl.ds(pl.multiple_of(b * part * dim, part * dim), part * dim), :]
            total[...] += jnp.dot(value, weight, preferred_element_type=jnp.float32)

        def settle(s):
            for copy in mid_copy(s):
                copy.wait_recv()
            a, b = mstat_out[s, :part, :], mstat_in[s, :part, :]
            top = jnp.maximum(a, b)
            fa, fb = jnp.exp2((a - top) * factor), jnp.exp2((b - top) * factor)
            denom = mstat_out[s, part:, :] * fa + mstat_in[s, part:, :] * fb
            fa, fb = fa / denom, fb / denom
            for j in range(part):
                here = slice(j * tokens, (j + 1) * tokens)
                value = own_acc[s, here, :] * as_column(fa[j : j + 1])
                value = value + mid_in[s, here, :].astype(jnp.float32) * as_column(fb[j : j + 1])
                attn[block_of(s) * part + j] = value.astype(jnp.bfloat16)
            final_copy(s).start()
            project_out(s)

        for g in range(kv_heads):
            load_k(g).wait()
            load_v(g).wait()

        def step(t, carry):
            @pl.when(t < steps)
            def _():
                attend(t)

            k = chunks + first_relay - 1 - t

            @pl.when(jnp.logical_and(relay, jnp.logical_and(k >= 0, k < chunks)))
            def _():
                q_copy(k, 0, 0).wait_recv()
                relay_copy(k).start()

            @pl.when(t == 2)
            def _():
                load_o.wait()

            @pl.when(jnp.logical_and(is_mid, jnp.logical_and(t >= lag, t < steps + lag)))
            def _():
                join(t - lag)

            @pl.when(jnp.logical_and(is_mid, jnp.logical_and(t >= 2 * lag, t < steps + 2 * lag)))
            def _():
                settle(t - 2 * lag)

            @pl.when(jnp.logical_and(is_end, t >= 3 * lag))
            def _():
                final_copy(t - 3 * lag).wait_recv()
                project_out(t - 3 * lag)

            return carry

        lax.fori_loop(0, steps + 3 * lag, step, 0)
        h_all[row] = total[...].astype(jnp.bfloat16)

        def h_copy(d, source):
            return send(
                h_all.at[source], h_all.at[source], h_s.at[d], h_r.at[d], "gx",
                lax.rem(row + d, rows_gx),
            )

        for d in range(1, rows_gx):
            h_copy(d, row).start()

        @pl.when(is_last)
        def _():
            for d in range(last):
                akv_copy(d, d).wait_send()

        @pl.when(jnp.logical_not(is_last))
        def _():
            akv_copy(0, last).wait_recv()

        akv_ref[...] = akv[0:accepted, :]

        def sent(c, carry):
            k = me * chunks + c
            for peer in range(count):

                @pl.when(direct(k, peer))
                def _():
                    q_copy(k, c, peer).wait_send()

            return carry

        def relayed(k, carry):
            @pl.when(relay)
            def _():
                relay_copy(k).wait_send()

            return carry

        def done(s, carry):
            @pl.when(is_end)
            def _():
                for copy in end_copy(s):
                    copy.wait_send()

            @pl.when(is_mid)
            def _():
                for copy in mid_copy(s):
                    copy.wait_send()
                final_copy(s).wait_send()

            return carry

        gain = fg_ref[...].reshape(1, cols).astype(jnp.float32)
        for d in range(rows_gx):
            source = lax.rem(row + rows_gx - d, rows_gx)
            if d:
                h_copy(d, source).wait_recv()
            value = h_all[source].astype(jnp.float32)
            scaled[source] = (value * gain).astype(jnp.bfloat16)
        square_of = lax.broadcasted_iota(jnp.int32, (lane, lane), 0) == lax.broadcasted_iota(
            jnp.int32, (lane, lane), 1
        )

        def multiply(h, s):
            e = h * split + s
            load_in(e).wait()
            value = jnp.dot(
                pick[e], scaled[...].reshape(everyone, cols), preferred_element_type=jnp.float32
            ).astype(jnp.bfloat16)
            value = jnp.dot(value, wbuf[e], preferred_element_type=jnp.float32)
            for j in range(sub):
                part_sum[h, s * sub + j] = value[j * grain : (j + 1) * grain].astype(jnp.bfloat16)

        multiply(1, 0)
        multiply(0, 0)
        sq_out[...] = jnp.zeros(sq_out.shape, jnp.float32)
        for i in range(everyone // lane):
            value = h_all[pl.ds(i * (lane // tokens), lane // tokens)].reshape(lane, cols)
            value = value.astype(jnp.float32)
            column = jnp.sum(value * value, 1, keepdims=True)
            line = jnp.sum(jnp.where(square_of, column, 0.0), 0, keepdims=True)
            sq_out[0:1, i * lane : (i + 1) * lane] = line

        def sq_copy(d):
            return send(
                sq_out, sq_in.at[d], sq_s.at[d], sq_r.at[d], "gy", lax.rem(me + d, count)
            )

        for d in range(1, count):
            sq_copy(d).start()

        def finish_squares():
            whole = sq_out[0:1, :]
            for d in range(1, count):
                sq_copy(d).wait()
                whole = whole + sq_in[d, 0:1, :]
            inv_row[...] = lax.rsqrt(whole / model + EPS)

        prev = lax.rem(me + count - 1, count)
        nxt = lax.rem(me + 1, count)
        at_low = me == 0
        at_high = is_last

        def rs_copy(h, c):
            return send(
                part_sum.at[h, c], rbuf.at[h, c], rs_s.at[h, c], rs_r.at[h, c], "gy",
                nxt if h else prev,
            )

        def hid_copy(h, c):
            return send(
                hid.at[h, c], hid.at[h, c], hid_s.at[h, c], hid_r.at[h, c], "gy",
                prev if h else nxt,
            )

        def ends(h):
            return (at_low, at_high) if h else (at_high, at_low)

        def reduce_strip(h, c):
            first, final = ends(h)

            @pl.when(jnp.logical_not(first))
            def _():
                rs_copy(h, c).wait_recv()

            @pl.when(jnp.logical_not(jnp.logical_or(first, final)))
            def _():
                part_sum[h, c] = (
                    part_sum[h, c].astype(jnp.float32) + rbuf[h, c].astype(jnp.float32)
                ).astype(jnp.bfloat16)

            @pl.when(jnp.logical_not(final))
            def _():
                rs_copy(h, c).start()

            @pl.when(final)
            def _():
                e = h * split + lax.div(c, sub)
                at = pl.multiple_of(lax.rem(c, sub) * grain, grain)
                chosen = pick[e, pl.ds(at, grain), :].astype(jnp.float32)
                inverse = jnp.sum(chosen * inv_row[...], 1, keepdims=True)
                summed = part_sum[h, c].astype(jnp.float32) + rbuf[h, c].astype(jnp.float32)
                gate = summed[:, :units] * inverse
                up = summed[:, units:] * inverse
                hid[h, c] = (gate / (1.0 + jnp.exp(-gate)) * up).astype(jnp.bfloat16)
                hid_copy(h, c).start()

        def return_strip(h, c):
            first, final = ends(h)

            @pl.when(jnp.logical_not(final))
            def _():
                hid_copy(h, c).wait_recv()

            @pl.when(jnp.logical_not(jnp.logical_or(first, final)))
            def _():
                hid_copy(h, c).start()

        def project_down(h, s):
            e = h * split + s
            load_down(e).wait()
            value = hid[h, pl.ds(s * sub, sub)].reshape(slots, units)
            value = jnp.dot(value, dbuf[e], preferred_element_type=jnp.float32)
            obuf[e] = (value * wcol[e, :, 0:1]).astype(jnp.bfloat16)

        def moe_step(t, carry):
            for h, place in ((1, 1), (0, sub // 2 + 1)):

                @pl.when(jnp.logical_and(t < strips - sub, lax.rem(t, sub) == place))
                def _():
                    multiply(h, lax.div(t, sub) + 1)

            @pl.when(t == far - 1)
            def _():
                finish_squares()

            for h in (1, 0):
                way = hop * (me if h else last - me)
                c = t - way

                @pl.when(jnp.logical_and(c >= 0, c < strips))
                def _():
                    reduce_strip(h, c)

            for h in (1, 0):
                way = hop * (me if h else last - me)
                b = t - 2 * far + way

                @pl.when(jnp.logical_and(b >= 0, b < strips))
                def _():
                    return_strip(h, b)

                    @pl.when(lax.rem(b, sub) == sub - 1)
                    def _():
                        project_down(h, lax.div(b, sub))

            return carry

        lax.fori_loop(0, strips + 2 * far, moe_step, 0)

        def finish(c, carry):
            for h in (1, 0):
                first, final = ends(h)

                @pl.when(jnp.logical_not(final))
                def _():
                    rs_copy(h, c).wait_send()

                @pl.when(jnp.logical_not(first))
                def _():
                    hid_copy(h, c).wait_send()

            return carry

        summed = lax.dot_general(
            pick[...].reshape(experts * slots, everyone),
            obuf[...].reshape(experts * slots, cols),
            (((0,), (0,)), ((), ())),
            preferred_element_type=jnp.float32,
        )
        for p in range(rows_gx):
            pbuf[p] = summed[p * tokens : (p + 1) * tokens].astype(jnp.bfloat16)

        def back_copy(d):
            peer = lax.rem(row + d, rows_gx)
            return send(pbuf.at[peer], ret.at[d], g_s.at[d], g_r.at[d], "gx", peer)

        for d in range(1, rows_gx):
            back_copy(d).start()
        moe = pbuf[row].astype(jnp.float32)
        lax.fori_loop(0, chunks, sent, 0)
        lax.fori_loop(0, chunks, relayed, 0)
        lax.fori_loop(0, steps, done, 0)
        lax.fori_loop(0, strips, finish, 0)
        for d in range(1, rows_gx):
            h_copy(d, row).wait_send()
        for d in range(1, rows_gx):
            back_copy(d).wait_recv()
            moe = moe + ret[d].astype(jnp.float32)
        out_ref[...] = (h_all[row].astype(jnp.float32) + moe).astype(jnp.bfloat16)
        for d in range(1, rows_gx):
            back_copy(d).wait_send()

    pad = -accepted % 16
    vmem = pl.BlockSpec(memory_space=pltpu.VMEM)
    hbm = pl.BlockSpec(memory_space=pl.ANY)
    dma = pltpu.SemaphoreType.DMA
    stat = pltpu.VMEM((steps, 2 * part, lane), jnp.float32)
    piece = pltpu.VMEM((steps, rows, dim), jnp.bfloat16)
    return pl.pallas_call(
        kernel,
        out_shape=[
            jax.ShapeDtypeStruct((tokens, cols), jnp.bfloat16),
            jax.ShapeDtypeStruct((accepted, 2 * kv_cols), jnp.bfloat16),
        ],
        in_specs=[pl.BlockSpec(memory_space=pltpu.SMEM)] + [vmem] * 9 + [hbm] * 6,
        out_specs=[vmem, vmem],
        scratch_shapes=[
            pltpu.VMEM((tokens, model), jnp.bfloat16),
            pltpu.VMEM((chunks, model, 2 * dim), jnp.bfloat16),
            pltpu.VMEM((own * count, tokens, dim), jnp.bfloat16),
            pltpu.VMEM((kv_heads, span + lane, dim), jnp.bfloat16),
            pltpu.VMEM((kv_heads, span + lane, 2 * dim), jnp.bfloat16),
            pltpu.VMEM(w_o.shape, jnp.bfloat16),
            pltpu.VMEM((1, span), jnp.float32),
            pltpu.VMEM((tokens, lane), jnp.float32),
            pltpu.VMEM((steps, rows, dim), jnp.float32),
            stat,
            piece,
            piece,
            stat,
            piece,
            piece,
            stat,
            stat,
            pltpu.VMEM((heads, tokens, dim), jnp.bfloat16),
            pltpu.VMEM((tokens, cols), jnp.float32),
            pltpu.VMEM((accepted + pad, 2 * kv_cols), jnp.bfloat16),
            dma((chunks,)),
            dma((kv_heads,)),
            dma((kv_heads,)),
            dma,
            dma((count, 2 * chunks)),
            dma((count * chunks,)),
        ]
        + [dma((steps,))] * 10
        + [dma((last,)), dma, dma((rows_gx,)), dma((rows_gx,))]
        + [
            pltpu.VMEM((rows_gx, tokens, cols), jnp.bfloat16),
            pltpu.VMEM((rows_gx, tokens, cols), jnp.bfloat16),
            pltpu.VMEM((experts, slots, everyone), jnp.bfloat16),
            pltpu.VMEM((experts, slots, lane), jnp.float32),
            pltpu.VMEM((8, everyone), jnp.float32),
            pltpu.VMEM((count, 8, everyone), jnp.float32),
            pltpu.VMEM((1, everyone), jnp.float32),
            pltpu.VMEM((2, strips, grain, units), jnp.bfloat16),
            pltpu.VMEM((experts, depth, wide), jnp.bfloat16),
            pltpu.VMEM((experts, units, cols), jnp.bfloat16),
            pltpu.VMEM((2, strips, grain, wide), jnp.bfloat16),
            pltpu.VMEM((2, strips, grain, wide), jnp.bfloat16),
            pltpu.VMEM((experts, slots, cols), jnp.bfloat16),
            pltpu.VMEM((rows_gx, tokens, cols), jnp.bfloat16),
            pltpu.VMEM((rows_gx, tokens, cols), jnp.bfloat16),
            dma((experts,)),
            dma((experts,)),
            dma((count,)),
            dma((count,)),
            dma((2, strips)),
            dma((2, strips)),
            dma((2, strips)),
            dma((2, strips)),
            dma((rows_gx,)),
            dma((rows_gx,)),
        ],
        compiler_params=pltpu.CompilerParams(
            collective_id=cid, has_side_effects=True, vmem_limit_bytes=62 * 1024 * 1024
        ),
        name="layer_line",
    )(
        cache_len, states, attn_gain, q_gain, k_gain, tree_mask,
        accept, ffn_gain, routing, route_weight, w_qkv, cache_k, cache_v, w_o, w_in, w_down,
    )


def rms_scale(values, gain):
    return values * lax.rsqrt(jnp.mean(values * values, -1, keepdims=True) + EPS) * gain


def angles_of(position, dim):
    freqs = jnp.exp(jnp.arange(dim // 2, dtype=jnp.float32) * (-2.0 * THETA_LOG / dim))
    angles = position.astype(jnp.float32)[..., None] * freqs
    cosine = jnp.cos(angles)
    sine = jnp.sin(angles)
    return jnp.concatenate([cosine, cosine], -1), jnp.concatenate([-sine, sine], -1)


def body(
    states,
    attn_gain,
    w_qkv,
    q_gain,
    k_gain,
    cache_k,
    cache_v,
    cache_len,
    tree_mask,
    w_o,
    ffn_gain,
    routing,
    route_weight,
    w_in,
    w_down,
    accept,
):
    tok_rows, model_width = states.shape
    head_dim = q_gain.shape[0]
    kv_cols = cache_k.shape[2]
    heads_all = w_o.shape[0] // head_dim
    cache_span = cache_k.shape[1]
    cols_here = w_o.shape[1]
    col_index = lax.axis_index("gy")
    row_index = lax.axis_index("gx")
    count_gx = lax.axis_size("gx")
    count_gy = lax.axis_size("gy")
    own_heads = w_qkv.shape[1] // head_dim
    kv_heads = kv_cols // head_dim
    on_line = (
        count_gy == 4
        and w_qkv.shape[1] % (2 * head_dim) == 0
        and own_heads >= 2 * kv_heads
        and (own_heads - 2 * kv_heads) % 2 == 0
        and heads_all % (4 * kv_heads) == 0
        and tok_rows % 16 == 0
        and 128 % tok_rows == 0
        and routing.shape[0] % 128 == 0
        and w_in.shape[1] == w_o.shape[1]
        and (3 * routing.shape[0] * routing.shape[1] // (2 * w_in.shape[0] * lax.axis_size("gx"))) % 16 == 0
    )
    if on_line:
        layer_out, accepted_kv = layer_line(
            states,
            attn_gain,
            w_qkv,
            q_gain[None],
            k_gain[None],
            cache_k[0],
            cache_v[0],
            cache_len,
            tree_mask[0],
            w_o,
            accept[0],
            ffn_gain,
            routing.T,
            route_weight.T,
            w_in,
            w_down,
            0,
        )
        return (layer_out, accepted_kv[None])
    normed = rms_scale(states.astype(jnp.float32), attn_gain.astype(jnp.float32)).astype(
        jnp.bfloat16
    )
    qkv_part = jnp.dot(normed, w_qkv, preferred_element_type=jnp.float32).astype(jnp.bfloat16)
    (qkv_blocks,) = exchange([qkv_part], "gy", False, 0)
    qkv_whole = jnp.swapaxes(qkv_blocks, 0, 1).reshape(tok_rows, -1)
    q_cols = heads_all * head_dim
    depth = jnp.sum(tree_mask, -1) - 1
    cosine, sine = angles_of((cache_len[:, None] + depth)[0], head_dim)
    states_here = lax.dynamic_slice_in_dim(states, col_index * cols_here, cols_here, 1)
    gathered, k_rot = attention_block(
        qkv_whole,
        q_gain[None],
        k_gain[None],
        cosine,
        sine,
        cache_k[0],
        cache_v[0],
        cache_len - col_index * cache_span,
        tree_mask[0],
        states_here,
        w_o,
        1,
    )
    kv_new = jnp.concatenate([k_rot, qkv_whole[:, q_cols + kv_cols :]], -1)[None]
    accepted_kv = jnp.einsum(
        "rat,rtc->rac", accept.astype(jnp.bfloat16), kv_new, preferred_element_type=jnp.float32
    ).astype(jnp.bfloat16)
    resid = lax.dynamic_index_in_dim(gathered, row_index, 0, False)
    exp_here = w_in.shape[0]
    expert_count = exp_here * count_gx
    top_k = routing.shape[1]
    most_rows = 3 * tok_rows * top_k // (2 * expert_count)
    hidden_units = w_down.shape[1]
    gain_float = ffn_gain.astype(jnp.float32)
    tokens = routing.shape[0]
    slots = count_gx * most_rows
    own_experts = row_index * exp_here + jnp.arange(exp_here, dtype=jnp.int32)
    matched = routing[:, None, :] == own_experts[None, :, None]
    hits = jnp.any(matched, -1)
    weights = jnp.sum(jnp.where(matched, route_weight[:, None, :], 0.0), -1)
    order = jnp.arange(tok_rows, dtype=jnp.int32)
    earlier = (order[:, None] > order[None, :]).astype(jnp.bfloat16)
    rank = jnp.einsum(
        "tu,bue->bte",
        earlier,
        hits.astype(jnp.bfloat16).reshape(count_gx, tok_rows, exp_here),
        preferred_element_type=jnp.float32,
    ).astype(jnp.int32)
    first_slot = jnp.arange(count_gx, dtype=jnp.int32)[:, None, None] * most_rows
    slot_of = jnp.where(hits, (rank + first_slot).reshape(tokens, exp_here), -1)
    pick = slot_of.T[:, None, :] == jnp.arange(slots, dtype=jnp.int32)[None, :, None]
    pick_matrix = pick.astype(jnp.bfloat16)
    slot_weight = jnp.sum(jnp.where(pick, weights.T[:, None, :], 0.0), -1)
    gathered = gathered.reshape(tokens, cols_here).astype(jnp.float32)
    token_squares = jnp.sum(gathered * gathered, -1)
    slot_squares = jnp.sum(jnp.where(pick, token_squares, 0.0), -1)
    piece = 16
    slot_squares = jnp.pad(slot_squares.reshape(-1, piece), ((0, 0), (0, 128 - piece)))
    scaled = (gathered * gain_float).astype(jnp.bfloat16)
    rows = jnp.einsum(
        "est,td->esd", pick_matrix, scaled, preferred_element_type=jnp.float32
    ).astype(jnp.bfloat16)
    layer_out = expert_layer(
        rows,
        slot_squares,
        w_in,
        w_down,
        slot_weight[..., None],
        pick_matrix.reshape(exp_here * slots, tokens),
        resid,
        model_width,
        4,
    )
    return (layer_out, accepted_kv)


def solution(mesh):
    in_specs = (
        P("gx", None),
        P(),
        P(None, "gy"),
        P(),
        P(),
        P("gx", "gy", None),
        P("gx", "gy", None),
        P("gx"),
        P("gx", None, None),
        P(None, "gy"),
        P("gy"),
        P(),
        P(),
        P("gx", "gy", None),
        P("gx", None, "gy"),
        P("gx", None, None),
    )
    out_specs = (P("gx", "gy"), P("gx", None, None))
    return jax.shard_map(body, mesh=mesh, in_specs=in_specs, out_specs=out_specs, check_vma=False)
```

```python
import math

import jax
import jax.numpy as jnp
from jax import lax
from jax.experimental import pallas as pl
from jax.experimental.pallas import tpu as pltpu
from jax.sharding import PartitionSpec as P

EPS = 1e-06
NEG = -1e30
THETA_LOG = math.log(1000000.0)


MESH = pl.DeviceIdType.MESH


def exchange(arrays, axis, scatter, cid):
    count = lax.axis_size(axis)
    number = len(arrays)

    def kernel(*refs):
        ins, outs = refs[:number], refs[number : 2 * number]
        send, recv, local = refs[2 * number :]
        me = lax.axis_index(axis)
        barrier = pltpu.get_barrier_semaphore()
        for d in range(1, count):
            pl.semaphore_signal(
                barrier, inc=1, device_id={axis: lax.rem(me + d, count)}, device_id_type=MESH
            )
        pl.semaphore_wait(barrier, count - 1)
        copies = []
        for d in range(1, count):
            peer = lax.rem(me + d, count)
            for i in range(number):
                copy = pltpu.make_async_remote_copy(
                    src_ref=ins[i].at[peer] if scatter else ins[i],
                    dst_ref=outs[i].at[me],
                    send_sem=send.at[i, d],
                    recv_sem=recv.at[i, d],
                    device_id={axis: peer},
                    device_id_type=MESH,
                )
                copy.start()
                copies.append(copy)
        own = []
        for i in range(number):
            copy = pltpu.make_async_copy(
                ins[i].at[me] if scatter else ins[i], outs[i].at[me], local.at[i]
            )
            copy.start()
            own.append(copy)
        for copy in own + copies:
            copy.wait()

    outs = [
        jax.ShapeDtypeStruct(x.shape if scatter else (count,) + x.shape, x.dtype) for x in arrays
    ]
    return pl.pallas_call(
        kernel,
        out_shape=outs,
        in_specs=[pl.BlockSpec(memory_space=pltpu.VMEM)] * number,
        out_specs=[pl.BlockSpec(memory_space=pltpu.VMEM)] * number,
        scratch_shapes=[
            pltpu.SemaphoreType.DMA((number, count)),
            pltpu.SemaphoreType.DMA((number, count)),
            pltpu.SemaphoreType.DMA((number,)),
        ],
        compiler_params=pltpu.CompilerParams(collective_id=cid, has_side_effects=True),
        name="exchange_%d" % cid,
    )(*arrays)


def expert_layer(rows, squares, w_in, w_down, slot_weight, pick_back, resid, model_width, cid):
    axis = "gy"
    count = lax.axis_size(axis)
    peers = lax.axis_size("gx")
    experts, slots, depth = rows.shape
    tokens, cols = resid.shape
    wide = w_in.shape[2]
    units = wide // 2
    half = experts // 2
    piece = 16
    sub = slots // piece
    chunks = half * sub
    hop = 2
    far = hop * (count - 1)

    def kernel(
        x_ref, sq_ref, weight_ref, pick_ref, resid_ref, w_hbm, d_hbm, out_ref,
        hid_ref, wbuf, dbuf, part, rbuf, sqbuf, inv_ref, obuf, pbuf, ret,
        wsem, dsem, rs_s, rs_r, h_s, h_r, sq_s, sq_r, g_s, g_r,
    ):
        me = lax.axis_index(axis)
        prev = lax.rem(me + count - 1, count)
        nxt = lax.rem(me + 1, count)
        at_low = me == 0
        at_high = me == count - 1

        def load(e):
            return pltpu.make_async_copy(w_hbm.at[e], wbuf.at[e], wsem.at[e])

        def load_down(e):
            return pltpu.make_async_copy(d_hbm.at[e], dbuf.at[e], dsem.at[e])

        row = lax.axis_index("gx")
        for s in range(half):
            load(half + s).start()
            load(s).start()
        for s in range(half):
            load_down(half + s).start()
            load_down(s).start()
        barrier = pltpu.get_barrier_semaphore()
        for d in range(1, count):
            pl.semaphore_signal(
                barrier, inc=1, device_id={axis: lax.rem(me + d, count)}, device_id_type=MESH
            )
        for d in range(1, peers):
            pl.semaphore_signal(
                barrier, inc=1, device_id={"gx": lax.rem(row + d, peers)}, device_id_type=MESH
            )

        def multiply(h, s):
            e = h * half + s
            load(e).wait()
            value = jnp.dot(x_ref[e], wbuf[e], preferred_element_type=jnp.float32)
            for j in range(sub):
                part[h, s * sub + j] = value[j * piece : (j + 1) * piece].astype(jnp.bfloat16)

        multiply(1, 0)
        multiply(0, 0)
        pl.semaphore_wait(barrier, count + peers - 2)

        def sq_copy(d):
            return pltpu.make_async_remote_copy(
                src_ref=sq_ref,
                dst_ref=sqbuf.at[d],
                send_sem=sq_s.at[d],
                recv_sem=sq_r.at[d],
                device_id={axis: lax.rem(me + d, count)},
                device_id_type=MESH,
            )

        for d in range(1, count):
            sq_copy(d).start()

        def finish_squares():
            total = sq_ref[...]
            for d in range(1, count):
                sq_copy(d).wait()
                total = total + sqbuf[d]
            inv_ref[...] = lax.rsqrt(total / model_width + EPS)

        diagonal = lax.broadcasted_iota(jnp.int32, (piece, 128), 0) == lax.broadcasted_iota(
            jnp.int32, (piece, 128), 1
        )

        def rs_copy(h, c):
            return pltpu.make_async_remote_copy(
                src_ref=part.at[h, c],
                dst_ref=rbuf.at[h, c],
                send_sem=rs_s.at[h, c],
                recv_sem=rs_r.at[h, c],
                device_id={axis: nxt if h else prev},
                device_id_type=MESH,
            )

        def hid_copy(h, c):
            return pltpu.make_async_remote_copy(
                src_ref=hid_ref.at[h, c],
                dst_ref=hid_ref.at[h, c],
                send_sem=h_s.at[h, c],
                recv_sem=h_r.at[h, c],
                device_id={axis: prev if h else nxt},
                device_id_type=MESH,
            )

        def ends(h):
            return (at_low, at_high) if h else (at_high, at_low)

        def reduce_chunk(h, c):
            first, last = ends(h)

            @pl.when(jnp.logical_not(first))
            def _():
                rs_copy(h, c).wait_recv()

            @pl.when(jnp.logical_not(jnp.logical_or(first, last)))
            def _():
                part[h, c] = (
                    part[h, c].astype(jnp.float32) + rbuf[h, c].astype(jnp.float32)
                ).astype(jnp.bfloat16)

            @pl.when(jnp.logical_not(last))
            def _():
                rs_copy(h, c).start()

            @pl.when(last)
            def _():
                row = inv_ref[pl.ds(h * chunks + c, 1), :]
                inverse = jnp.sum(jnp.where(diagonal, row, 0.0), 1, keepdims=True)
                summed = part[h, c].astype(jnp.float32) + rbuf[h, c].astype(jnp.float32)
                gate = summed[:, :units] * inverse
                up = summed[:, units:] * inverse
                hid_ref[h, c] = (gate / (1.0 + jnp.exp(-gate)) * up).astype(jnp.bfloat16)
                hid_copy(h, c).start()

        def return_chunk(h, c):
            first, last = ends(h)

            @pl.when(jnp.logical_not(last))
            def _():
                hid_copy(h, c).wait_recv()

            @pl.when(jnp.logical_not(jnp.logical_or(first, last)))
            def _():
                hid_copy(h, c).start()

        def project(h, s):
            e = h * half + s
            load_down(e).wait()
            value = hid_ref[h, pl.ds(s * sub, sub)].reshape(slots, units)
            value = jnp.dot(value, dbuf[e], preferred_element_type=jnp.float32)
            obuf[e] = (value * weight_ref[e]).astype(jnp.bfloat16)

        def step(t, carry):
            for h, place in ((1, 1), (0, sub // 2 + 1)):

                @pl.when(jnp.logical_and(t < chunks - sub, lax.rem(t, sub) == place))
                def _():
                    multiply(h, lax.div(t, sub) + 1)

            @pl.when(t == far - 1)
            def _():
                finish_squares()

            for h in (1, 0):
                way = hop * (me if h else count - 1 - me)
                c = t - way

                @pl.when(jnp.logical_and(c >= 0, c < chunks))
                def _():
                    reduce_chunk(h, c)

            for h in (1, 0):
                way = hop * (me if h else count - 1 - me)
                b = t - 2 * far + way

                @pl.when(jnp.logical_and(b >= 0, b < chunks))
                def _():
                    return_chunk(h, b)

                    @pl.when(lax.rem(b, sub) == sub - 1)
                    def _():
                        project(h, lax.div(b, sub))

            return carry

        lax.fori_loop(0, chunks + 2 * far, step, 0)

        def finish(c, carry):
            for h in (1, 0):
                first, last = ends(h)

                @pl.when(jnp.logical_not(last))
                def _():
                    rs_copy(h, c).wait_send()

                @pl.when(jnp.logical_not(first))
                def _():
                    hid_copy(h, c).wait_send()

            return carry

        summed = lax.dot_general(
            pick_ref[...],
            obuf[...].reshape(experts * slots, cols),
            (((0,), (0,)), ((), ())),
            preferred_element_type=jnp.float32,
        )
        for p in range(peers):
            pbuf[p] = summed[p * tokens : (p + 1) * tokens].astype(jnp.bfloat16)

        def back_copy(d):
            peer = lax.rem(row + d, peers)
            return pltpu.make_async_remote_copy(
                src_ref=pbuf.at[peer],
                dst_ref=ret.at[d],
                send_sem=g_s.at[d],
                recv_sem=g_r.at[d],
                device_id={"gx": peer},
                device_id_type=MESH,
            )

        for d in range(1, peers):
            back_copy(d).start()
        moe = pbuf[row].astype(jnp.float32)
        lax.fori_loop(0, chunks, finish, 0)
        for d in range(1, peers):
            back_copy(d).wait_recv()
            moe = moe + ret[d].astype(jnp.float32)
        out_ref[...] = (resid_ref[...].astype(jnp.float32) + moe).astype(jnp.bfloat16)
        for d in range(1, peers):
            back_copy(d).wait_send()

    vmem = pl.BlockSpec(memory_space=pltpu.VMEM)
    hbm = pl.BlockSpec(memory_space=pl.ANY)
    dma = pltpu.SemaphoreType.DMA
    return pl.pallas_call(
        kernel,
        out_shape=jax.ShapeDtypeStruct((tokens, cols), jnp.bfloat16),
        in_specs=[vmem] * 5 + [hbm, hbm],
        out_specs=vmem,
        scratch_shapes=[
            pltpu.VMEM((2, chunks, piece, units), jnp.bfloat16),
            pltpu.VMEM((experts, depth, wide), jnp.bfloat16),
            pltpu.VMEM((experts, units, cols), jnp.bfloat16),
            pltpu.VMEM((2, chunks, piece, wide), jnp.bfloat16),
            pltpu.VMEM((2, chunks, piece, wide), jnp.bfloat16),
            pltpu.VMEM((count, 2 * chunks, 128), jnp.float32),
            pltpu.VMEM((2 * chunks, 128), jnp.float32),
            pltpu.VMEM((experts, slots, cols), jnp.bfloat16),
            pltpu.VMEM((peers, tokens, cols), jnp.bfloat16),
            pltpu.VMEM((peers, tokens, cols), jnp.bfloat16),
            dma((experts,)),
            dma((experts,)),
            dma((2, chunks)),
            dma((2, chunks)),
            dma((2, chunks)),
            dma((2, chunks)),
            dma((count,)),
            dma((count,)),
            dma((peers,)),
            dma((peers,)),
        ],
        compiler_params=pltpu.CompilerParams(
            collective_id=cid, has_side_effects=True, vmem_limit_bytes=52 * 1024 * 1024
        ),
        name="expert_layer",
    )(rows, squares, slot_weight, pick_back, resid, w_in, w_down)


def attention_block(
    qkv, q_gain, k_gain, cosine, sine, cache_k, cache_v, limit, tree_mask, states_here, w_o, cid
):
    blocks = lax.axis_size("gy")
    rows_gx = lax.axis_size("gx")
    tokens = qkv.shape[0]
    span, kv_cols = cache_k.shape
    dim = q_gain.shape[1]
    kv_heads = kv_cols // dim
    heads = qkv.shape[1] // dim - 2 * kv_heads
    group = heads // kv_heads
    per_block = heads // blocks
    blocks_here = blocks // kv_heads
    width = per_block * dim
    cols = w_o.shape[1]
    scale = dim ** (-0.5)

    def kernel(
        limit_ref, q_ref, qg_ref, kg_ref, cos_ref, sin_ref, k_ref, v_ref, mask_ref, st_ref, wo_hbm,
        h_ref, rot_ref,
        acc_out, stat_out, acc_in, stat_in, attn, wo,
        wo_sem, a_s, a_r, s_s, s_r, t_s, t_r, h_s, h_r,
    ):
        me = lax.axis_index("gy")
        row = lax.axis_index("gx")
        load = pltpu.make_async_copy(wo_hbm, wo, wo_sem)
        load.start()
        barrier = pltpu.get_barrier_semaphore()
        for axis, here, count in (("gy", me, blocks), ("gx", row, rows_gx)):
            for d in range(1, count):
                pl.semaphore_signal(
                    barrier, inc=1, device_id={axis: lax.rem(here + d, count)}, device_id_type=MESH
                )
        pl.semaphore_wait(barrier, blocks + rows_gx - 2)

        def send(src, dst, send_sem, recv_sem, axis, peer):
            return pltpu.make_async_remote_copy(
                src_ref=src,
                dst_ref=dst,
                send_sem=send_sem,
                recv_sem=recv_sem,
                device_id={axis: peer},
                device_id_type=MESH,
            )

        def part_copies(block, source):
            return (
                send(acc_out.at[block], acc_in.at[source], a_s.at[block], a_r.at[source], "gy", block),
                send(stat_out.at[block], stat_in.at[source], s_s.at[block], s_r.at[source], "gy", block),
            )

        cos = cos_ref[...]
        sin = sin_ref[...]

        def turn(value, gain):
            value = value.astype(jnp.float32)
            value = value * lax.rsqrt(jnp.mean(value * value, -1, keepdims=True) + EPS) * gain
            return (value * cos + pltpu.roll(value, dim // 2, 1) * sin).astype(jnp.bfloat16)

        q_gain_row = qg_ref[...].astype(jnp.float32)
        k_gain_row = kg_ref[...].astype(jnp.float32)
        contract = (((1,), (1,)), ((), ()))
        diagonal = lax.broadcasted_iota(jnp.int32, (tokens, 128), 0) == lax.broadcasted_iota(
            jnp.int32, (tokens, 128), 1
        )

        def one_head(i, carry):
            g = lax.rem(lax.div(me, blocks_here) + 1 + i, kv_heads)

            def lanes(first, size):
                return pl.ds(pl.multiple_of(first, 128), size)

            query = jnp.concatenate(
                [
                    turn(q_ref[:, lanes((g * group + j) * dim, dim)], q_gain_row)
                    for j in range(group)
                ],
                0,
            )
            keys = turn(q_ref[:, lanes((heads + g) * dim, dim)], k_gain_row)
            values = q_ref[:, lanes((heads + kv_heads + g) * dim, dim)]
            rot_ref[:, lanes(g * dim, dim)] = keys
            tree = (
                lax.dot_general(query, keys, contract, preferred_element_type=jnp.float32) * scale
            )
            mask = jnp.concatenate([mask_ref[...]] * group, 0)
            tree_ok = jnp.logical_and(mask == 1, me == 0)
            tree = jnp.where(tree_ok, tree, NEG)
            score = (
                lax.dot_general(
                    query,
                    k_ref[:, lanes(g * dim, dim)],
                    contract,
                    preferred_element_type=jnp.float32,
                )
                * scale
            )
            valid = lax.broadcasted_iota(jnp.int32, score.shape, 1) < limit_ref[0]
            score = jnp.where(valid, score, NEG)
            top = jnp.maximum(jnp.max(score, 1, keepdims=True), jnp.max(tree, 1, keepdims=True))
            prob = jnp.where(valid, jnp.exp(score - top), 0.0).astype(jnp.bfloat16)
            prob_tree = jnp.where(tree_ok, jnp.exp(tree - top), 0.0).astype(jnp.bfloat16)
            total = jnp.sum(prob.astype(jnp.float32), 1, keepdims=True) + jnp.sum(
                prob_tree.astype(jnp.float32), 1, keepdims=True
            )
            acc = jnp.dot(prob, v_ref[:, lanes(g * dim, dim)], preferred_element_type=jnp.float32)
            acc = acc + jnp.dot(prob_tree, values, preferred_element_type=jnp.float32)
            acc = acc.astype(jnp.bfloat16)
            for b in range(blocks_here):
                block = g * blocks_here + b
                for place in range(per_block):
                    j = b * per_block + place
                    rows = slice(j * tokens, (j + 1) * tokens)
                    acc_out[block, :, place * dim : (place + 1) * dim] = acc[rows]
                    for k, column in enumerate((top, total)):
                        stat_out[block, k * per_block + place : k * per_block + place + 1, :] = (
                            jnp.sum(jnp.where(diagonal, column[rows], 0.0), 0, keepdims=True)
                        )

                @pl.when(block != me)
                def _():
                    for copy in part_copies(block, me):
                        copy.start()

            return carry

        lax.fori_loop(0, kv_heads, one_head, 0)

        acc_in[me] = acc_out[me]
        stat_in[me] = stat_out[me]
        for d in range(1, blocks):
            source = lax.rem(me + d, blocks)
            for copy in part_copies(source, source):
                copy.wait_recv()
        tops = [stat_in[j, :per_block, :] for j in range(blocks)]
        best = tops[0]
        for j in range(1, blocks):
            best = jnp.maximum(best, tops[j])
        factors = [jnp.exp(tops[j] - best) for j in range(blocks)]
        denom = stat_in[0, per_block:, :] * factors[0]
        for j in range(1, blocks):
            denom = denom + stat_in[j, per_block:, :] * factors[j]
        for place in range(per_block):
            joined = jnp.zeros((tokens, dim), jnp.float32)
            for j in range(blocks):
                line = (factors[j] / denom)[place : place + 1, :]
                column = jnp.sum(jnp.where(diagonal, line, 0.0), 1, keepdims=True)
                joined = joined + column * acc_in[
                    j, :, place * dim : (place + 1) * dim
                ].astype(jnp.float32)
            attn[me, :, place * dim : (place + 1) * dim] = joined.astype(jnp.bfloat16)

        def attn_copy(d, source):
            return send(
                attn.at[source], attn.at[source], t_s.at[d], t_r.at[d], "gy", lax.rem(me + d, blocks)
            )

        for d in range(1, blocks):
            attn_copy(d, me).start()
        load.wait()

        def project(source):
            return jnp.dot(
                attn[source],
                wo[pl.ds(pl.multiple_of(source * width, width), width), :],
                preferred_element_type=jnp.float32,
            )

        total = st_ref[...].astype(jnp.float32) + project(me)
        for d in range(1, blocks):
            source = lax.rem(me + blocks - d, blocks)
            attn_copy(d, source).wait_recv()
            total = total + project(source)
        h_ref[row] = total.astype(jnp.bfloat16)

        def h_copy(d, source):
            return send(
                h_ref.at[source], h_ref.at[source], h_s.at[d], h_r.at[d], "gx",
                lax.rem(row + d, rows_gx),
            )

        for d in range(1, rows_gx):
            h_copy(d, row).start()
        for d in range(1, blocks):
            block = lax.rem(me + d, blocks)
            for copy in part_copies(block, me):
                copy.wait_send()
            attn_copy(d, me).wait_send()
        for d in range(1, rows_gx):
            h_copy(d, lax.rem(row + rows_gx - d, rows_gx)).wait_recv()
            h_copy(d, row).wait_send()

    vmem = pl.BlockSpec(memory_space=pltpu.VMEM)
    dma = pltpu.SemaphoreType.DMA
    return pl.pallas_call(
        kernel,
        out_shape=[
            jax.ShapeDtypeStruct((rows_gx, tokens, cols), jnp.bfloat16),
            jax.ShapeDtypeStruct((tokens, kv_cols), jnp.bfloat16),
        ],
        in_specs=[pl.BlockSpec(memory_space=pltpu.SMEM)]
        + [vmem] * 9
        + [pl.BlockSpec(memory_space=pl.ANY)],
        out_specs=[vmem, vmem],
        scratch_shapes=[
            pltpu.VMEM((blocks, tokens, width), jnp.bfloat16),
            pltpu.VMEM((blocks, 2 * per_block, 128), jnp.float32),
            pltpu.VMEM((blocks, tokens, width), jnp.bfloat16),
            pltpu.VMEM((blocks, 2 * per_block, 128), jnp.float32),
            pltpu.VMEM((blocks, tokens, width), jnp.bfloat16),
            pltpu.VMEM(w_o.shape, jnp.bfloat16),
            dma,
            dma((blocks,)),
            dma((blocks,)),
            dma((blocks,)),
            dma((blocks,)),
            dma((blocks,)),
            dma((blocks,)),
            dma((rows_gx,)),
            dma((rows_gx,)),
        ],
        compiler_params=pltpu.CompilerParams(
            collective_id=cid, has_side_effects=True, vmem_limit_bytes=48 * 1024 * 1024
        ),
        name="attention_block",
    )(
        limit, qkv, q_gain, k_gain, cosine, sine, cache_k, cache_v, tree_mask, states_here, w_o
    )


def layer_line(
    states, attn_gain, w_qkv, q_gain, k_gain, cache_k, cache_v, cache_len, tree_mask, w_o, accept,
    ffn_gain, routing, route_weight, w_in, w_down, cid
):
    count = lax.axis_size("gy")
    rows_gx = lax.axis_size("gx")
    tokens, model = states.shape
    span, kv_cols = cache_k.shape
    dim = q_gain.shape[1]
    kv_heads = kv_cols // dim
    own = w_qkv.shape[1] // dim
    heads = own * count - 2 * kv_heads
    group = heads // kv_heads
    cols = w_o.shape[1]
    chunks = own // 2
    part = group // 2
    steps = heads // part
    first_relay = 2
    lag = 3
    rows = part * tokens
    lane = 128
    accepted = accept.shape[0]
    last = count - 1
    factor = dim ** (-0.5) / math.log(2.0)
    top_k, everyone = routing.shape
    experts, depth, wide = w_in.shape
    units = wide // 2
    most_rows = 3 * tokens * top_k // (2 * experts * rows_gx)
    slots = rows_gx * most_rows
    split = experts // 2
    grain = 16
    sub = slots // grain
    strips = split * sub
    turn_slots = slots // 2
    turn_sub = sub // 2
    turn_strips = strips // 2
    hop = 3
    far = hop * last
    straight = 4
    chained = strips - straight

    def kernel(
        len_ref, st_ref, ag_ref, qg_ref, kg_ref, mask_ref, acc_ref, fg_ref, rt_ref, rw_ref,
        wq_hbm, k_hbm, v_hbm, wo_hbm, w_hbm, d_hbm,
        out_ref, akv_ref,
        normed, wq, qall, kext, vext, wo, bias, tree_bias,
        own_acc, own_stat, end_out, end_in, stat_in, mid_out, mid_in, mstat_out, mstat_in,
        attn, total, akv,
        wq_sem, k_sem, v_sem, wo_sem, q_s, q_r, e_s, e_r, es_s, es_r, m_s, m_r, ms_s, ms_r,
        f_s, f_r, a_s, a_r, h_s, h_r,
        h_all, scaled, pick, wcol, sq_out, sq_in, inv_row, hid, wbuf, dbuf, part_sum, rbuf, obuf, pbuf, ret,
        w_sem, d_sem, sq_s, sq_r, rs_s, rs_r, hid_s, hid_r, st_s, g_s, g_r,
    ):
        me = lax.axis_index("gy")
        row = lax.axis_index("gx")
        is_last = me == last
        is_end = jnp.logical_or(me == 0, is_last)
        is_mid = jnp.logical_not(is_end)
        low = me < 2
        mid_of = jnp.where(low, 1, 2)
        end_of = jnp.where(low, 0, last)
        other_mid = 3 - mid_of

        def send(src, dst, send_sem, recv_sem, axis, peer):
            return pltpu.make_async_remote_copy(
                src_ref=src,
                dst_ref=dst,
                send_sem=send_sem,
                recv_sem=recv_sem,
                device_id={axis: peer},
                device_id_type=MESH,
            )

        def chunk_at(i):
            return jnp.where(is_last, i, chunks - 1 - i)

        def load_w(c):
            return pltpu.make_async_copy(
                wq_hbm.at[:, pl.ds(pl.multiple_of(c * 2 * dim, 2 * dim), 2 * dim)],
                wq.at[c],
                wq_sem.at[c],
            )

        def load_k(g):
            return pltpu.make_async_copy(
                k_hbm.at[:, g * dim : (g + 1) * dim], kext.at[g, 0:span, :], k_sem.at[g]
            )

        def load_v(g):
            return pltpu.make_async_copy(
                v_hbm.at[:, g * dim : (g + 1) * dim], vext.at[g, 0:span, 0:dim], v_sem.at[g]
            )

        load_o = pltpu.make_async_copy(wo_hbm, wo, wo_sem)
        for i in range(chunks):
            load_w(chunk_at(i)).start()
        for g in range(kv_heads - 1, -1, -1):
            load_k(g).start()
            load_v(g).start()
        load_o.start()
        barrier = pltpu.get_barrier_semaphore()
        for axis, here, number in (("gy", me, count), ("gx", row, rows_gx)):
            for d in range(1, number):
                pl.semaphore_signal(
                    barrier, inc=1, device_id={axis: lax.rem(here + d, number)}, device_id_type=MESH
                )

        value = st_ref[...].astype(jnp.float32)
        value = value * lax.rsqrt(jnp.mean(value * value, -1, keepdims=True) + EPS)
        normed[...] = (value * ag_ref[...].reshape(1, model).astype(jnp.float32)).astype(jnp.bfloat16)
        mask = mask_ref[...]
        position = len_ref[0] + jnp.sum(mask, -1, keepdims=True) - 1
        place = lax.broadcasted_iota(jnp.int32, (tokens, dim), 1)
        half = lax.rem(place, dim // 2).astype(jnp.float32)
        angle = position.astype(jnp.float32) * jnp.exp(half * (-2.0 * THETA_LOG / dim))
        cos = jnp.cos(angle)
        sin = jnp.sin(angle)
        sin = jnp.where(place < dim // 2, -sin, sin)
        limit = len_ref[0] - me * span
        spot = lax.broadcasted_iota(jnp.int32, (1, span), 1)
        bias[...] = jnp.where(spot < limit, 0.0, NEG)
        allowed = jnp.logical_and(mask == 1, is_last)
        tree_bias[...] = jnp.full((tokens, lane), NEG, jnp.float32)
        tree_bias[:, 0:tokens] = jnp.where(allowed, 0.0, NEG)
        for g in range(kv_heads):
            kext[g, span : span + lane, :] = jnp.zeros((lane, dim), jnp.bfloat16)
            vext[g, span : span + lane, 0:dim] = jnp.zeros((lane, dim), jnp.bfloat16)
            vext[g, :, dim : 2 * dim] = jnp.ones((span + lane, dim), jnp.bfloat16)
        total[...] = st_ref[:, pl.ds(pl.multiple_of(me * cols, 128), cols)].astype(jnp.float32)
        q_gain_row = qg_ref[...].astype(jnp.float32)
        k_gain_row = kg_ref[...].astype(jnp.float32)

        def q_copy(k, c, peer):
            block = qall.at[pl.ds(2 * k, 2)]
            return send(block, block, q_s.at[peer, c], q_r.at[k], "gy", peer)

        relay = me == last - 1

        def direct(k, peer):
            far_pair = jnp.logical_and(me == 0, peer == last)
            there = jnp.logical_and(me != peer, jnp.logical_not(far_pair))
            return jnp.logical_and(there, 2 * k < heads)

        def relay_copy(k):
            return q_copy(k, chunks + k, last)

        pl.semaphore_wait(barrier, count + rows_gx - 2)

        def project_in(i, carry):
            c = chunk_at(i)
            load_w(c).wait()
            value = jnp.dot(normed[...], wq[c], preferred_element_type=jnp.float32)
            value = value.astype(jnp.bfloat16)
            k = me * chunks + c
            for j in range(2):
                head = 2 * k + j
                raw = value[:, j * dim : (j + 1) * dim]
                turned = raw.astype(jnp.float32)
                gain = jnp.where(head < heads, q_gain_row, k_gain_row)
                scale = lax.rsqrt(jnp.mean(turned * turned, -1, keepdims=True) + EPS)
                turned = turned * scale * gain
                turned = (turned * cos + pltpu.roll(turned, dim // 2, 1) * sin).astype(jnp.bfloat16)
                qall[head] = jnp.where(head < heads + kv_heads, turned, raw)
            for peer in range(count - 1, -1, -1):

                @pl.when(direct(k, peer))
                def _():
                    q_copy(k, c, peer).start()

            return carry

        lax.fori_loop(0, chunks, project_in, 0)

        def load_in(e):
            return pltpu.make_async_copy(w_hbm.at[e], wbuf.at[e], w_sem.at[e])

        def load_down(e):
            return pltpu.make_async_copy(d_hbm.at[e], dbuf.at[e], d_sem.at[e])

        for e in range(split):
            load_in(split + e).start()
            load_in(e).start()
        for e in range(split):
            load_down(split + e).start()
            load_down(e).start()

        names = rt_ref[...]
        shares = rw_ref[...]
        hits, weights = [], []
        for e in range(experts):
            matched = names == row * experts + e
            hits.append(jnp.sum(jnp.where(matched, 1.0, 0.0), 0, keepdims=True))
            weights.append(jnp.sum(jnp.where(matched, shares, 0.0), 0, keepdims=True))
        hit = jnp.concatenate(hits, 0)
        before = lax.broadcasted_iota(jnp.int32, (lane, lane), 0)
        after = lax.broadcasted_iota(jnp.int32, (lane, lane), 1)
        same = lax.div(before, tokens) == lax.div(after, tokens)
        earlier = jnp.where(jnp.logical_and(before < after, same), 1.0, 0.0).astype(jnp.bfloat16)
        rank = jnp.concatenate(
            [
                jnp.dot(
                    hit[:, i : i + lane].astype(jnp.bfloat16),
                    earlier,
                    preferred_element_type=jnp.float32,
                )
                for i in range(0, everyone, lane)
            ],
            1,
        )
        block_no = lax.div(lax.broadcasted_iota(jnp.int32, (experts, everyone), 1), tokens)
        first_slot = (lax.div(block_no, 2) * most_rows).astype(jnp.float32)
        slot_no = lax.broadcasted_iota(jnp.int32, (turn_slots, everyone), 0).astype(jnp.float32)
        for turn in range(2):
            here = jnp.logical_and(hit > 0.5, lax.rem(block_no, 2) == turn)
            slot_of = jnp.where(here, rank + first_slot, -1.0)
            for e in range(experts):
                chosen = slot_no == slot_of[e : e + 1]
                pick[turn, e] = jnp.where(chosen, 1.0, 0.0).astype(jnp.bfloat16)
                column = jnp.sum(jnp.where(chosen, weights[e], 0.0), 1, keepdims=True)
                wcol[turn, e] = jnp.broadcast_to(column, (turn_slots, lane))

        def akv_copy(d, peer):
            return send(akv, akv, a_s.at[d], a_r, "gy", peer)

        @pl.when(is_last)
        def _():
            pick = acc_ref[...].astype(jnp.bfloat16)
            akv[...] = jnp.zeros(akv.shape, jnp.bfloat16)
            for i in range(2 * kv_heads):
                akv[0:accepted, i * dim : (i + 1) * dim] = jnp.dot(
                    pick, qall[heads + i], preferred_element_type=jnp.float32
                ).astype(jnp.bfloat16)
            for d in range(last):
                akv_copy(d, d).start()
            for g in range(kv_heads):
                kext[g, span : span + tokens, :] = qall[heads + g]
                vext[g, span : span + tokens, 0:dim] = qall[heads + kv_heads + g]

        diagonal = lax.broadcasted_iota(jnp.int32, (tokens, lane), 0) == lax.broadcasted_iota(
            jnp.int32, (tokens, lane), 1
        )

        def as_row(column):
            return jnp.sum(jnp.where(diagonal, column, 0.0), 0, keepdims=True)

        def as_column(line):
            return jnp.sum(jnp.where(diagonal, line, 0.0), 1, keepdims=True)

        contract = (((1,), (1,)), ((), ()))

        def end_copy(s):
            return (
                send(end_out.at[s], end_in.at[s], e_s.at[s], e_r.at[s], "gy", mid_of),
                send(own_stat.at[s], stat_in.at[s], es_s.at[s], es_r.at[s], "gy", mid_of),
            )

        def mid_copy(s):
            return (
                send(mid_out.at[s], mid_in.at[s], m_s.at[s], m_r.at[s], "gy", other_mid),
                send(mstat_out.at[s], mstat_in.at[s], ms_s.at[s], ms_r.at[s], "gy", other_mid),
            )

        def block_of(s):
            return steps - 1 - s

        def final_copy(s):
            place = attn.at[pl.ds(block_of(s) * part, part)]
            return send(place, place, f_s.at[s], f_r.at[s], "gy", end_of)

        def attend(s):
            b = block_of(s)
            for n in range(part // 2):
                k = b * (part // 2) + n
                source = lax.div(k, chunks)
                relayed = jnp.logical_and(relay, source == 0)

                @pl.when(jnp.logical_and(source != me, jnp.logical_not(relayed)))
                def _():
                    q_copy(k, 0, source).wait_recv()

            g = lax.div(b * part, group)
            query = qall[pl.ds(b * part, part)].reshape(rows, dim)
            score = lax.dot_general(query, kext[g], contract, preferred_element_type=jnp.float32)
            cached = score[:, :span] + bias[...]
            tree = score[:, span:] + jnp.concatenate([tree_bias[...]] * part, 0)
            top = jnp.maximum(jnp.max(cached, 1, keepdims=True), jnp.max(tree, 1, keepdims=True))
            top = jnp.maximum(top, 0.5 * NEG)
            prob = jnp.concatenate(
                [
                    jnp.exp2((cached - top) * factor).astype(jnp.bfloat16),
                    jnp.exp2((tree - top) * factor).astype(jnp.bfloat16),
                ],
                1,
            )
            out = jnp.dot(prob, vext[g], preferred_element_type=jnp.float32)
            for j in range(part):
                here = slice(j * tokens, (j + 1) * tokens)
                own_stat[s, j : j + 1, :] = as_row(top[here])
                own_stat[s, part + j : part + j + 1, :] = as_row(out[here, dim:])

            @pl.when(is_end)
            def _():
                end_out[s] = out[:, :dim].astype(jnp.bfloat16)
                for copy in end_copy(s):
                    copy.start()

            @pl.when(is_mid)
            def _():
                own_acc[s] = out[:, :dim]

        def join(s):
            for copy in end_copy(s):
                copy.wait_recv()
            a, b = own_stat[s, :part, :], stat_in[s, :part, :]
            top = jnp.maximum(a, b)
            fa, fb = jnp.exp2((a - top) * factor), jnp.exp2((b - top) * factor)
            mstat_out[s, :part, :] = top
            mstat_out[s, part:, :] = own_stat[s, part:, :] * fa + stat_in[s, part:, :] * fb
            for j in range(part):
                here = slice(j * tokens, (j + 1) * tokens)
                value = own_acc[s, here, :] * as_column(fa[j : j + 1])
                value = value + end_in[s, here, :].astype(jnp.float32) * as_column(fb[j : j + 1])
                own_acc[s, here, :] = value
                mid_out[s, here, :] = value.astype(jnp.bfloat16)
            for copy in mid_copy(s):
                copy.start()

        def project_out(s):
            b = block_of(s)
            value = jnp.concatenate([attn[b * part + j] for j in range(part)], 1)
            weight = wo[pl.ds(pl.multiple_of(b * part * dim, part * dim), part * dim), :]
            total[...] += jnp.dot(value, weight, preferred_element_type=jnp.float32)

        def settle(s):
            for copy in mid_copy(s):
                copy.wait_recv()
            a, b = mstat_out[s, :part, :], mstat_in[s, :part, :]
            top = jnp.maximum(a, b)
            fa, fb = jnp.exp2((a - top) * factor), jnp.exp2((b - top) * factor)
            denom = mstat_out[s, part:, :] * fa + mstat_in[s, part:, :] * fb
            fa, fb = fa / denom, fb / denom
            for j in range(part):
                here = slice(j * tokens, (j + 1) * tokens)
                value = own_acc[s, here, :] * as_column(fa[j : j + 1])
                value = value + mid_in[s, here, :].astype(jnp.float32) * as_column(fb[j : j + 1])
                attn[block_of(s) * part + j] = value.astype(jnp.bfloat16)
            final_copy(s).start()
            project_out(s)

        for g in range(kv_heads):
            load_k(g).wait()
            load_v(g).wait()

        def step(t, carry):
            @pl.when(t < steps)
            def _():
                attend(t)

            k = chunks + first_relay - 1 - t

            @pl.when(jnp.logical_and(relay, jnp.logical_and(k >= 0, k < chunks)))
            def _():
                q_copy(k, 0, 0).wait_recv()
                relay_copy(k).start()

            @pl.when(t == 2)
            def _():
                load_o.wait()

            @pl.when(jnp.logical_and(is_mid, jnp.logical_and(t >= lag, t < steps + lag)))
            def _():
                join(t - lag)

            @pl.when(jnp.logical_and(is_mid, jnp.logical_and(t >= 2 * lag, t < steps + 2 * lag)))
            def _():
                settle(t - 2 * lag)

            @pl.when(jnp.logical_and(is_end, t >= 3 * lag))
            def _():
                final_copy(t - 3 * lag).wait_recv()
                project_out(t - 3 * lag)

            return carry

        lax.fori_loop(0, steps + 3 * lag, step, 0)
        h_all[row] = total[...].astype(jnp.bfloat16)

        def h_copy(d, source):
            return send(
                h_all.at[source], h_all.at[source], h_s.at[d], h_r.at[d], "gx",
                lax.rem(row + d, rows_gx),
            )

        for d in range(1, rows_gx):
            h_copy(d, row).start()

        @pl.when(is_last)
        def _():
            for d in range(last):
                akv_copy(d, d).wait_send()

        @pl.when(jnp.logical_not(is_last))
        def _():
            akv_copy(0, last).wait_recv()

        akv_ref[...] = akv[0:accepted, :]

        def sent(c, carry):
            k = me * chunks + c
            for peer in range(count):

                @pl.when(direct(k, peer))
                def _():
                    q_copy(k, c, peer).wait_send()

            return carry

        def relayed(k, carry):
            @pl.when(relay)
            def _():
                relay_copy(k).wait_send()

            return carry

        def done(s, carry):
            @pl.when(is_end)
            def _():
                for copy in end_copy(s):
                    copy.wait_send()

            @pl.when(is_mid)
            def _():
                for copy in mid_copy(s):
                    copy.wait_send()
                final_copy(s).wait_send()

            return carry

        gain = fg_ref[...].reshape(1, cols).astype(jnp.float32)
        for d in range(rows_gx):
            source = lax.rem(row + rows_gx - d, rows_gx)
            if d:
                h_copy(d, source).wait_recv()
            value = h_all[source].astype(jnp.float32)
            scaled[source] = (value * gain).astype(jnp.bfloat16)
        square_of = lax.broadcasted_iota(jnp.int32, (lane, lane), 0) == lax.broadcasted_iota(
            jnp.int32, (lane, lane), 1
        )

        def multiply(h, s):
            e = h * split + s
            load_in(e).wait()
            value = jnp.dot(
                jnp.concatenate([pick[0, e], pick[1, e]], 0),
                scaled[...].reshape(everyone, cols),
                preferred_element_type=jnp.float32,
            ).astype(jnp.bfloat16)
            value = jnp.dot(value, wbuf[e], preferred_element_type=jnp.float32)
            for j in range(sub):
                c = j // turn_sub * turn_strips + s * turn_sub + j % turn_sub
                part_sum[h, c] = value[j * grain : (j + 1) * grain].astype(jnp.bfloat16)

        prev = lax.rem(me + count - 1, count)
        nxt = lax.rem(me + 1, count)
        at_low = me == 0
        at_high = is_last

        def rs_copy(h, c):
            return send(
                part_sum.at[h, c], rbuf.at[h, c], rs_s.at[h, c], rs_r.at[h, c], "gy",
                jnp.where(h == 1, nxt, prev),
            )

        first_h = jnp.where(low, 1, 0)
        multiply(first_h, 0)

        @pl.when(is_end)
        def _():
            for c in range(turn_sub):
                rs_copy(first_h, c).start()

        multiply(1 - first_h, 0)
        sq_out[...] = jnp.zeros(sq_out.shape, jnp.float32)
        for i in range(everyone // lane):
            value = h_all[pl.ds(i * (lane // tokens), lane // tokens)].reshape(lane, cols)
            value = value.astype(jnp.float32)
            column = jnp.sum(value * value, 1, keepdims=True)
            line = jnp.sum(jnp.where(square_of, column, 0.0), 0, keepdims=True)
            sq_out[0:1, i * lane : (i + 1) * lane] = line

        def sq_copy(d):
            return send(
                sq_out, sq_in.at[d], sq_s.at[d], sq_r.at[d], "gy", lax.rem(me + d, count)
            )

        for d in range(1, count):
            sq_copy(d).start()

        def finish_squares():
            whole = sq_out[0:1, :]
            for d in range(1, count):
                sq_copy(d).wait()
                whole = whole + sq_in[d, 0:1, :]
            inv_row[...] = lax.rsqrt(whole / model + EPS)

        def hid_copy(h, c):
            return send(
                hid.at[h, c], hid.at[h, c], hid_s.at[h, c], hid_r.at[h, c], "gy",
                prev if h else nxt,
            )

        def straight_copy(h, c, d):
            peer = lax.rem(me + (count - d if h else d), count)
            return send(
                hid.at[h, c], hid.at[h, c], st_s.at[h, c - chained, d], hid_r.at[h, c], "gy", peer
            )

        def ends(h):
            return (at_low, at_high) if h else (at_high, at_low)

        def reduce_strip(h, c):
            first, final = ends(h)

            @pl.when(jnp.logical_not(first))
            def _():
                rs_copy(h, c).wait_recv()

            @pl.when(jnp.logical_not(jnp.logical_or(first, final)))
            def _():
                part_sum[h, c] = (
                    part_sum[h, c].astype(jnp.float32) + rbuf[h, c].astype(jnp.float32)
                ).astype(jnp.bfloat16)

            begun = jnp.logical_and(first, c < turn_sub)

            @pl.when(jnp.logical_not(jnp.logical_or(final, begun)))
            def _():
                rs_copy(h, c).start()

            @pl.when(final)
            def _():
                turn = lax.div(c, turn_strips)
                e = h * split + lax.div(lax.rem(c, turn_strips), turn_sub)
                at = pl.multiple_of(lax.rem(c, turn_sub) * grain, grain)
                chosen = pick[turn, e, pl.ds(at, grain), :].astype(jnp.float32)
                inverse = jnp.sum(chosen * inv_row[...], 1, keepdims=True)
                summed = part_sum[h, c].astype(jnp.float32) + rbuf[h, c].astype(jnp.float32)
                gate = summed[:, :units] * inverse
                up = summed[:, units:] * inverse
                hid[h, c] = (gate / (1.0 + jnp.exp(-gate)) * up).astype(jnp.bfloat16)

                @pl.when(c < chained)
                def _():
                    hid_copy(h, c).start()

                @pl.when(c >= chained)
                def _():
                    for d in range(last, 0, -1):
                        straight_copy(h, c, d).start()

        def return_strip(h, c):
            first, final = ends(h)

            @pl.when(jnp.logical_not(final))
            def _():
                hid_copy(h, c).wait_recv()

            passed = jnp.logical_not(jnp.logical_or(first, final))

            @pl.when(jnp.logical_and(passed, c < chained))
            def _():
                hid_copy(h, c).start()

        def project_down(h, b):
            turn = lax.div(b, turn_strips)
            e = h * split + lax.div(lax.rem(b, turn_strips), turn_sub)

            @pl.when(turn == 0)
            def _():
                load_down(e).wait()

            value = hid[h, pl.ds(b + 1 - turn_sub, turn_sub)].reshape(turn_slots, units)
            value = jnp.dot(value, dbuf[e], preferred_element_type=jnp.float32)
            obuf[turn, e] = (value * wcol[turn, e, :, 0:1]).astype(jnp.bfloat16)

        def back_copy(d):
            peer = lax.rem(row + d, rows_gx)
            return send(pbuf.at[peer], ret.at[d], g_s.at[d], g_r.at[d], "gx", peer)

        def send_back(turn):
            summed = lax.dot_general(
                pick[turn].reshape(experts * turn_slots, everyone),
                obuf[turn].reshape(experts * turn_slots, cols),
                (((0,), (0,)), ((), ())),
                preferred_element_type=jnp.float32,
            )
            for p in range(turn, rows_gx, 2):
                pbuf[p] = summed[p * tokens : (p + 1) * tokens].astype(jnp.bfloat16)
            for d in range(1, rows_gx):

                @pl.when(lax.rem(row + d, 2) == turn)
                def _():
                    back_copy(d).start()

        home = turn_strips - 1 + 2 * far - hop * jnp.minimum(me, last - me)

        def moe_step(t, carry):
            for h, place in ((1, turn_sub // 2), (0, turn_sub - 1)):

                ready = jnp.logical_and(t < turn_strips - turn_sub, lax.rem(t, turn_sub) == place)

                @pl.when(ready)
                def _():
                    multiply(h, lax.div(t, turn_sub) + 1)

            @pl.when(t == far - 1)
            def _():
                finish_squares()

            for h in (1, 0):
                way = hop * (me if h else last - me)
                c = t - way

                @pl.when(jnp.logical_and(c >= 0, c < strips))
                def _():
                    reduce_strip(h, c)

            for h in (1, 0):
                way = hop * (me if h else last - me)
                b = t - 2 * far + way

                @pl.when(jnp.logical_and(b >= 0, b < strips))
                def _():
                    return_strip(h, b)

                    @pl.when(lax.rem(b, turn_sub) == turn_sub - 1)
                    def _():
                        project_down(h, b)

            @pl.when(t == home)
            def _():
                send_back(0)

            return carry

        lax.fori_loop(0, strips + 2 * far, moe_step, 0)

        def finish(c, carry):
            for h in (1, 0):
                first, final = ends(h)

                @pl.when(jnp.logical_not(final))
                def _():
                    rs_copy(h, c).wait_send()

                @pl.when(jnp.logical_and(jnp.logical_not(first), c < chained))
                def _():
                    hid_copy(h, c).wait_send()

                @pl.when(jnp.logical_and(final, c >= chained))
                def _():
                    for d in range(1, count):
                        straight_copy(h, c, d).wait_send()

            return carry

        send_back(1)
        moe = pbuf[row].astype(jnp.float32)
        lax.fori_loop(0, chunks, sent, 0)
        lax.fori_loop(0, chunks, relayed, 0)
        lax.fori_loop(0, steps, done, 0)
        lax.fori_loop(0, strips, finish, 0)
        for d in range(1, rows_gx):
            h_copy(d, row).wait_send()
        for d in range(1, rows_gx):
            back_copy(d).wait_recv()
            moe = moe + ret[d].astype(jnp.float32)
        out_ref[...] = (h_all[row].astype(jnp.float32) + moe).astype(jnp.bfloat16)
        for d in range(1, rows_gx):
            back_copy(d).wait_send()

    pad = -accepted % 16
    vmem = pl.BlockSpec(memory_space=pltpu.VMEM)
    hbm = pl.BlockSpec(memory_space=pl.ANY)
    dma = pltpu.SemaphoreType.DMA
    stat = pltpu.VMEM((steps, 2 * part, lane), jnp.float32)
    piece = pltpu.VMEM((steps, rows, dim), jnp.bfloat16)
    return pl.pallas_call(
        kernel,
        out_shape=[
            jax.ShapeDtypeStruct((tokens, cols), jnp.bfloat16),
            jax.ShapeDtypeStruct((accepted, 2 * kv_cols), jnp.bfloat16),
        ],
        in_specs=[pl.BlockSpec(memory_space=pltpu.SMEM)] + [vmem] * 9 + [hbm] * 6,
        out_specs=[vmem, vmem],
        scratch_shapes=[
            pltpu.VMEM((tokens, model), jnp.bfloat16),
            pltpu.VMEM((chunks, model, 2 * dim), jnp.bfloat16),
            pltpu.VMEM((own * count, tokens, dim), jnp.bfloat16),
            pltpu.VMEM((kv_heads, span + lane, dim), jnp.bfloat16),
            pltpu.VMEM((kv_heads, span + lane, 2 * dim), jnp.bfloat16),
            pltpu.VMEM(w_o.shape, jnp.bfloat16),
            pltpu.VMEM((1, span), jnp.float32),
            pltpu.VMEM((tokens, lane), jnp.float32),
            pltpu.VMEM((steps, rows, dim), jnp.float32),
            stat,
            piece,
            piece,
            stat,
            piece,
            piece,
            stat,
            stat,
            pltpu.VMEM((heads, tokens, dim), jnp.bfloat16),
            pltpu.VMEM((tokens, cols), jnp.float32),
            pltpu.VMEM((accepted + pad, 2 * kv_cols), jnp.bfloat16),
            dma((chunks,)),
            dma((kv_heads,)),
            dma((kv_heads,)),
            dma,
            dma((count, 2 * chunks)),
            dma((count * chunks,)),
        ]
        + [dma((steps,))] * 10
        + [dma((last,)), dma, dma((rows_gx,)), dma((rows_gx,))]
        + [
            pltpu.VMEM((rows_gx, tokens, cols), jnp.bfloat16),
            pltpu.VMEM((rows_gx, tokens, cols), jnp.bfloat16),
            pltpu.VMEM((2, experts, turn_slots, everyone), jnp.bfloat16),
            pltpu.VMEM((2, experts, turn_slots, lane), jnp.float32),
            pltpu.VMEM((8, everyone), jnp.float32),
            pltpu.VMEM((count, 8, everyone), jnp.float32),
            pltpu.VMEM((1, everyone), jnp.float32),
            pltpu.VMEM((2, strips, grain, units), jnp.bfloat16),
            pltpu.VMEM((experts, depth, wide), jnp.bfloat16),
            pltpu.VMEM((experts, units, cols), jnp.bfloat16),
            pltpu.VMEM((2, strips, grain, wide), jnp.bfloat16),
            pltpu.VMEM((2, strips, grain, wide), jnp.bfloat16),
            pltpu.VMEM((2, experts, turn_slots, cols), jnp.bfloat16),
            pltpu.VMEM((rows_gx, tokens, cols), jnp.bfloat16),
            pltpu.VMEM((rows_gx, tokens, cols), jnp.bfloat16),
            dma((experts,)),
            dma((experts,)),
            dma((count,)),
            dma((count,)),
            dma((2, strips)),
            dma((2, strips)),
            dma((2, strips)),
            dma((2, strips)),
            dma((2, straight, count)),
            dma((rows_gx,)),
            dma((rows_gx,)),
        ],
        compiler_params=pltpu.CompilerParams(
            collective_id=cid, has_side_effects=True, vmem_limit_bytes=62 * 1024 * 1024
        ),
        name="layer_line",
    )(
        cache_len, states, attn_gain, q_gain, k_gain, tree_mask,
        accept, ffn_gain, routing, route_weight, w_qkv, cache_k, cache_v, w_o, w_in, w_down,
    )


def hand_over(first, second):
    def kernel(a_ref, b_ref, c_ref, d_ref):
        c_ref[...] = a_ref[...]
        d_ref[...] = b_ref[...]

    vmem = pl.BlockSpec(memory_space=pltpu.VMEM)
    return pl.pallas_call(
        kernel,
        out_shape=[
            jax.ShapeDtypeStruct(first.shape, first.dtype),
            jax.ShapeDtypeStruct(second.shape, second.dtype),
        ],
        in_specs=[vmem, vmem],
        out_specs=[vmem, vmem],
        name="hand_over",
    )(first, second)


def rms_scale(values, gain):
    return values * lax.rsqrt(jnp.mean(values * values, -1, keepdims=True) + EPS) * gain


def angles_of(position, dim):
    freqs = jnp.exp(jnp.arange(dim // 2, dtype=jnp.float32) * (-2.0 * THETA_LOG / dim))
    angles = position.astype(jnp.float32)[..., None] * freqs
    cosine = jnp.cos(angles)
    sine = jnp.sin(angles)
    return jnp.concatenate([cosine, cosine], -1), jnp.concatenate([-sine, sine], -1)


def body(
    states,
    attn_gain,
    w_qkv,
    q_gain,
    k_gain,
    cache_k,
    cache_v,
    cache_len,
    tree_mask,
    w_o,
    ffn_gain,
    routing,
    route_weight,
    w_in,
    w_down,
    accept,
):
    tok_rows, model_width = states.shape
    head_dim = q_gain.shape[0]
    kv_cols = cache_k.shape[2]
    heads_all = w_o.shape[0] // head_dim
    cache_span = cache_k.shape[1]
    cols_here = w_o.shape[1]
    col_index = lax.axis_index("gy")
    row_index = lax.axis_index("gx")
    count_gx = lax.axis_size("gx")
    count_gy = lax.axis_size("gy")
    own_heads = w_qkv.shape[1] // head_dim
    kv_heads = kv_cols // head_dim
    on_line = (
        count_gy == 4
        and w_qkv.shape[1] % (2 * head_dim) == 0
        and own_heads >= 2 * kv_heads
        and (own_heads - 2 * kv_heads) % 2 == 0
        and heads_all % (4 * kv_heads) == 0
        and tok_rows % 16 == 0
        and 128 % tok_rows == 0
        and routing.shape[0] % 128 == 0
        and w_in.shape[1] == w_o.shape[1]
        and (3 * routing.shape[0] * routing.shape[1] // (2 * w_in.shape[0] * lax.axis_size("gx"))) % 32 == 0
        and lax.axis_size("gx") % 2 == 0
    )
    if on_line:
        layer_out, accepted_kv = layer_line(
            states,
            attn_gain,
            w_qkv,
            q_gain[None],
            k_gain[None],
            cache_k[0],
            cache_v[0],
            cache_len,
            tree_mask[0],
            w_o,
            accept[0],
            ffn_gain,
            routing.T,
            route_weight.T,
            w_in,
            w_down,
            0,
        )
        layer_out, accepted_kv = hand_over(layer_out, accepted_kv)
        return (layer_out, accepted_kv[None])
    normed = rms_scale(states.astype(jnp.float32), attn_gain.astype(jnp.float32)).astype(
        jnp.bfloat16
    )
    qkv_part = jnp.dot(normed, w_qkv, preferred_element_type=jnp.float32).astype(jnp.bfloat16)
    (qkv_blocks,) = exchange([qkv_part], "gy", False, 0)
    qkv_whole = jnp.swapaxes(qkv_blocks, 0, 1).reshape(tok_rows, -1)
    q_cols = heads_all * head_dim
    depth = jnp.sum(tree_mask, -1) - 1
    cosine, sine = angles_of((cache_len[:, None] + depth)[0], head_dim)
    states_here = lax.dynamic_slice_in_dim(states, col_index * cols_here, cols_here, 1)
    gathered, k_rot = attention_block(
        qkv_whole,
        q_gain[None],
        k_gain[None],
        cosine,
        sine,
        cache_k[0],
        cache_v[0],
        cache_len - col_index * cache_span,
        tree_mask[0],
        states_here,
        w_o,
        1,
    )
    kv_new = jnp.concatenate([k_rot, qkv_whole[:, q_cols + kv_cols :]], -1)[None]
    accepted_kv = jnp.einsum(
        "rat,rtc->rac", accept.astype(jnp.bfloat16), kv_new, preferred_element_type=jnp.float32
    ).astype(jnp.bfloat16)
    resid = lax.dynamic_index_in_dim(gathered, row_index, 0, False)
    exp_here = w_in.shape[0]
    expert_count = exp_here * count_gx
    top_k = routing.shape[1]
    most_rows = 3 * tok_rows * top_k // (2 * expert_count)
    hidden_units = w_down.shape[1]
    gain_float = ffn_gain.astype(jnp.float32)
    tokens = routing.shape[0]
    slots = count_gx * most_rows
    own_experts = row_index * exp_here + jnp.arange(exp_here, dtype=jnp.int32)
    matched = routing[:, None, :] == own_experts[None, :, None]
    hits = jnp.any(matched, -1)
    weights = jnp.sum(jnp.where(matched, route_weight[:, None, :], 0.0), -1)
    order = jnp.arange(tok_rows, dtype=jnp.int32)
    earlier = (order[:, None] > order[None, :]).astype(jnp.bfloat16)
    rank = jnp.einsum(
        "tu,bue->bte",
        earlier,
        hits.astype(jnp.bfloat16).reshape(count_gx, tok_rows, exp_here),
        preferred_element_type=jnp.float32,
    ).astype(jnp.int32)
    first_slot = jnp.arange(count_gx, dtype=jnp.int32)[:, None, None] * most_rows
    slot_of = jnp.where(hits, (rank + first_slot).reshape(tokens, exp_here), -1)
    pick = slot_of.T[:, None, :] == jnp.arange(slots, dtype=jnp.int32)[None, :, None]
    pick_matrix = pick.astype(jnp.bfloat16)
    slot_weight = jnp.sum(jnp.where(pick, weights.T[:, None, :], 0.0), -1)
    gathered = gathered.reshape(tokens, cols_here).astype(jnp.float32)
    token_squares = jnp.sum(gathered * gathered, -1)
    slot_squares = jnp.sum(jnp.where(pick, token_squares, 0.0), -1)
    piece = 16
    slot_squares = jnp.pad(slot_squares.reshape(-1, piece), ((0, 0), (0, 128 - piece)))
    scaled = (gathered * gain_float).astype(jnp.bfloat16)
    rows = jnp.einsum(
        "est,td->esd", pick_matrix, scaled, preferred_element_type=jnp.float32
    ).astype(jnp.bfloat16)
    layer_out = expert_layer(
        rows,
        slot_squares,
        w_in,
        w_down,
        slot_weight[..., None],
        pick_matrix.reshape(exp_here * slots, tokens),
        resid,
        model_width,
        4,
    )
    return (layer_out, accepted_kv)


def solution(mesh):
    in_specs = (
        P("gx", None),
        P(),
        P(None, "gy"),
        P(),
        P(),
        P("gx", "gy", None),
        P("gx", "gy", None),
        P("gx"),
        P("gx", None, None),
        P(None, "gy"),
        P("gy"),
        P(),
        P(),
        P("gx", "gy", None),
        P("gx", None, "gy"),
        P("gx", None, None),
    )
    out_specs = (P("gx", "gy"), P("gx", None, None))
    return jax.shard_map(body, mesh=mesh, in_specs=in_specs, out_specs=out_specs, check_vma=False)
```

```python
import math

import jax
import jax.numpy as jnp
from jax import lax
from jax.experimental import pallas as pl
from jax.experimental.pallas import tpu as pltpu
from jax.sharding import PartitionSpec as P

EPS = 1e-06
NEG = -1e30
THETA_LOG = math.log(1000000.0)


MESH = pl.DeviceIdType.MESH


def exchange(arrays, axis, scatter, cid):
    count = lax.axis_size(axis)
    number = len(arrays)

    def kernel(*refs):
        ins, outs = refs[:number], refs[number : 2 * number]
        send, recv, local = refs[2 * number :]
        me = lax.axis_index(axis)
        barrier = pltpu.get_barrier_semaphore()
        for d in range(1, count):
            pl.semaphore_signal(
                barrier, inc=1, device_id={axis: lax.rem(me + d, count)}, device_id_type=MESH
            )
        pl.semaphore_wait(barrier, count - 1)
        copies = []
        for d in range(1, count):
            peer = lax.rem(me + d, count)
            for i in range(number):
                copy = pltpu.make_async_remote_copy(
                    src_ref=ins[i].at[peer] if scatter else ins[i],
                    dst_ref=outs[i].at[me],
                    send_sem=send.at[i, d],
                    recv_sem=recv.at[i, d],
                    device_id={axis: peer},
                    device_id_type=MESH,
                )
                copy.start()
                copies.append(copy)
        own = []
        for i in range(number):
            copy = pltpu.make_async_copy(
                ins[i].at[me] if scatter else ins[i], outs[i].at[me], local.at[i]
            )
            copy.start()
            own.append(copy)
        for copy in own + copies:
            copy.wait()

    outs = [
        jax.ShapeDtypeStruct(x.shape if scatter else (count,) + x.shape, x.dtype) for x in arrays
    ]
    return pl.pallas_call(
        kernel,
        out_shape=outs,
        in_specs=[pl.BlockSpec(memory_space=pltpu.VMEM)] * number,
        out_specs=[pl.BlockSpec(memory_space=pltpu.VMEM)] * number,
        scratch_shapes=[
            pltpu.SemaphoreType.DMA((number, count)),
            pltpu.SemaphoreType.DMA((number, count)),
            pltpu.SemaphoreType.DMA((number,)),
        ],
        compiler_params=pltpu.CompilerParams(collective_id=cid, has_side_effects=True),
        name="exchange_%d" % cid,
    )(*arrays)


def expert_layer(rows, squares, w_in, w_down, slot_weight, pick_back, resid, model_width, cid):
    axis = "gy"
    count = lax.axis_size(axis)
    peers = lax.axis_size("gx")
    experts, slots, depth = rows.shape
    tokens, cols = resid.shape
    wide = w_in.shape[2]
    units = wide // 2
    half = experts // 2
    piece = 16
    sub = slots // piece
    chunks = half * sub
    hop = 2
    far = hop * (count - 1)

    def kernel(
        x_ref, sq_ref, weight_ref, pick_ref, resid_ref, w_hbm, d_hbm, out_ref,
        hid_ref, wbuf, dbuf, part, rbuf, sqbuf, inv_ref, obuf, pbuf, ret,
        wsem, dsem, rs_s, rs_r, h_s, h_r, sq_s, sq_r, g_s, g_r,
    ):
        me = lax.axis_index(axis)
        prev = lax.rem(me + count - 1, count)
        nxt = lax.rem(me + 1, count)
        at_low = me == 0
        at_high = me == count - 1

        def load(e):
            return pltpu.make_async_copy(w_hbm.at[e], wbuf.at[e], wsem.at[e])

        def load_down(e):
            return pltpu.make_async_copy(d_hbm.at[e], dbuf.at[e], dsem.at[e])

        row = lax.axis_index("gx")
        for s in range(half):
            load(half + s).start()
            load(s).start()
        for s in range(half):
            load_down(half + s).start()
            load_down(s).start()
        barrier = pltpu.get_barrier_semaphore()
        for d in range(1, count):
            pl.semaphore_signal(
                barrier, inc=1, device_id={axis: lax.rem(me + d, count)}, device_id_type=MESH
            )
        for d in range(1, peers):
            pl.semaphore_signal(
                barrier, inc=1, device_id={"gx": lax.rem(row + d, peers)}, device_id_type=MESH
            )

        def multiply(h, s):
            e = h * half + s
            load(e).wait()
            value = jnp.dot(x_ref[e], wbuf[e], preferred_element_type=jnp.float32)
            for j in range(sub):
                part[h, s * sub + j] = value[j * piece : (j + 1) * piece].astype(jnp.bfloat16)

        multiply(1, 0)
        multiply(0, 0)
        pl.semaphore_wait(barrier, count + peers - 2)

        def sq_copy(d):
            return pltpu.make_async_remote_copy(
                src_ref=sq_ref,
                dst_ref=sqbuf.at[d],
                send_sem=sq_s.at[d],
                recv_sem=sq_r.at[d],
                device_id={axis: lax.rem(me + d, count)},
                device_id_type=MESH,
            )

        for d in range(1, count):
            sq_copy(d).start()

        def finish_squares():
            total = sq_ref[...]
            for d in range(1, count):
                sq_copy(d).wait()
                total = total + sqbuf[d]
            inv_ref[...] = lax.rsqrt(total / model_width + EPS)

        diagonal = lax.broadcasted_iota(jnp.int32, (piece, 128), 0) == lax.broadcasted_iota(
            jnp.int32, (piece, 128), 1
        )

        def rs_copy(h, c):
            return pltpu.make_async_remote_copy(
                src_ref=part.at[h, c],
                dst_ref=rbuf.at[h, c],
                send_sem=rs_s.at[h, c],
                recv_sem=rs_r.at[h, c],
                device_id={axis: nxt if h else prev},
                device_id_type=MESH,
            )

        def hid_copy(h, c):
            return pltpu.make_async_remote_copy(
                src_ref=hid_ref.at[h, c],
                dst_ref=hid_ref.at[h, c],
                send_sem=h_s.at[h, c],
                recv_sem=h_r.at[h, c],
                device_id={axis: prev if h else nxt},
                device_id_type=MESH,
            )

        def ends(h):
            return (at_low, at_high) if h else (at_high, at_low)

        def reduce_chunk(h, c):
            first, last = ends(h)

            @pl.when(jnp.logical_not(first))
            def _():
                rs_copy(h, c).wait_recv()

            @pl.when(jnp.logical_not(jnp.logical_or(first, last)))
            def _():
                part[h, c] = (
                    part[h, c].astype(jnp.float32) + rbuf[h, c].astype(jnp.float32)
                ).astype(jnp.bfloat16)

            @pl.when(jnp.logical_not(last))
            def _():
                rs_copy(h, c).start()

            @pl.when(last)
            def _():
                row = inv_ref[pl.ds(h * chunks + c, 1), :]
                inverse = jnp.sum(jnp.where(diagonal, row, 0.0), 1, keepdims=True)
                summed = part[h, c].astype(jnp.float32) + rbuf[h, c].astype(jnp.float32)
                gate = summed[:, :units] * inverse
                up = summed[:, units:] * inverse
                hid_ref[h, c] = (gate / (1.0 + jnp.exp(-gate)) * up).astype(jnp.bfloat16)
                hid_copy(h, c).start()

        def return_chunk(h, c):
            first, last = ends(h)

            @pl.when(jnp.logical_not(last))
            def _():
                hid_copy(h, c).wait_recv()

            @pl.when(jnp.logical_not(jnp.logical_or(first, last)))
            def _():
                hid_copy(h, c).start()

        def project(h, s):
            e = h * half + s
            load_down(e).wait()
            value = hid_ref[h, pl.ds(s * sub, sub)].reshape(slots, units)
            value = jnp.dot(value, dbuf[e], preferred_element_type=jnp.float32)
            obuf[e] = (value * weight_ref[e]).astype(jnp.bfloat16)

        def step(t, carry):
            for h, place in ((1, 1), (0, sub // 2 + 1)):

                @pl.when(jnp.logical_and(t < chunks - sub, lax.rem(t, sub) == place))
                def _():
                    multiply(h, lax.div(t, sub) + 1)

            @pl.when(t == far - 1)
            def _():
                finish_squares()

            for h in (1, 0):
                way = hop * (me if h else count - 1 - me)
                c = t - way

                @pl.when(jnp.logical_and(c >= 0, c < chunks))
                def _():
                    reduce_chunk(h, c)

            for h in (1, 0):
                way = hop * (me if h else count - 1 - me)
                b = t - 2 * far + way

                @pl.when(jnp.logical_and(b >= 0, b < chunks))
                def _():
                    return_chunk(h, b)

                    @pl.when(lax.rem(b, sub) == sub - 1)
                    def _():
                        project(h, lax.div(b, sub))

            return carry

        lax.fori_loop(0, chunks + 2 * far, step, 0)

        def finish(c, carry):
            for h in (1, 0):
                first, last = ends(h)

                @pl.when(jnp.logical_not(last))
                def _():
                    rs_copy(h, c).wait_send()

                @pl.when(jnp.logical_not(first))
                def _():
                    hid_copy(h, c).wait_send()

            return carry

        summed = lax.dot_general(
            pick_ref[...],
            obuf[...].reshape(experts * slots, cols),
            (((0,), (0,)), ((), ())),
            preferred_element_type=jnp.float32,
        )
        for p in range(peers):
            pbuf[p] = summed[p * tokens : (p + 1) * tokens].astype(jnp.bfloat16)

        def back_copy(d):
            peer = lax.rem(row + d, peers)
            return pltpu.make_async_remote_copy(
                src_ref=pbuf.at[peer],
                dst_ref=ret.at[d],
                send_sem=g_s.at[d],
                recv_sem=g_r.at[d],
                device_id={"gx": peer},
                device_id_type=MESH,
            )

        for d in range(1, peers):
            back_copy(d).start()
        moe = pbuf[row].astype(jnp.float32)
        lax.fori_loop(0, chunks, finish, 0)
        for d in range(1, peers):
            back_copy(d).wait_recv()
            moe = moe + ret[d].astype(jnp.float32)
        out_ref[...] = (resid_ref[...].astype(jnp.float32) + moe).astype(jnp.bfloat16)
        for d in range(1, peers):
            back_copy(d).wait_send()

    vmem = pl.BlockSpec(memory_space=pltpu.VMEM)
    hbm = pl.BlockSpec(memory_space=pl.ANY)
    dma = pltpu.SemaphoreType.DMA
    return pl.pallas_call(
        kernel,
        out_shape=jax.ShapeDtypeStruct((tokens, cols), jnp.bfloat16),
        in_specs=[vmem] * 5 + [hbm, hbm],
        out_specs=vmem,
        scratch_shapes=[
            pltpu.VMEM((2, chunks, piece, units), jnp.bfloat16),
            pltpu.VMEM((experts, depth, wide), jnp.bfloat16),
            pltpu.VMEM((experts, units, cols), jnp.bfloat16),
            pltpu.VMEM((2, chunks, piece, wide), jnp.bfloat16),
            pltpu.VMEM((2, chunks, piece, wide), jnp.bfloat16),
            pltpu.VMEM((count, 2 * chunks, 128), jnp.float32),
            pltpu.VMEM((2 * chunks, 128), jnp.float32),
            pltpu.VMEM((experts, slots, cols), jnp.bfloat16),
            pltpu.VMEM((peers, tokens, cols), jnp.bfloat16),
            pltpu.VMEM((peers, tokens, cols), jnp.bfloat16),
            dma((experts,)),
            dma((experts,)),
            dma((2, chunks)),
            dma((2, chunks)),
            dma((2, chunks)),
            dma((2, chunks)),
            dma((count,)),
            dma((count,)),
            dma((peers,)),
            dma((peers,)),
        ],
        compiler_params=pltpu.CompilerParams(
            collective_id=cid, has_side_effects=True, vmem_limit_bytes=52 * 1024 * 1024
        ),
        name="expert_layer",
    )(rows, squares, slot_weight, pick_back, resid, w_in, w_down)


def attention_block(
    qkv, q_gain, k_gain, cosine, sine, cache_k, cache_v, limit, tree_mask, states_here, w_o, cid
):
    blocks = lax.axis_size("gy")
    rows_gx = lax.axis_size("gx")
    tokens = qkv.shape[0]
    span, kv_cols = cache_k.shape
    dim = q_gain.shape[1]
    kv_heads = kv_cols // dim
    heads = qkv.shape[1] // dim - 2 * kv_heads
    group = heads // kv_heads
    per_block = heads // blocks
    blocks_here = blocks // kv_heads
    width = per_block * dim
    cols = w_o.shape[1]
    scale = dim ** (-0.5)

    def kernel(
        limit_ref, q_ref, qg_ref, kg_ref, cos_ref, sin_ref, k_ref, v_ref, mask_ref, st_ref, wo_hbm,
        h_ref, rot_ref,
        acc_out, stat_out, acc_in, stat_in, attn, wo,
        wo_sem, a_s, a_r, s_s, s_r, t_s, t_r, h_s, h_r,
    ):
        me = lax.axis_index("gy")
        row = lax.axis_index("gx")
        load = pltpu.make_async_copy(wo_hbm, wo, wo_sem)
        load.start()
        barrier = pltpu.get_barrier_semaphore()
        for axis, here, count in (("gy", me, blocks), ("gx", row, rows_gx)):
            for d in range(1, count):
                pl.semaphore_signal(
                    barrier, inc=1, device_id={axis: lax.rem(here + d, count)}, device_id_type=MESH
                )
        pl.semaphore_wait(barrier, blocks + rows_gx - 2)

        def send(src, dst, send_sem, recv_sem, axis, peer):
            return pltpu.make_async_remote_copy(
                src_ref=src,
                dst_ref=dst,
                send_sem=send_sem,
                recv_sem=recv_sem,
                device_id={axis: peer},
                device_id_type=MESH,
            )

        def part_copies(block, source):
            return (
                send(acc_out.at[block], acc_in.at[source], a_s.at[block], a_r.at[source], "gy", block),
                send(stat_out.at[block], stat_in.at[source], s_s.at[block], s_r.at[source], "gy", block),
            )

        cos = cos_ref[...]
        sin = sin_ref[...]

        def turn(value, gain):
            value = value.astype(jnp.float32)
            value = value * lax.rsqrt(jnp.mean(value * value, -1, keepdims=True) + EPS) * gain
            return (value * cos + pltpu.roll(value, dim // 2, 1) * sin).astype(jnp.bfloat16)

        q_gain_row = qg_ref[...].astype(jnp.float32)
        k_gain_row = kg_ref[...].astype(jnp.float32)
        contract = (((1,), (1,)), ((), ()))
        diagonal = lax.broadcasted_iota(jnp.int32, (tokens, 128), 0) == lax.broadcasted_iota(
            jnp.int32, (tokens, 128), 1
        )

        def one_head(i, carry):
            g = lax.rem(lax.div(me, blocks_here) + 1 + i, kv_heads)

            def lanes(first, size):
                return pl.ds(pl.multiple_of(first, 128), size)

            query = jnp.concatenate(
                [
                    turn(q_ref[:, lanes((g * group + j) * dim, dim)], q_gain_row)
                    for j in range(group)
                ],
                0,
            )
            keys = turn(q_ref[:, lanes((heads + g) * dim, dim)], k_gain_row)
            values = q_ref[:, lanes((heads + kv_heads + g) * dim, dim)]
            rot_ref[:, lanes(g * dim, dim)] = keys
            tree = (
                lax.dot_general(query, keys, contract, preferred_element_type=jnp.float32) * scale
            )
            mask = jnp.concatenate([mask_ref[...]] * group, 0)
            tree_ok = jnp.logical_and(mask == 1, me == 0)
            tree = jnp.where(tree_ok, tree, NEG)
            score = (
                lax.dot_general(
                    query,
                    k_ref[:, lanes(g * dim, dim)],
                    contract,
                    preferred_element_type=jnp.float32,
                )
                * scale
            )
            valid = lax.broadcasted_iota(jnp.int32, score.shape, 1) < limit_ref[0]
            score = jnp.where(valid, score, NEG)
            top = jnp.maximum(jnp.max(score, 1, keepdims=True), jnp.max(tree, 1, keepdims=True))
            prob = jnp.where(valid, jnp.exp(score - top), 0.0).astype(jnp.bfloat16)
            prob_tree = jnp.where(tree_ok, jnp.exp(tree - top), 0.0).astype(jnp.bfloat16)
            total = jnp.sum(prob.astype(jnp.float32), 1, keepdims=True) + jnp.sum(
                prob_tree.astype(jnp.float32), 1, keepdims=True
            )
            acc = jnp.dot(prob, v_ref[:, lanes(g * dim, dim)], preferred_element_type=jnp.float32)
            acc = acc + jnp.dot(prob_tree, values, preferred_element_type=jnp.float32)
            acc = acc.astype(jnp.bfloat16)
            for b in range(blocks_here):
                block = g * blocks_here + b
                for place in range(per_block):
                    j = b * per_block + place
                    rows = slice(j * tokens, (j + 1) * tokens)
                    acc_out[block, :, place * dim : (place + 1) * dim] = acc[rows]
                    for k, column in enumerate((top, total)):
                        stat_out[block, k * per_block + place : k * per_block + place + 1, :] = (
                            jnp.sum(jnp.where(diagonal, column[rows], 0.0), 0, keepdims=True)
                        )

                @pl.when(block != me)
                def _():
                    for copy in part_copies(block, me):
                        copy.start()

            return carry

        lax.fori_loop(0, kv_heads, one_head, 0)

        acc_in[me] = acc_out[me]
        stat_in[me] = stat_out[me]
        for d in range(1, blocks):
            source = lax.rem(me + d, blocks)
            for copy in part_copies(source, source):
                copy.wait_recv()
        tops = [stat_in[j, :per_block, :] for j in range(blocks)]
        best = tops[0]
        for j in range(1, blocks):
            best = jnp.maximum(best, tops[j])
        factors = [jnp.exp(tops[j] - best) for j in range(blocks)]
        denom = stat_in[0, per_block:, :] * factors[0]
        for j in range(1, blocks):
            denom = denom + stat_in[j, per_block:, :] * factors[j]
        for place in range(per_block):
            joined = jnp.zeros((tokens, dim), jnp.float32)
            for j in range(blocks):
                line = (factors[j] / denom)[place : place + 1, :]
                column = jnp.sum(jnp.where(diagonal, line, 0.0), 1, keepdims=True)
                joined = joined + column * acc_in[
                    j, :, place * dim : (place + 1) * dim
                ].astype(jnp.float32)
            attn[me, :, place * dim : (place + 1) * dim] = joined.astype(jnp.bfloat16)

        def attn_copy(d, source):
            return send(
                attn.at[source], attn.at[source], t_s.at[d], t_r.at[d], "gy", lax.rem(me + d, blocks)
            )

        for d in range(1, blocks):
            attn_copy(d, me).start()
        load.wait()

        def project(source):
            return jnp.dot(
                attn[source],
                wo[pl.ds(pl.multiple_of(source * width, width), width), :],
                preferred_element_type=jnp.float32,
            )

        total = st_ref[...].astype(jnp.float32) + project(me)
        for d in range(1, blocks):
            source = lax.rem(me + blocks - d, blocks)
            attn_copy(d, source).wait_recv()
            total = total + project(source)
        h_ref[row] = total.astype(jnp.bfloat16)

        def h_copy(d, source):
            return send(
                h_ref.at[source], h_ref.at[source], h_s.at[d], h_r.at[d], "gx",
                lax.rem(row + d, rows_gx),
            )

        for d in range(1, rows_gx):
            h_copy(d, row).start()
        for d in range(1, blocks):
            block = lax.rem(me + d, blocks)
            for copy in part_copies(block, me):
                copy.wait_send()
            attn_copy(d, me).wait_send()
        for d in range(1, rows_gx):
            h_copy(d, lax.rem(row + rows_gx - d, rows_gx)).wait_recv()
            h_copy(d, row).wait_send()

    vmem = pl.BlockSpec(memory_space=pltpu.VMEM)
    dma = pltpu.SemaphoreType.DMA
    return pl.pallas_call(
        kernel,
        out_shape=[
            jax.ShapeDtypeStruct((rows_gx, tokens, cols), jnp.bfloat16),
            jax.ShapeDtypeStruct((tokens, kv_cols), jnp.bfloat16),
        ],
        in_specs=[pl.BlockSpec(memory_space=pltpu.SMEM)]
        + [vmem] * 9
        + [pl.BlockSpec(memory_space=pl.ANY)],
        out_specs=[vmem, vmem],
        scratch_shapes=[
            pltpu.VMEM((blocks, tokens, width), jnp.bfloat16),
            pltpu.VMEM((blocks, 2 * per_block, 128), jnp.float32),
            pltpu.VMEM((blocks, tokens, width), jnp.bfloat16),
            pltpu.VMEM((blocks, 2 * per_block, 128), jnp.float32),
            pltpu.VMEM((blocks, tokens, width), jnp.bfloat16),
            pltpu.VMEM(w_o.shape, jnp.bfloat16),
            dma,
            dma((blocks,)),
            dma((blocks,)),
            dma((blocks,)),
            dma((blocks,)),
            dma((blocks,)),
            dma((blocks,)),
            dma((rows_gx,)),
            dma((rows_gx,)),
        ],
        compiler_params=pltpu.CompilerParams(
            collective_id=cid, has_side_effects=True, vmem_limit_bytes=48 * 1024 * 1024
        ),
        name="attention_block",
    )(
        limit, qkv, q_gain, k_gain, cosine, sine, cache_k, cache_v, tree_mask, states_here, w_o
    )


def layer_line(
    states, attn_gain, w_qkv, q_gain, k_gain, cache_k, cache_v, cache_len, tree_mask, w_o, accept,
    ffn_gain, routing, route_weight, w_in, w_down, cid
):
    count = lax.axis_size("gy")
    rows_gx = lax.axis_size("gx")
    tokens, model = states.shape
    span, kv_cols = cache_k.shape
    dim = q_gain.shape[1]
    kv_heads = kv_cols // dim
    own = w_qkv.shape[1] // dim
    heads = own * count - 2 * kv_heads
    group = heads // kv_heads
    cols = w_o.shape[1]
    chunks = own // 2
    part = group // 2
    steps = heads // part
    first_relay = 2
    lag = 3
    rows = part * tokens
    lane = 128
    accepted = accept.shape[0]
    last = count - 1
    factor = dim ** (-0.5) / math.log(2.0)
    top_k, everyone = routing.shape
    experts, depth, wide = w_in.shape
    units = wide // 2
    most_rows = 3 * tokens * top_k // (2 * experts * rows_gx)
    slots = rows_gx * most_rows
    split = experts // 2
    grain = 16
    sub = slots // grain
    strips = split * sub
    turn_slots = slots // 2
    turn_sub = sub // 2
    turn_strips = strips // 2
    hop = 3
    far = hop * last
    straight = 4
    chained = strips - straight

    def kernel(
        len_ref, st_ref, ag_ref, qg_ref, kg_ref, mask_ref, acc_ref, fg_ref, rt_ref, rw_ref,
        wq_hbm, k_hbm, v_hbm, wo_hbm, w_hbm, d_hbm,
        out_ref, akv_ref,
        normed, wq, qall, kext, vext, wo, bias, tree_bias,
        own_acc, own_stat, end_out, end_in, stat_in, mid_out, mid_in, mstat_out, mstat_in,
        attn, total, akv,
        wq_sem, k_sem, v_sem, wo_sem, q_s, q_r, e_s, e_r, es_s, es_r, m_s, m_r, ms_s, ms_r,
        f_s, f_r, a_s, a_r, h_s, h_r,
        h_all, scaled, pick, wcol, sq_out, sq_in, inv_row, hid, wbuf, dbuf, part_sum, rbuf, obuf, pbuf, ret,
        w_sem, d_sem, sq_s, sq_r, rs_s, rs_r, hid_s, hid_r, st_s, g_s, g_r,
    ):
        me = lax.axis_index("gy")
        row = lax.axis_index("gx")
        is_last = me == last
        is_end = jnp.logical_or(me == 0, is_last)
        is_mid = jnp.logical_not(is_end)
        low = me < 2
        mid_of = jnp.where(low, 1, 2)
        end_of = jnp.where(low, 0, last)
        other_mid = 3 - mid_of

        def send(src, dst, send_sem, recv_sem, axis, peer):
            return pltpu.make_async_remote_copy(
                src_ref=src,
                dst_ref=dst,
                send_sem=send_sem,
                recv_sem=recv_sem,
                device_id={axis: peer},
                device_id_type=MESH,
            )

        def chunk_at(i):
            return jnp.where(is_last, i, chunks - 1 - i)

        def load_w(c):
            return pltpu.make_async_copy(
                wq_hbm.at[:, pl.ds(pl.multiple_of(c * 2 * dim, 2 * dim), 2 * dim)],
                wq.at[c],
                wq_sem.at[c],
            )

        def load_k(g):
            return pltpu.make_async_copy(
                k_hbm.at[:, g * dim : (g + 1) * dim], kext.at[g, 0:span, :], k_sem.at[g]
            )

        def load_v(g):
            return pltpu.make_async_copy(
                v_hbm.at[:, g * dim : (g + 1) * dim], vext.at[g, 0:span, 0:dim], v_sem.at[g]
            )

        load_o = pltpu.make_async_copy(wo_hbm, wo, wo_sem)
        for i in range(chunks):
            load_w(chunk_at(i)).start()
        for g in range(kv_heads - 1, -1, -1):
            load_k(g).start()
            load_v(g).start()
        load_o.start()
        barrier = pltpu.get_barrier_semaphore()
        for axis, here, number in (("gy", me, count), ("gx", row, rows_gx)):
            for d in range(1, number):
                pl.semaphore_signal(
                    barrier, inc=1, device_id={axis: lax.rem(here + d, number)}, device_id_type=MESH
                )

        value = st_ref[...].astype(jnp.float32)
        value = value * lax.rsqrt(jnp.mean(value * value, -1, keepdims=True) + EPS)
        normed[...] = (value * ag_ref[...].reshape(1, model).astype(jnp.float32)).astype(jnp.bfloat16)
        mask = mask_ref[...]
        position = len_ref[0] + jnp.sum(mask, -1, keepdims=True) - 1
        place = lax.broadcasted_iota(jnp.int32, (tokens, dim), 1)
        half = lax.rem(place, dim // 2).astype(jnp.float32)
        angle = position.astype(jnp.float32) * jnp.exp(half * (-2.0 * THETA_LOG / dim))
        cos = jnp.cos(angle)
        sin = jnp.sin(angle)
        sin = jnp.where(place < dim // 2, -sin, sin)
        limit = len_ref[0] - me * span
        spot = lax.broadcasted_iota(jnp.int32, (1, span), 1)
        bias[...] = jnp.where(spot < limit, 0.0, NEG)
        allowed = jnp.logical_and(mask == 1, is_last)
        tree_bias[...] = jnp.full((tokens, lane), NEG, jnp.float32)
        tree_bias[:, 0:tokens] = jnp.where(allowed, 0.0, NEG)
        for g in range(kv_heads):
            kext[g, span : span + lane, :] = jnp.zeros((lane, dim), jnp.bfloat16)
            vext[g, span : span + lane, 0:dim] = jnp.zeros((lane, dim), jnp.bfloat16)
            vext[g, :, dim : 2 * dim] = jnp.ones((span + lane, dim), jnp.bfloat16)
        total[...] = st_ref[:, pl.ds(pl.multiple_of(me * cols, 128), cols)].astype(jnp.float32)
        q_gain_row = qg_ref[...].astype(jnp.float32)
        k_gain_row = kg_ref[...].astype(jnp.float32)

        def q_copy(k, c, peer):
            block = qall.at[pl.ds(2 * k, 2)]
            return send(block, block, q_s.at[peer, c], q_r.at[k], "gy", peer)

        relay = me == last - 1

        def direct(k, peer):
            far_pair = jnp.logical_and(me == 0, peer == last)
            there = jnp.logical_and(me != peer, jnp.logical_not(far_pair))
            return jnp.logical_and(there, 2 * k < heads)

        def relay_copy(k):
            return q_copy(k, chunks + k, last)

        pl.semaphore_wait(barrier, count + rows_gx - 2)

        def project_in(i, carry):
            c = chunk_at(i)
            load_w(c).wait()
            value = jnp.dot(normed[...], wq[c], preferred_element_type=jnp.float32)
            value = value.astype(jnp.bfloat16)
            k = me * chunks + c
            for j in range(2):
                head = 2 * k + j
                raw = value[:, j * dim : (j + 1) * dim]
                turned = raw.astype(jnp.float32)
                gain = jnp.where(head < heads, q_gain_row, k_gain_row)
                scale = lax.rsqrt(jnp.mean(turned * turned, -1, keepdims=True) + EPS)
                turned = turned * scale * gain
                turned = (turned * cos + pltpu.roll(turned, dim // 2, 1) * sin).astype(jnp.bfloat16)
                qall[head] = jnp.where(head < heads + kv_heads, turned, raw)
            for peer in range(count - 1, -1, -1):

                @pl.when(direct(k, peer))
                def _():
                    q_copy(k, c, peer).start()

            return carry

        lax.fori_loop(0, chunks, project_in, 0)

        def load_in(e):
            return pltpu.make_async_copy(w_hbm.at[e], wbuf.at[e], w_sem.at[e])

        def load_down(e):
            return pltpu.make_async_copy(d_hbm.at[e], dbuf.at[e], d_sem.at[e])

        for e in range(split):
            load_in(split + e).start()
            load_in(e).start()
        for e in range(split):
            load_down(split + e).start()
            load_down(e).start()

        names = rt_ref[...]
        shares = rw_ref[...]
        hits, weights = [], []
        for e in range(experts):
            matched = names == row * experts + e
            hits.append(jnp.sum(jnp.where(matched, 1.0, 0.0), 0, keepdims=True))
            weights.append(jnp.sum(jnp.where(matched, shares, 0.0), 0, keepdims=True))
        hit = jnp.concatenate(hits, 0)
        before = lax.broadcasted_iota(jnp.int32, (lane, lane), 0)
        after = lax.broadcasted_iota(jnp.int32, (lane, lane), 1)
        same = lax.div(before, tokens) == lax.div(after, tokens)
        earlier = jnp.where(jnp.logical_and(before < after, same), 1.0, 0.0).astype(jnp.bfloat16)
        rank = jnp.concatenate(
            [
                jnp.dot(
                    hit[:, i : i + lane].astype(jnp.bfloat16),
                    earlier,
                    preferred_element_type=jnp.float32,
                )
                for i in range(0, everyone, lane)
            ],
            1,
        )
        block_no = lax.div(lax.broadcasted_iota(jnp.int32, (experts, everyone), 1), tokens)
        first_slot = (lax.div(block_no, 2) * most_rows).astype(jnp.float32)
        slot_no = lax.broadcasted_iota(jnp.int32, (turn_slots, everyone), 0).astype(jnp.float32)
        for turn in range(2):
            here = jnp.logical_and(hit > 0.5, lax.rem(block_no, 2) == turn)
            slot_of = jnp.where(here, rank + first_slot, -1.0)
            for e in range(experts):
                chosen = slot_no == slot_of[e : e + 1]
                pick[turn, e] = jnp.where(chosen, 1.0, 0.0).astype(jnp.bfloat16)
                column = jnp.sum(jnp.where(chosen, weights[e], 0.0), 1, keepdims=True)
                wcol[turn, e] = jnp.broadcast_to(column, (turn_slots, lane))

        def akv_copy(d, peer):
            return send(akv, akv, a_s.at[d], a_r, "gy", peer)

        @pl.when(is_last)
        def _():
            pick = acc_ref[...].astype(jnp.bfloat16)
            akv[...] = jnp.zeros(akv.shape, jnp.bfloat16)
            for i in range(2 * kv_heads):
                akv[0:accepted, i * dim : (i + 1) * dim] = jnp.dot(
                    pick, qall[heads + i], preferred_element_type=jnp.float32
                ).astype(jnp.bfloat16)
            for d in range(last):
                akv_copy(d, d).start()
            for g in range(kv_heads):
                kext[g, span : span + tokens, :] = qall[heads + g]
                vext[g, span : span + tokens, 0:dim] = qall[heads + kv_heads + g]

        diagonal = lax.broadcasted_iota(jnp.int32, (tokens, lane), 0) == lax.broadcasted_iota(
            jnp.int32, (tokens, lane), 1
        )

        def as_row(column):
            return jnp.sum(jnp.where(diagonal, column, 0.0), 0, keepdims=True)

        def as_column(line):
            return jnp.sum(jnp.where(diagonal, line, 0.0), 1, keepdims=True)

        contract = (((1,), (1,)), ((), ()))

        def end_copy(s):
            return (
                send(end_out.at[s], end_in.at[s], e_s.at[s], e_r.at[s], "gy", mid_of),
                send(own_stat.at[s], stat_in.at[s], es_s.at[s], es_r.at[s], "gy", mid_of),
            )

        def mid_copy(s):
            return (
                send(mid_out.at[s], mid_in.at[s], m_s.at[s], m_r.at[s], "gy", other_mid),
                send(mstat_out.at[s], mstat_in.at[s], ms_s.at[s], ms_r.at[s], "gy", other_mid),
            )

        def block_of(s):
            return steps - 1 - s

        def final_copy(s):
            place = attn.at[pl.ds(block_of(s) * part, part)]
            return send(place, place, f_s.at[s], f_r.at[s], "gy", end_of)

        def attend(s):
            b = block_of(s)
            for n in range(part // 2):
                k = b * (part // 2) + n
                source = lax.div(k, chunks)
                relayed = jnp.logical_and(relay, source == 0)

                @pl.when(jnp.logical_and(source != me, jnp.logical_not(relayed)))
                def _():
                    q_copy(k, 0, source).wait_recv()

            g = lax.div(b * part, group)
            query = qall[pl.ds(b * part, part)].reshape(rows, dim)
            score = lax.dot_general(query, kext[g], contract, preferred_element_type=jnp.float32)
            cached = score[:, :span] + bias[...]
            tree = score[:, span:] + jnp.concatenate([tree_bias[...]] * part, 0)
            top = jnp.maximum(jnp.max(cached, 1, keepdims=True), jnp.max(tree, 1, keepdims=True))
            top = jnp.maximum(top, 0.5 * NEG)
            prob = jnp.concatenate(
                [
                    jnp.exp2((cached - top) * factor).astype(jnp.bfloat16),
                    jnp.exp2((tree - top) * factor).astype(jnp.bfloat16),
                ],
                1,
            )
            out = jnp.dot(prob, vext[g], preferred_element_type=jnp.float32)
            for j in range(part):
                here = slice(j * tokens, (j + 1) * tokens)
                own_stat[s, j : j + 1, :] = as_row(top[here])
                own_stat[s, part + j : part + j + 1, :] = as_row(out[here, dim:])

            @pl.when(is_end)
            def _():
                end_out[s] = out[:, :dim].astype(jnp.bfloat16)
                for copy in end_copy(s):
                    copy.start()

            @pl.when(is_mid)
            def _():
                own_acc[s] = out[:, :dim]

        def join(s):
            for copy in end_copy(s):
                copy.wait_recv()
            a, b = own_stat[s, :part, :], stat_in[s, :part, :]
            top = jnp.maximum(a, b)
            fa, fb = jnp.exp2((a - top) * factor), jnp.exp2((b - top) * factor)
            mstat_out[s, :part, :] = top
            mstat_out[s, part:, :] = own_stat[s, part:, :] * fa + stat_in[s, part:, :] * fb
            for j in range(part):
                here = slice(j * tokens, (j + 1) * tokens)
                value = own_acc[s, here, :] * as_column(fa[j : j + 1])
                value = value + end_in[s, here, :].astype(jnp.float32) * as_column(fb[j : j + 1])
                own_acc[s, here, :] = value
                mid_out[s, here, :] = value.astype(jnp.bfloat16)
            for copy in mid_copy(s):
                copy.start()

        def project_out(s):
            b = block_of(s)
            value = jnp.concatenate([attn[b * part + j] for j in range(part)], 1)
            weight = wo[pl.ds(pl.multiple_of(b * part * dim, part * dim), part * dim), :]
            total[...] += jnp.dot(value, weight, preferred_element_type=jnp.float32)

        def settle(s):
            for copy in mid_copy(s):
                copy.wait_recv()
            a, b = mstat_out[s, :part, :], mstat_in[s, :part, :]
            top = jnp.maximum(a, b)
            fa, fb = jnp.exp2((a - top) * factor), jnp.exp2((b - top) * factor)
            denom = mstat_out[s, part:, :] * fa + mstat_in[s, part:, :] * fb
            fa, fb = fa / denom, fb / denom
            for j in range(part):
                here = slice(j * tokens, (j + 1) * tokens)
                value = own_acc[s, here, :] * as_column(fa[j : j + 1])
                value = value + mid_in[s, here, :].astype(jnp.float32) * as_column(fb[j : j + 1])
                attn[block_of(s) * part + j] = value.astype(jnp.bfloat16)
            final_copy(s).start()
            project_out(s)

        for g in range(kv_heads):
            load_k(g).wait()
            load_v(g).wait()

        def step(t, carry):
            @pl.when(t < steps)
            def _():
                attend(t)

            k = chunks + first_relay - 1 - t

            @pl.when(jnp.logical_and(relay, jnp.logical_and(k >= 0, k < chunks)))
            def _():
                q_copy(k, 0, 0).wait_recv()
                relay_copy(k).start()

            @pl.when(t == 2)
            def _():
                load_o.wait()

            @pl.when(jnp.logical_and(is_mid, jnp.logical_and(t >= lag, t < steps + lag)))
            def _():
                join(t - lag)

            @pl.when(jnp.logical_and(is_mid, jnp.logical_and(t >= 2 * lag, t < steps + 2 * lag)))
            def _():
                settle(t - 2 * lag)

            @pl.when(jnp.logical_and(is_end, t >= 3 * lag))
            def _():
                final_copy(t - 3 * lag).wait_recv()
                project_out(t - 3 * lag)

            return carry

        lax.fori_loop(0, steps + 3 * lag, step, 0)
        h_all[row] = total[...].astype(jnp.bfloat16)

        pair = row + 1 - 2 * lax.rem(row, 2)

        def block_from(start, d):
            return lax.rem(start + rows_gx - d, rows_gx)

        def h_copy(d):
            place = h_all.at[row]
            return send(place, place, h_s.at[d], h_r.at[d], "gx", lax.rem(row + d, rows_gx))

        def pair_copy(d):
            place = h_all.at[block_from(row, d)]
            return send(place, place, h_s.at[d + 1], h_r.at[d + 1], "gx", pair)

        for d in range(2, rows_gx, 2):
            h_copy(d).start()
        pair_copy(0).start()

        @pl.when(is_last)
        def _():
            for d in range(last):
                akv_copy(d, d).wait_send()

        @pl.when(jnp.logical_not(is_last))
        def _():
            akv_copy(0, last).wait_recv()

        akv_ref[...] = akv[0:accepted, :]

        def sent(c, carry):
            k = me * chunks + c
            for peer in range(count):

                @pl.when(direct(k, peer))
                def _():
                    q_copy(k, c, peer).wait_send()

            return carry

        def relayed(k, carry):
            @pl.when(relay)
            def _():
                relay_copy(k).wait_send()

            return carry

        def done(s, carry):
            @pl.when(is_end)
            def _():
                for copy in end_copy(s):
                    copy.wait_send()

            @pl.when(is_mid)
            def _():
                for copy in mid_copy(s):
                    copy.wait_send()
                final_copy(s).wait_send()

            return carry

        gain = fg_ref[...].reshape(1, cols).astype(jnp.float32)

        def scale(source):
            scaled[source] = (h_all[source].astype(jnp.float32) * gain).astype(jnp.bfloat16)

        scale(row)
        for d in range(2, rows_gx, 2):
            h_copy(d).wait_recv()
            pair_copy(d).start()
            scale(block_from(row, d))
        for d in range(0, rows_gx, 2):
            pair_copy(d).wait_recv()
            scale(block_from(pair, d))
        square_of = lax.broadcasted_iota(jnp.int32, (lane, lane), 0) == lax.broadcasted_iota(
            jnp.int32, (lane, lane), 1
        )

        def multiply(h, s):
            e = h * split + s
            load_in(e).wait()
            value = jnp.dot(
                jnp.concatenate([pick[0, e], pick[1, e]], 0),
                scaled[...].reshape(everyone, cols),
                preferred_element_type=jnp.float32,
            ).astype(jnp.bfloat16)
            value = jnp.dot(value, wbuf[e], preferred_element_type=jnp.float32)
            for j in range(sub):
                c = j // turn_sub * turn_strips + s * turn_sub + j % turn_sub
                part_sum[h, c] = value[j * grain : (j + 1) * grain].astype(jnp.bfloat16)

        prev = lax.rem(me + count - 1, count)
        nxt = lax.rem(me + 1, count)
        at_low = me == 0
        at_high = is_last

        def rs_copy(h, c):
            return send(
                part_sum.at[h, c], rbuf.at[h, c], rs_s.at[h, c], rs_r.at[h, c], "gy",
                jnp.where(h == 1, nxt, prev),
            )

        first_h = jnp.where(low, 1, 0)
        multiply(first_h, 0)

        @pl.when(is_end)
        def _():
            for c in range(turn_sub):
                rs_copy(first_h, c).start()

        multiply(1 - first_h, 0)
        sq_out[...] = jnp.zeros(sq_out.shape, jnp.float32)
        for i in range(everyone // lane):
            value = h_all[pl.ds(i * (lane // tokens), lane // tokens)].reshape(lane, cols)
            value = value.astype(jnp.float32)
            column = jnp.sum(value * value, 1, keepdims=True)
            line = jnp.sum(jnp.where(square_of, column, 0.0), 0, keepdims=True)
            sq_out[0:1, i * lane : (i + 1) * lane] = line

        def sq_copy(d):
            return send(
                sq_out, sq_in.at[d], sq_s.at[d], sq_r.at[d], "gy", lax.rem(me + d, count)
            )

        for d in range(1, count):
            sq_copy(d).start()

        def finish_squares():
            whole = sq_out[0:1, :]
            for d in range(1, count):
                sq_copy(d).wait()
                whole = whole + sq_in[d, 0:1, :]
            inv_row[...] = lax.rsqrt(whole / model + EPS)

        def hid_copy(h, c):
            return send(
                hid.at[h, c], hid.at[h, c], hid_s.at[h, c], hid_r.at[h, c], "gy",
                prev if h else nxt,
            )

        def straight_copy(h, c, d):
            peer = lax.rem(me + (count - d if h else d), count)
            return send(
                hid.at[h, c], hid.at[h, c], st_s.at[h, c - chained, d], hid_r.at[h, c], "gy", peer
            )

        def ends(h):
            return (at_low, at_high) if h else (at_high, at_low)

        def reduce_strip(h, c):
            first, final = ends(h)

            @pl.when(jnp.logical_not(first))
            def _():
                rs_copy(h, c).wait_recv()

            @pl.when(jnp.logical_not(jnp.logical_or(first, final)))
            def _():
                part_sum[h, c] = (
                    part_sum[h, c].astype(jnp.float32) + rbuf[h, c].astype(jnp.float32)
                ).astype(jnp.bfloat16)

            begun = jnp.logical_and(first, c < turn_sub)

            @pl.when(jnp.logical_not(jnp.logical_or(final, begun)))
            def _():
                rs_copy(h, c).start()

            @pl.when(final)
            def _():
                turn = lax.div(c, turn_strips)
                e = h * split + lax.div(lax.rem(c, turn_strips), turn_sub)
                at = pl.multiple_of(lax.rem(c, turn_sub) * grain, grain)
                chosen = pick[turn, e, pl.ds(at, grain), :].astype(jnp.float32)
                inverse = jnp.sum(chosen * inv_row[...], 1, keepdims=True)
                summed = part_sum[h, c].astype(jnp.float32) + rbuf[h, c].astype(jnp.float32)
                gate = summed[:, :units] * inverse
                up = summed[:, units:] * inverse
                hid[h, c] = (gate / (1.0 + jnp.exp(-gate)) * up).astype(jnp.bfloat16)

                @pl.when(c < chained)
                def _():
                    hid_copy(h, c).start()

                @pl.when(c >= chained)
                def _():
                    for d in range(last, 0, -1):
                        straight_copy(h, c, d).start()

        def return_strip(h, c):
            first, final = ends(h)

            @pl.when(jnp.logical_not(final))
            def _():
                hid_copy(h, c).wait_recv()

            passed = jnp.logical_not(jnp.logical_or(first, final))

            @pl.when(jnp.logical_and(passed, c < chained))
            def _():
                hid_copy(h, c).start()

        def project_down(h, b):
            turn = lax.div(b, turn_strips)
            e = h * split + lax.div(lax.rem(b, turn_strips), turn_sub)

            @pl.when(turn == 0)
            def _():
                load_down(e).wait()

            value = hid[h, pl.ds(b + 1 - turn_sub, turn_sub)].reshape(turn_slots, units)
            value = jnp.dot(value, dbuf[e], preferred_element_type=jnp.float32)
            obuf[turn, e] = (value * wcol[turn, e, :, 0:1]).astype(jnp.bfloat16)

        def back_copy(d):
            peer = lax.rem(row + d, rows_gx)
            return send(pbuf.at[peer], ret.at[d], g_s.at[d], g_r.at[d], "gx", peer)

        def send_back(turn):
            summed = lax.dot_general(
                pick[turn].reshape(experts * turn_slots, everyone),
                obuf[turn].reshape(experts * turn_slots, cols),
                (((0,), (0,)), ((), ())),
                preferred_element_type=jnp.float32,
            )
            for p in range(turn, rows_gx, 2):
                pbuf[p] = summed[p * tokens : (p + 1) * tokens].astype(jnp.bfloat16)
            for d in range(1, rows_gx):

                @pl.when(lax.rem(row + d, 2) == turn)
                def _():
                    back_copy(d).start()

        home = turn_strips - 1 + 2 * far - hop * jnp.minimum(me, last - me)

        def moe_step(t, carry):
            for h, place in ((1, turn_sub // 2), (0, turn_sub - 1)):

                ready = jnp.logical_and(t < turn_strips - turn_sub, lax.rem(t, turn_sub) == place)

                @pl.when(ready)
                def _():
                    multiply(h, lax.div(t, turn_sub) + 1)

            @pl.when(t == far - 1)
            def _():
                finish_squares()

            for h in (1, 0):
                way = hop * (me if h else last - me)
                c = t - way

                @pl.when(jnp.logical_and(c >= 0, c < strips))
                def _():
                    reduce_strip(h, c)

            for h in (1, 0):
                way = hop * (me if h else last - me)
                b = t - 2 * far + way

                @pl.when(jnp.logical_and(b >= 0, b < strips))
                def _():
                    return_strip(h, b)

                    @pl.when(lax.rem(b, turn_sub) == turn_sub - 1)
                    def _():
                        project_down(h, b)

            @pl.when(t == home)
            def _():
                send_back(0)

            return carry

        lax.fori_loop(0, strips + 2 * far, moe_step, 0)

        def finish(c, carry):
            for h in (1, 0):
                first, final = ends(h)

                @pl.when(jnp.logical_not(final))
                def _():
                    rs_copy(h, c).wait_send()

                @pl.when(jnp.logical_and(jnp.logical_not(first), c < chained))
                def _():
                    hid_copy(h, c).wait_send()

                @pl.when(jnp.logical_and(final, c >= chained))
                def _():
                    for d in range(1, count):
                        straight_copy(h, c, d).wait_send()

            return carry

        send_back(1)
        moe = pbuf[row].astype(jnp.float32)
        lax.fori_loop(0, chunks, sent, 0)
        lax.fori_loop(0, chunks, relayed, 0)
        lax.fori_loop(0, steps, done, 0)
        lax.fori_loop(0, strips, finish, 0)
        for d in range(0, rows_gx, 2):
            pair_copy(d).wait_send()
            if d:
                h_copy(d).wait_send()
        for d in range(1, rows_gx):
            back_copy(d).wait_recv()
            moe = moe + ret[d].astype(jnp.float32)
        out_ref[...] = (h_all[row].astype(jnp.float32) + moe).astype(jnp.bfloat16)
        for d in range(1, rows_gx):
            back_copy(d).wait_send()

    pad = -accepted % 16
    vmem = pl.BlockSpec(memory_space=pltpu.VMEM)
    hbm = pl.BlockSpec(memory_space=pl.ANY)
    dma = pltpu.SemaphoreType.DMA
    stat = pltpu.VMEM((steps, 2 * part, lane), jnp.float32)
    piece = pltpu.VMEM((steps, rows, dim), jnp.bfloat16)
    return pl.pallas_call(
        kernel,
        out_shape=[
            jax.ShapeDtypeStruct((tokens, cols), jnp.bfloat16),
            jax.ShapeDtypeStruct((accepted, 2 * kv_cols), jnp.bfloat16),
        ],
        in_specs=[pl.BlockSpec(memory_space=pltpu.SMEM)] + [vmem] * 9 + [hbm] * 6,
        out_specs=[vmem, vmem],
        scratch_shapes=[
            pltpu.VMEM((tokens, model), jnp.bfloat16),
            pltpu.VMEM((chunks, model, 2 * dim), jnp.bfloat16),
            pltpu.VMEM((own * count, tokens, dim), jnp.bfloat16),
            pltpu.VMEM((kv_heads, span + lane, dim), jnp.bfloat16),
            pltpu.VMEM((kv_heads, span + lane, 2 * dim), jnp.bfloat16),
            pltpu.VMEM(w_o.shape, jnp.bfloat16),
            pltpu.VMEM((1, span), jnp.float32),
            pltpu.VMEM((tokens, lane), jnp.float32),
            pltpu.VMEM((steps, rows, dim), jnp.float32),
            stat,
            piece,
            piece,
            stat,
            piece,
            piece,
            stat,
            stat,
            pltpu.VMEM((heads, tokens, dim), jnp.bfloat16),
            pltpu.VMEM((tokens, cols), jnp.float32),
            pltpu.VMEM((accepted + pad, 2 * kv_cols), jnp.bfloat16),
            dma((chunks,)),
            dma((kv_heads,)),
            dma((kv_heads,)),
            dma,
            dma((count, 2 * chunks)),
            dma((count * chunks,)),
        ]
        + [dma((steps,))] * 10
        + [dma((last,)), dma, dma((rows_gx,)), dma((rows_gx,))]
        + [
            pltpu.VMEM((rows_gx, tokens, cols), jnp.bfloat16),
            pltpu.VMEM((rows_gx, tokens, cols), jnp.bfloat16),
            pltpu.VMEM((2, experts, turn_slots, everyone), jnp.bfloat16),
            pltpu.VMEM((2, experts, turn_slots, lane), jnp.float32),
            pltpu.VMEM((8, everyone), jnp.float32),
            pltpu.VMEM((count, 8, everyone), jnp.float32),
            pltpu.VMEM((1, everyone), jnp.float32),
            pltpu.VMEM((2, strips, grain, units), jnp.bfloat16),
            pltpu.VMEM((experts, depth, wide), jnp.bfloat16),
            pltpu.VMEM((experts, units, cols), jnp.bfloat16),
            pltpu.VMEM((2, strips, grain, wide), jnp.bfloat16),
            pltpu.VMEM((2, strips, grain, wide), jnp.bfloat16),
            pltpu.VMEM((2, experts, turn_slots, cols), jnp.bfloat16),
            pltpu.VMEM((rows_gx, tokens, cols), jnp.bfloat16),
            pltpu.VMEM((rows_gx, tokens, cols), jnp.bfloat16),
            dma((experts,)),
            dma((experts,)),
            dma((count,)),
            dma((count,)),
            dma((2, strips)),
            dma((2, strips)),
            dma((2, strips)),
            dma((2, strips)),
            dma((2, straight, count)),
            dma((rows_gx,)),
            dma((rows_gx,)),
        ],
        compiler_params=pltpu.CompilerParams(
            collective_id=cid, has_side_effects=True, vmem_limit_bytes=62 * 1024 * 1024
        ),
        name="layer_line",
    )(
        cache_len, states, attn_gain, q_gain, k_gain, tree_mask,
        accept, ffn_gain, routing, route_weight, w_qkv, cache_k, cache_v, w_o, w_in, w_down,
    )


def hand_over(first, second):
    def kernel(a_ref, b_ref, c_ref, d_ref):
        c_ref[...] = a_ref[...]
        d_ref[...] = b_ref[...]

    vmem = pl.BlockSpec(memory_space=pltpu.VMEM)
    return pl.pallas_call(
        kernel,
        out_shape=[
            jax.ShapeDtypeStruct(first.shape, first.dtype),
            jax.ShapeDtypeStruct(second.shape, second.dtype),
        ],
        in_specs=[vmem, vmem],
        out_specs=[vmem, vmem],
        name="hand_over",
    )(first, second)


def rms_scale(values, gain):
    return values * lax.rsqrt(jnp.mean(values * values, -1, keepdims=True) + EPS) * gain


def angles_of(position, dim):
    freqs = jnp.exp(jnp.arange(dim // 2, dtype=jnp.float32) * (-2.0 * THETA_LOG / dim))
    angles = position.astype(jnp.float32)[..., None] * freqs
    cosine = jnp.cos(angles)
    sine = jnp.sin(angles)
    return jnp.concatenate([cosine, cosine], -1), jnp.concatenate([-sine, sine], -1)


def body(
    states,
    attn_gain,
    w_qkv,
    q_gain,
    k_gain,
    cache_k,
    cache_v,
    cache_len,
    tree_mask,
    w_o,
    ffn_gain,
    routing,
    route_weight,
    w_in,
    w_down,
    accept,
):
    tok_rows, model_width = states.shape
    head_dim = q_gain.shape[0]
    kv_cols = cache_k.shape[2]
    heads_all = w_o.shape[0] // head_dim
    cache_span = cache_k.shape[1]
    cols_here = w_o.shape[1]
    col_index = lax.axis_index("gy")
    row_index = lax.axis_index("gx")
    count_gx = lax.axis_size("gx")
    count_gy = lax.axis_size("gy")
    own_heads = w_qkv.shape[1] // head_dim
    kv_heads = kv_cols // head_dim
    on_line = (
        count_gy == 4
        and w_qkv.shape[1] % (2 * head_dim) == 0
        and own_heads >= 2 * kv_heads
        and (own_heads - 2 * kv_heads) % 2 == 0
        and heads_all % (4 * kv_heads) == 0
        and tok_rows % 16 == 0
        and 128 % tok_rows == 0
        and routing.shape[0] % 128 == 0
        and w_in.shape[1] == w_o.shape[1]
        and (3 * routing.shape[0] * routing.shape[1] // (2 * w_in.shape[0] * lax.axis_size("gx"))) % 32 == 0
        and lax.axis_size("gx") % 2 == 0
    )
    if on_line:
        layer_out, accepted_kv = layer_line(
            states,
            attn_gain,
            w_qkv,
            q_gain[None],
            k_gain[None],
            cache_k[0],
            cache_v[0],
            cache_len,
            tree_mask[0],
            w_o,
            accept[0],
            ffn_gain,
            routing.T,
            route_weight.T,
            w_in,
            w_down,
            0,
        )
        layer_out, accepted_kv = hand_over(layer_out, accepted_kv)
        return (layer_out, accepted_kv[None])
    normed = rms_scale(states.astype(jnp.float32), attn_gain.astype(jnp.float32)).astype(
        jnp.bfloat16
    )
    qkv_part = jnp.dot(normed, w_qkv, preferred_element_type=jnp.float32).astype(jnp.bfloat16)
    (qkv_blocks,) = exchange([qkv_part], "gy", False, 0)
    qkv_whole = jnp.swapaxes(qkv_blocks, 0, 1).reshape(tok_rows, -1)
    q_cols = heads_all * head_dim
    depth = jnp.sum(tree_mask, -1) - 1
    cosine, sine = angles_of((cache_len[:, None] + depth)[0], head_dim)
    states_here = lax.dynamic_slice_in_dim(states, col_index * cols_here, cols_here, 1)
    gathered, k_rot = attention_block(
        qkv_whole,
        q_gain[None],
        k_gain[None],
        cosine,
        sine,
        cache_k[0],
        cache_v[0],
        cache_len - col_index * cache_span,
        tree_mask[0],
        states_here,
        w_o,
        1,
    )
    kv_new = jnp.concatenate([k_rot, qkv_whole[:, q_cols + kv_cols :]], -1)[None]
    accepted_kv = jnp.einsum(
        "rat,rtc->rac", accept.astype(jnp.bfloat16), kv_new, preferred_element_type=jnp.float32
    ).astype(jnp.bfloat16)
    resid = lax.dynamic_index_in_dim(gathered, row_index, 0, False)
    exp_here = w_in.shape[0]
    expert_count = exp_here * count_gx
    top_k = routing.shape[1]
    most_rows = 3 * tok_rows * top_k // (2 * expert_count)
    hidden_units = w_down.shape[1]
    gain_float = ffn_gain.astype(jnp.float32)
    tokens = routing.shape[0]
    slots = count_gx * most_rows
    own_experts = row_index * exp_here + jnp.arange(exp_here, dtype=jnp.int32)
    matched = routing[:, None, :] == own_experts[None, :, None]
    hits = jnp.any(matched, -1)
    weights = jnp.sum(jnp.where(matched, route_weight[:, None, :], 0.0), -1)
    order = jnp.arange(tok_rows, dtype=jnp.int32)
    earlier = (order[:, None] > order[None, :]).astype(jnp.bfloat16)
    rank = jnp.einsum(
        "tu,bue->bte",
        earlier,
        hits.astype(jnp.bfloat16).reshape(count_gx, tok_rows, exp_here),
        preferred_element_type=jnp.float32,
    ).astype(jnp.int32)
    first_slot = jnp.arange(count_gx, dtype=jnp.int32)[:, None, None] * most_rows
    slot_of = jnp.where(hits, (rank + first_slot).reshape(tokens, exp_here), -1)
    pick = slot_of.T[:, None, :] == jnp.arange(slots, dtype=jnp.int32)[None, :, None]
    pick_matrix = pick.astype(jnp.bfloat16)
    slot_weight = jnp.sum(jnp.where(pick, weights.T[:, None, :], 0.0), -1)
    gathered = gathered.reshape(tokens, cols_here).astype(jnp.float32)
    token_squares = jnp.sum(gathered * gathered, -1)
    slot_squares = jnp.sum(jnp.where(pick, token_squares, 0.0), -1)
    piece = 16
    slot_squares = jnp.pad(slot_squares.reshape(-1, piece), ((0, 0), (0, 128 - piece)))
    scaled = (gathered * gain_float).astype(jnp.bfloat16)
    rows = jnp.einsum(
        "est,td->esd", pick_matrix, scaled, preferred_element_type=jnp.float32
    ).astype(jnp.bfloat16)
    layer_out = expert_layer(
        rows,
        slot_squares,
        w_in,
        w_down,
        slot_weight[..., None],
        pick_matrix.reshape(exp_here * slots, tokens),
        resid,
        model_width,
        4,
    )
    return (layer_out, accepted_kv)


def solution(mesh):
    in_specs = (
        P("gx", None),
        P(),
        P(None, "gy"),
        P(),
        P(),
        P("gx", "gy", None),
        P("gx", "gy", None),
        P("gx"),
        P("gx", None, None),
        P(None, "gy"),
        P("gy"),
        P(),
        P(),
        P("gx", "gy", None),
        P("gx", None, "gy"),
        P("gx", None, None),
    )
    out_specs = (P("gx", "gy"), P("gx", None, None))
    return jax.shard_map(body, mesh=mesh, in_specs=in_specs, out_specs=out_specs, check_vma=False)
```

```python
import math

import jax
import jax.numpy as jnp
from jax import lax
from jax.experimental import pallas as pl
from jax.experimental.pallas import tpu as pltpu
from jax.sharding import PartitionSpec as P

EPS = 1e-06
NEG = -1e30
THETA_LOG = math.log(1000000.0)


MESH = pl.DeviceIdType.MESH


def exchange(arrays, axis, scatter, cid):
    count = lax.axis_size(axis)
    number = len(arrays)

    def kernel(*refs):
        ins, outs = refs[:number], refs[number : 2 * number]
        send, recv, local = refs[2 * number :]
        me = lax.axis_index(axis)
        barrier = pltpu.get_barrier_semaphore()
        for d in range(1, count):
            pl.semaphore_signal(
                barrier, inc=1, device_id={axis: lax.rem(me + d, count)}, device_id_type=MESH
            )
        pl.semaphore_wait(barrier, count - 1)
        copies = []
        for d in range(1, count):
            peer = lax.rem(me + d, count)
            for i in range(number):
                copy = pltpu.make_async_remote_copy(
                    src_ref=ins[i].at[peer] if scatter else ins[i],
                    dst_ref=outs[i].at[me],
                    send_sem=send.at[i, d],
                    recv_sem=recv.at[i, d],
                    device_id={axis: peer},
                    device_id_type=MESH,
                )
                copy.start()
                copies.append(copy)
        own = []
        for i in range(number):
            copy = pltpu.make_async_copy(
                ins[i].at[me] if scatter else ins[i], outs[i].at[me], local.at[i]
            )
            copy.start()
            own.append(copy)
        for copy in own + copies:
            copy.wait()

    outs = [
        jax.ShapeDtypeStruct(x.shape if scatter else (count,) + x.shape, x.dtype) for x in arrays
    ]
    return pl.pallas_call(
        kernel,
        out_shape=outs,
        in_specs=[pl.BlockSpec(memory_space=pltpu.VMEM)] * number,
        out_specs=[pl.BlockSpec(memory_space=pltpu.VMEM)] * number,
        scratch_shapes=[
            pltpu.SemaphoreType.DMA((number, count)),
            pltpu.SemaphoreType.DMA((number, count)),
            pltpu.SemaphoreType.DMA((number,)),
        ],
        compiler_params=pltpu.CompilerParams(collective_id=cid, has_side_effects=True),
        name="exchange_%d" % cid,
    )(*arrays)


def expert_layer(rows, squares, w_in, w_down, slot_weight, pick_back, resid, model_width, cid):
    axis = "gy"
    count = lax.axis_size(axis)
    peers = lax.axis_size("gx")
    experts, slots, depth = rows.shape
    tokens, cols = resid.shape
    wide = w_in.shape[2]
    units = wide // 2
    half = experts // 2
    piece = 16
    sub = slots // piece
    chunks = half * sub
    hop = 2
    far = hop * (count - 1)

    def kernel(
        x_ref, sq_ref, weight_ref, pick_ref, resid_ref, w_hbm, d_hbm, out_ref,
        hid_ref, wbuf, dbuf, part, rbuf, sqbuf, inv_ref, obuf, pbuf, ret,
        wsem, dsem, rs_s, rs_r, h_s, h_r, sq_s, sq_r, g_s, g_r,
    ):
        me = lax.axis_index(axis)
        prev = lax.rem(me + count - 1, count)
        nxt = lax.rem(me + 1, count)
        at_low = me == 0
        at_high = me == count - 1

        def load(e):
            return pltpu.make_async_copy(w_hbm.at[e], wbuf.at[e], wsem.at[e])

        def load_down(e):
            return pltpu.make_async_copy(d_hbm.at[e], dbuf.at[e], dsem.at[e])

        row = lax.axis_index("gx")
        for s in range(half):
            load(half + s).start()
            load(s).start()
        for s in range(half):
            load_down(half + s).start()
            load_down(s).start()
        barrier = pltpu.get_barrier_semaphore()
        for d in range(1, count):
            pl.semaphore_signal(
                barrier, inc=1, device_id={axis: lax.rem(me + d, count)}, device_id_type=MESH
            )
        for d in range(1, peers):
            pl.semaphore_signal(
                barrier, inc=1, device_id={"gx": lax.rem(row + d, peers)}, device_id_type=MESH
            )

        def multiply(h, s):
            e = h * half + s
            load(e).wait()
            value = jnp.dot(x_ref[e], wbuf[e], preferred_element_type=jnp.float32)
            for j in range(sub):
                part[h, s * sub + j] = value[j * piece : (j + 1) * piece].astype(jnp.bfloat16)

        multiply(1, 0)
        multiply(0, 0)
        pl.semaphore_wait(barrier, count + peers - 2)

        def sq_copy(d):
            return pltpu.make_async_remote_copy(
                src_ref=sq_ref,
                dst_ref=sqbuf.at[d],
                send_sem=sq_s.at[d],
                recv_sem=sq_r.at[d],
                device_id={axis: lax.rem(me + d, count)},
                device_id_type=MESH,
            )

        for d in range(1, count):
            sq_copy(d).start()

        def finish_squares():
            total = sq_ref[...]
            for d in range(1, count):
                sq_copy(d).wait()
                total = total + sqbuf[d]
            inv_ref[...] = lax.rsqrt(total / model_width + EPS)

        diagonal = lax.broadcasted_iota(jnp.int32, (piece, 128), 0) == lax.broadcasted_iota(
            jnp.int32, (piece, 128), 1
        )

        def rs_copy(h, c):
            return pltpu.make_async_remote_copy(
                src_ref=part.at[h, c],
                dst_ref=rbuf.at[h, c],
                send_sem=rs_s.at[h, c],
                recv_sem=rs_r.at[h, c],
                device_id={axis: nxt if h else prev},
                device_id_type=MESH,
            )

        def hid_copy(h, c):
            return pltpu.make_async_remote_copy(
                src_ref=hid_ref.at[h, c],
                dst_ref=hid_ref.at[h, c],
                send_sem=h_s.at[h, c],
                recv_sem=h_r.at[h, c],
                device_id={axis: prev if h else nxt},
                device_id_type=MESH,
            )

        def ends(h):
            return (at_low, at_high) if h else (at_high, at_low)

        def reduce_chunk(h, c):
            first, last = ends(h)

            @pl.when(jnp.logical_not(first))
            def _():
                rs_copy(h, c).wait_recv()

            @pl.when(jnp.logical_not(jnp.logical_or(first, last)))
            def _():
                part[h, c] = (
                    part[h, c].astype(jnp.float32) + rbuf[h, c].astype(jnp.float32)
                ).astype(jnp.bfloat16)

            @pl.when(jnp.logical_not(last))
            def _():
                rs_copy(h, c).start()

            @pl.when(last)
            def _():
                row = inv_ref[pl.ds(h * chunks + c, 1), :]
                inverse = jnp.sum(jnp.where(diagonal, row, 0.0), 1, keepdims=True)
                summed = part[h, c].astype(jnp.float32) + rbuf[h, c].astype(jnp.float32)
                gate = summed[:, :units] * inverse
                up = summed[:, units:] * inverse
                hid_ref[h, c] = (gate / (1.0 + jnp.exp(-gate)) * up).astype(jnp.bfloat16)
                hid_copy(h, c).start()

        def return_chunk(h, c):
            first, last = ends(h)

            @pl.when(jnp.logical_not(last))
            def _():
                hid_copy(h, c).wait_recv()

            @pl.when(jnp.logical_not(jnp.logical_or(first, last)))
            def _():
                hid_copy(h, c).start()

        def project(h, s):
            e = h * half + s
            load_down(e).wait()
            value = hid_ref[h, pl.ds(s * sub, sub)].reshape(slots, units)
            value = jnp.dot(value, dbuf[e], preferred_element_type=jnp.float32)
            obuf[e] = (value * weight_ref[e]).astype(jnp.bfloat16)

        def step(t, carry):
            for h, place in ((1, 1), (0, sub // 2 + 1)):

                @pl.when(jnp.logical_and(t < chunks - sub, lax.rem(t, sub) == place))
                def _():
                    multiply(h, lax.div(t, sub) + 1)

            @pl.when(t == far - 1)
            def _():
                finish_squares()

            for h in (1, 0):
                way = hop * (me if h else count - 1 - me)
                c = t - way

                @pl.when(jnp.logical_and(c >= 0, c < chunks))
                def _():
                    reduce_chunk(h, c)

            for h in (1, 0):
                way = hop * (me if h else count - 1 - me)
                b = t - 2 * far + way

                @pl.when(jnp.logical_and(b >= 0, b < chunks))
                def _():
                    return_chunk(h, b)

                    @pl.when(lax.rem(b, sub) == sub - 1)
                    def _():
                        project(h, lax.div(b, sub))

            return carry

        lax.fori_loop(0, chunks + 2 * far, step, 0)

        def finish(c, carry):
            for h in (1, 0):
                first, last = ends(h)

                @pl.when(jnp.logical_not(last))
                def _():
                    rs_copy(h, c).wait_send()

                @pl.when(jnp.logical_not(first))
                def _():
                    hid_copy(h, c).wait_send()

            return carry

        summed = lax.dot_general(
            pick_ref[...],
            obuf[...].reshape(experts * slots, cols),
            (((0,), (0,)), ((), ())),
            preferred_element_type=jnp.float32,
        )
        for p in range(peers):
            pbuf[p] = summed[p * tokens : (p + 1) * tokens].astype(jnp.bfloat16)

        def back_copy(d):
            peer = lax.rem(row + d, peers)
            return pltpu.make_async_remote_copy(
                src_ref=pbuf.at[peer],
                dst_ref=ret.at[d],
                send_sem=g_s.at[d],
                recv_sem=g_r.at[d],
                device_id={"gx": peer},
                device_id_type=MESH,
            )

        for d in range(1, peers):
            back_copy(d).start()
        moe = pbuf[row].astype(jnp.float32)
        lax.fori_loop(0, chunks, finish, 0)
        for d in range(1, peers):
            back_copy(d).wait_recv()
            moe = moe + ret[d].astype(jnp.float32)
        out_ref[...] = (resid_ref[...].astype(jnp.float32) + moe).astype(jnp.bfloat16)
        for d in range(1, peers):
            back_copy(d).wait_send()

    vmem = pl.BlockSpec(memory_space=pltpu.VMEM)
    hbm = pl.BlockSpec(memory_space=pl.ANY)
    dma = pltpu.SemaphoreType.DMA
    return pl.pallas_call(
        kernel,
        out_shape=jax.ShapeDtypeStruct((tokens, cols), jnp.bfloat16),
        in_specs=[vmem] * 5 + [hbm, hbm],
        out_specs=vmem,
        scratch_shapes=[
            pltpu.VMEM((2, chunks, piece, units), jnp.bfloat16),
            pltpu.VMEM((experts, depth, wide), jnp.bfloat16),
            pltpu.VMEM((experts, units, cols), jnp.bfloat16),
            pltpu.VMEM((2, chunks, piece, wide), jnp.bfloat16),
            pltpu.VMEM((2, chunks, piece, wide), jnp.bfloat16),
            pltpu.VMEM((count, 2 * chunks, 128), jnp.float32),
            pltpu.VMEM((2 * chunks, 128), jnp.float32),
            pltpu.VMEM((experts, slots, cols), jnp.bfloat16),
            pltpu.VMEM((peers, tokens, cols), jnp.bfloat16),
            pltpu.VMEM((peers, tokens, cols), jnp.bfloat16),
            dma((experts,)),
            dma((experts,)),
            dma((2, chunks)),
            dma((2, chunks)),
            dma((2, chunks)),
            dma((2, chunks)),
            dma((count,)),
            dma((count,)),
            dma((peers,)),
            dma((peers,)),
        ],
        compiler_params=pltpu.CompilerParams(
            collective_id=cid, has_side_effects=True, vmem_limit_bytes=52 * 1024 * 1024
        ),
        name="expert_layer",
    )(rows, squares, slot_weight, pick_back, resid, w_in, w_down)


def attention_block(
    qkv, q_gain, k_gain, cosine, sine, cache_k, cache_v, limit, tree_mask, states_here, w_o, cid
):
    blocks = lax.axis_size("gy")
    rows_gx = lax.axis_size("gx")
    tokens = qkv.shape[0]
    span, kv_cols = cache_k.shape
    dim = q_gain.shape[1]
    kv_heads = kv_cols // dim
    heads = qkv.shape[1] // dim - 2 * kv_heads
    group = heads // kv_heads
    per_block = heads // blocks
    blocks_here = blocks // kv_heads
    width = per_block * dim
    cols = w_o.shape[1]
    scale = dim ** (-0.5)

    def kernel(
        limit_ref, q_ref, qg_ref, kg_ref, cos_ref, sin_ref, k_ref, v_ref, mask_ref, st_ref, wo_hbm,
        h_ref, rot_ref,
        acc_out, stat_out, acc_in, stat_in, attn, wo,
        wo_sem, a_s, a_r, s_s, s_r, t_s, t_r, h_s, h_r,
    ):
        me = lax.axis_index("gy")
        row = lax.axis_index("gx")
        load = pltpu.make_async_copy(wo_hbm, wo, wo_sem)
        load.start()
        barrier = pltpu.get_barrier_semaphore()
        for axis, here, count in (("gy", me, blocks), ("gx", row, rows_gx)):
            for d in range(1, count):
                pl.semaphore_signal(
                    barrier, inc=1, device_id={axis: lax.rem(here + d, count)}, device_id_type=MESH
                )
        pl.semaphore_wait(barrier, blocks + rows_gx - 2)

        def send(src, dst, send_sem, recv_sem, axis, peer):
            return pltpu.make_async_remote_copy(
                src_ref=src,
                dst_ref=dst,
                send_sem=send_sem,
                recv_sem=recv_sem,
                device_id={axis: peer},
                device_id_type=MESH,
            )

        def part_copies(block, source):
            return (
                send(acc_out.at[block], acc_in.at[source], a_s.at[block], a_r.at[source], "gy", block),
                send(stat_out.at[block], stat_in.at[source], s_s.at[block], s_r.at[source], "gy", block),
            )

        cos = cos_ref[...]
        sin = sin_ref[...]

        def turn(value, gain):
            value = value.astype(jnp.float32)
            value = value * lax.rsqrt(jnp.mean(value * value, -1, keepdims=True) + EPS) * gain
            return (value * cos + pltpu.roll(value, dim // 2, 1) * sin).astype(jnp.bfloat16)

        q_gain_row = qg_ref[...].astype(jnp.float32)
        k_gain_row = kg_ref[...].astype(jnp.float32)
        contract = (((1,), (1,)), ((), ()))
        diagonal = lax.broadcasted_iota(jnp.int32, (tokens, 128), 0) == lax.broadcasted_iota(
            jnp.int32, (tokens, 128), 1
        )

        def one_head(i, carry):
            g = lax.rem(lax.div(me, blocks_here) + 1 + i, kv_heads)

            def lanes(first, size):
                return pl.ds(pl.multiple_of(first, 128), size)

            query = jnp.concatenate(
                [
                    turn(q_ref[:, lanes((g * group + j) * dim, dim)], q_gain_row)
                    for j in range(group)
                ],
                0,
            )
            keys = turn(q_ref[:, lanes((heads + g) * dim, dim)], k_gain_row)
            values = q_ref[:, lanes((heads + kv_heads + g) * dim, dim)]
            rot_ref[:, lanes(g * dim, dim)] = keys
            tree = (
                lax.dot_general(query, keys, contract, preferred_element_type=jnp.float32) * scale
            )
            mask = jnp.concatenate([mask_ref[...]] * group, 0)
            tree_ok = jnp.logical_and(mask == 1, me == 0)
            tree = jnp.where(tree_ok, tree, NEG)
            score = (
                lax.dot_general(
                    query,
                    k_ref[:, lanes(g * dim, dim)],
                    contract,
                    preferred_element_type=jnp.float32,
                )
                * scale
            )
            valid = lax.broadcasted_iota(jnp.int32, score.shape, 1) < limit_ref[0]
            score = jnp.where(valid, score, NEG)
            top = jnp.maximum(jnp.max(score, 1, keepdims=True), jnp.max(tree, 1, keepdims=True))
            prob = jnp.where(valid, jnp.exp(score - top), 0.0).astype(jnp.bfloat16)
            prob_tree = jnp.where(tree_ok, jnp.exp(tree - top), 0.0).astype(jnp.bfloat16)
            total = jnp.sum(prob.astype(jnp.float32), 1, keepdims=True) + jnp.sum(
                prob_tree.astype(jnp.float32), 1, keepdims=True
            )
            acc = jnp.dot(prob, v_ref[:, lanes(g * dim, dim)], preferred_element_type=jnp.float32)
            acc = acc + jnp.dot(prob_tree, values, preferred_element_type=jnp.float32)
            acc = acc.astype(jnp.bfloat16)
            for b in range(blocks_here):
                block = g * blocks_here + b
                for place in range(per_block):
                    j = b * per_block + place
                    rows = slice(j * tokens, (j + 1) * tokens)
                    acc_out[block, :, place * dim : (place + 1) * dim] = acc[rows]
                    for k, column in enumerate((top, total)):
                        stat_out[block, k * per_block + place : k * per_block + place + 1, :] = (
                            jnp.sum(jnp.where(diagonal, column[rows], 0.0), 0, keepdims=True)
                        )

                @pl.when(block != me)
                def _():
                    for copy in part_copies(block, me):
                        copy.start()

            return carry

        lax.fori_loop(0, kv_heads, one_head, 0)

        acc_in[me] = acc_out[me]
        stat_in[me] = stat_out[me]
        for d in range(1, blocks):
            source = lax.rem(me + d, blocks)
            for copy in part_copies(source, source):
                copy.wait_recv()
        tops = [stat_in[j, :per_block, :] for j in range(blocks)]
        best = tops[0]
        for j in range(1, blocks):
            best = jnp.maximum(best, tops[j])
        factors = [jnp.exp(tops[j] - best) for j in range(blocks)]
        denom = stat_in[0, per_block:, :] * factors[0]
        for j in range(1, blocks):
            denom = denom + stat_in[j, per_block:, :] * factors[j]
        for place in range(per_block):
            joined = jnp.zeros((tokens, dim), jnp.float32)
            for j in range(blocks):
                line = (factors[j] / denom)[place : place + 1, :]
                column = jnp.sum(jnp.where(diagonal, line, 0.0), 1, keepdims=True)
                joined = joined + column * acc_in[
                    j, :, place * dim : (place + 1) * dim
                ].astype(jnp.float32)
            attn[me, :, place * dim : (place + 1) * dim] = joined.astype(jnp.bfloat16)

        def attn_copy(d, source):
            return send(
                attn.at[source], attn.at[source], t_s.at[d], t_r.at[d], "gy", lax.rem(me + d, blocks)
            )

        for d in range(1, blocks):
            attn_copy(d, me).start()
        load.wait()

        def project(source):
            return jnp.dot(
                attn[source],
                wo[pl.ds(pl.multiple_of(source * width, width), width), :],
                preferred_element_type=jnp.float32,
            )

        total = st_ref[...].astype(jnp.float32) + project(me)
        for d in range(1, blocks):
            source = lax.rem(me + blocks - d, blocks)
            attn_copy(d, source).wait_recv()
            total = total + project(source)
        h_ref[row] = total.astype(jnp.bfloat16)

        def h_copy(d, source):
            return send(
                h_ref.at[source], h_ref.at[source], h_s.at[d], h_r.at[d], "gx",
                lax.rem(row + d, rows_gx),
            )

        for d in range(1, rows_gx):
            h_copy(d, row).start()
        for d in range(1, blocks):
            block = lax.rem(me + d, blocks)
            for copy in part_copies(block, me):
                copy.wait_send()
            attn_copy(d, me).wait_send()
        for d in range(1, rows_gx):
            h_copy(d, lax.rem(row + rows_gx - d, rows_gx)).wait_recv()
            h_copy(d, row).wait_send()

    vmem = pl.BlockSpec(memory_space=pltpu.VMEM)
    dma = pltpu.SemaphoreType.DMA
    return pl.pallas_call(
        kernel,
        out_shape=[
            jax.ShapeDtypeStruct((rows_gx, tokens, cols), jnp.bfloat16),
            jax.ShapeDtypeStruct((tokens, kv_cols), jnp.bfloat16),
        ],
        in_specs=[pl.BlockSpec(memory_space=pltpu.SMEM)]
        + [vmem] * 9
        + [pl.BlockSpec(memory_space=pl.ANY)],
        out_specs=[vmem, vmem],
        scratch_shapes=[
            pltpu.VMEM((blocks, tokens, width), jnp.bfloat16),
            pltpu.VMEM((blocks, 2 * per_block, 128), jnp.float32),
            pltpu.VMEM((blocks, tokens, width), jnp.bfloat16),
            pltpu.VMEM((blocks, 2 * per_block, 128), jnp.float32),
            pltpu.VMEM((blocks, tokens, width), jnp.bfloat16),
            pltpu.VMEM(w_o.shape, jnp.bfloat16),
            dma,
            dma((blocks,)),
            dma((blocks,)),
            dma((blocks,)),
            dma((blocks,)),
            dma((blocks,)),
            dma((blocks,)),
            dma((rows_gx,)),
            dma((rows_gx,)),
        ],
        compiler_params=pltpu.CompilerParams(
            collective_id=cid, has_side_effects=True, vmem_limit_bytes=48 * 1024 * 1024
        ),
        name="attention_block",
    )(
        limit, qkv, q_gain, k_gain, cosine, sine, cache_k, cache_v, tree_mask, states_here, w_o
    )


def layer_line(
    states, attn_gain, w_qkv, q_gain, k_gain, cache_k, cache_v, cache_len, tree_mask, w_o, accept,
    ffn_gain, routing, route_weight, w_in, w_down, cid
):
    count = lax.axis_size("gy")
    rows_gx = lax.axis_size("gx")
    tokens, model = states.shape
    span, kv_cols = cache_k.shape
    dim = q_gain.shape[1]
    kv_heads = kv_cols // dim
    own = w_qkv.shape[1] // dim
    heads = own * count - 2 * kv_heads
    group = heads // kv_heads
    cols = w_o.shape[1]
    chunks = own // 2
    part = group // 2
    steps = heads // part
    first_relay = 2
    lag = 3
    rows = part * tokens
    lane = 128
    accepted = accept.shape[0]
    last = count - 1
    factor = dim ** (-0.5) / math.log(2.0)
    top_k, everyone = routing.shape
    experts, depth, wide = w_in.shape
    units = wide // 2
    most_rows = 3 * tokens * top_k // (2 * experts * rows_gx)
    slots = rows_gx * most_rows
    split = experts // 2
    grain = 16
    sub = slots // grain
    strips = split * sub
    turn_slots = slots // 2
    turn_sub = sub // 2
    turn_strips = strips // 2
    hop = 3
    far = hop * last
    straight = 4
    chained = strips - straight

    def kernel(
        len_ref, st_ref, ag_ref, qg_ref, kg_ref, mask_ref, acc_ref, fg_ref, rt_ref, rw_ref,
        wq_hbm, k_hbm, v_hbm, wo_hbm, w_hbm, d_hbm,
        out_ref, akv_ref,
        normed, wq, qall, kext, vext, wo, bias, tree_bias,
        own_acc, own_stat, end_out, end_in, stat_in, mid_out, mid_in, mstat_out, mstat_in,
        attn, total, akv,
        wq_sem, k_sem, v_sem, wo_sem, q_s, q_r, e_s, e_r, es_s, es_r, m_s, m_r, ms_s, ms_r,
        f_s, f_r, a_s, a_r, h_s, h_r,
        h_all, scaled, pick, wcol, sq_out, sq_in, inv_row, hid, wbuf, dbuf, part_sum, rbuf, obuf, pbuf, ret,
        w_sem, d_sem, sq_s, sq_r, rs_s, rs_r, hid_s, hid_r, st_s, g_s, g_r,
    ):
        me = lax.axis_index("gy")
        row = lax.axis_index("gx")
        is_last = me == last
        is_end = jnp.logical_or(me == 0, is_last)
        is_mid = jnp.logical_not(is_end)
        low = me < 2
        mid_of = jnp.where(low, 1, 2)
        end_of = jnp.where(low, 0, last)
        other_mid = 3 - mid_of

        def send(src, dst, send_sem, recv_sem, axis, peer):
            return pltpu.make_async_remote_copy(
                src_ref=src,
                dst_ref=dst,
                send_sem=send_sem,
                recv_sem=recv_sem,
                device_id={axis: peer},
                device_id_type=MESH,
            )

        def chunk_at(i):
            return jnp.where(is_last, i, chunks - 1 - i)

        def load_w(c):
            return pltpu.make_async_copy(
                wq_hbm.at[:, pl.ds(pl.multiple_of(c * 2 * dim, 2 * dim), 2 * dim)],
                wq.at[c],
                wq_sem.at[c],
            )

        def load_k(g):
            return pltpu.make_async_copy(
                k_hbm.at[:, g * dim : (g + 1) * dim], kext.at[g, 0:span, :], k_sem.at[g]
            )

        def load_v(g):
            return pltpu.make_async_copy(
                v_hbm.at[:, g * dim : (g + 1) * dim], vext.at[g, 0:span, 0:dim], v_sem.at[g]
            )

        load_o = pltpu.make_async_copy(wo_hbm, wo, wo_sem)
        for i in range(chunks):
            load_w(chunk_at(i)).start()
        for g in range(kv_heads - 1, -1, -1):
            load_k(g).start()
            load_v(g).start()
        load_o.start()
        barrier = pltpu.get_barrier_semaphore()
        for axis, here, number in (("gy", me, count), ("gx", row, rows_gx)):
            for d in range(1, number):
                pl.semaphore_signal(
                    barrier, inc=1, device_id={axis: lax.rem(here + d, number)}, device_id_type=MESH
                )

        value = st_ref[...].astype(jnp.float32)
        value = value * lax.rsqrt(jnp.mean(value * value, -1, keepdims=True) + EPS)
        normed[...] = (value * ag_ref[...].reshape(1, model).astype(jnp.float32)).astype(jnp.bfloat16)
        mask = mask_ref[...]
        position = len_ref[0] + jnp.sum(mask, -1, keepdims=True) - 1
        place = lax.broadcasted_iota(jnp.int32, (tokens, dim), 1)
        half = lax.rem(place, dim // 2).astype(jnp.float32)
        angle = position.astype(jnp.float32) * jnp.exp(half * (-2.0 * THETA_LOG / dim))
        cos = jnp.cos(angle)
        sin = jnp.sin(angle)
        sin = jnp.where(place < dim // 2, -sin, sin)
        limit = len_ref[0] - me * span
        spot = lax.broadcasted_iota(jnp.int32, (1, span), 1)
        bias[...] = jnp.where(spot < limit, 0.0, NEG)
        allowed = jnp.logical_and(mask == 1, is_last)
        tree_bias[...] = jnp.full((tokens, lane), NEG, jnp.float32)
        tree_bias[:, 0:tokens] = jnp.where(allowed, 0.0, NEG)
        for g in range(kv_heads):
            kext[g, span : span + lane, :] = jnp.zeros((lane, dim), jnp.bfloat16)
            vext[g, span : span + lane, 0:dim] = jnp.zeros((lane, dim), jnp.bfloat16)
            vext[g, :, dim : 2 * dim] = jnp.ones((span + lane, dim), jnp.bfloat16)
        total[...] = st_ref[:, pl.ds(pl.multiple_of(me * cols, 128), cols)].astype(jnp.float32)
        q_gain_row = qg_ref[...].astype(jnp.float32)
        k_gain_row = kg_ref[...].astype(jnp.float32)

        def q_copy(k, c, peer):
            block = qall.at[pl.ds(2 * k, 2)]
            return send(block, block, q_s.at[peer, c], q_r.at[k], "gy", peer)

        relay = me == last - 1

        def direct(k, peer):
            far_pair = jnp.logical_and(me == 0, peer == last)
            there = jnp.logical_and(me != peer, jnp.logical_not(far_pair))
            return jnp.logical_and(there, 2 * k < heads)

        def relay_copy(k):
            return q_copy(k, chunks + k, last)

        pl.semaphore_wait(barrier, count + rows_gx - 2)

        def project_in(i, carry):
            c = chunk_at(i)
            load_w(c).wait()
            value = jnp.dot(normed[...], wq[c], preferred_element_type=jnp.float32)
            value = value.astype(jnp.bfloat16)
            k = me * chunks + c
            for j in range(2):
                head = 2 * k + j
                raw = value[:, j * dim : (j + 1) * dim]
                turned = raw.astype(jnp.float32)
                gain = jnp.where(head < heads, q_gain_row, k_gain_row)
                scale = lax.rsqrt(jnp.mean(turned * turned, -1, keepdims=True) + EPS)
                turned = turned * scale * gain
                turned = (turned * cos + pltpu.roll(turned, dim // 2, 1) * sin).astype(jnp.bfloat16)
                qall[head] = jnp.where(head < heads + kv_heads, turned, raw)
            for peer in range(count - 1, -1, -1):

                @pl.when(direct(k, peer))
                def _():
                    q_copy(k, c, peer).start()

            return carry

        lax.fori_loop(0, chunks, project_in, 0)

        def load_in(e):
            return pltpu.make_async_copy(w_hbm.at[e], wbuf.at[e], w_sem.at[e])

        def load_down(e):
            return pltpu.make_async_copy(d_hbm.at[e], dbuf.at[e], d_sem.at[e])

        for e in range(split):
            load_in(split + e).start()
            load_in(e).start()
        for e in range(split):
            load_down(split + e).start()
            load_down(e).start()

        names = rt_ref[...]
        shares = rw_ref[...]
        hits, weights = [], []
        for e in range(experts):
            matched = names == row * experts + e
            hits.append(jnp.sum(jnp.where(matched, 1.0, 0.0), 0, keepdims=True))
            weights.append(jnp.sum(jnp.where(matched, shares, 0.0), 0, keepdims=True))
        hit = jnp.concatenate(hits, 0)
        before = lax.broadcasted_iota(jnp.int32, (lane, lane), 0)
        after = lax.broadcasted_iota(jnp.int32, (lane, lane), 1)
        same = lax.div(before, tokens) == lax.div(after, tokens)
        earlier = jnp.where(jnp.logical_and(before < after, same), 1.0, 0.0).astype(jnp.bfloat16)
        rank = jnp.concatenate(
            [
                jnp.dot(
                    hit[:, i : i + lane].astype(jnp.bfloat16),
                    earlier,
                    preferred_element_type=jnp.float32,
                )
                for i in range(0, everyone, lane)
            ],
            1,
        )
        block_no = lax.div(lax.broadcasted_iota(jnp.int32, (experts, everyone), 1), tokens)
        first_slot = (lax.div(block_no, 2) * most_rows).astype(jnp.float32)
        slot_no = lax.broadcasted_iota(jnp.int32, (turn_slots, everyone), 0).astype(jnp.float32)
        for turn in range(2):
            here = jnp.logical_and(hit > 0.5, lax.rem(block_no, 2) == turn)
            slot_of = jnp.where(here, rank + first_slot, -1.0)
            for e in range(experts):
                chosen = slot_no == slot_of[e : e + 1]
                pick[turn, e] = jnp.where(chosen, 1.0, 0.0).astype(jnp.bfloat16)
                column = jnp.sum(jnp.where(chosen, weights[e], 0.0), 1, keepdims=True)
                wcol[turn, e] = jnp.broadcast_to(column, (turn_slots, lane))

        def akv_copy(d, peer):
            return send(akv, akv, a_s.at[d], a_r, "gy", peer)

        @pl.when(is_last)
        def _():
            pick = acc_ref[...].astype(jnp.bfloat16)
            akv[...] = jnp.zeros(akv.shape, jnp.bfloat16)
            for i in range(2 * kv_heads):
                akv[0:accepted, i * dim : (i + 1) * dim] = jnp.dot(
                    pick, qall[heads + i], preferred_element_type=jnp.float32
                ).astype(jnp.bfloat16)
            for d in range(last):
                akv_copy(d, d).start()
            for g in range(kv_heads):
                kext[g, span : span + tokens, :] = qall[heads + g]
                vext[g, span : span + tokens, 0:dim] = qall[heads + kv_heads + g]

        diagonal = lax.broadcasted_iota(jnp.int32, (tokens, lane), 0) == lax.broadcasted_iota(
            jnp.int32, (tokens, lane), 1
        )

        def as_row(column):
            return jnp.sum(jnp.where(diagonal, column, 0.0), 0, keepdims=True)

        def as_column(line):
            return jnp.sum(jnp.where(diagonal, line, 0.0), 1, keepdims=True)

        contract = (((1,), (1,)), ((), ()))

        def end_copy(s):
            return (
                send(end_out.at[s], end_in.at[s], e_s.at[s], e_r.at[s], "gy", mid_of),
                send(own_stat.at[s], stat_in.at[s], es_s.at[s], es_r.at[s], "gy", mid_of),
            )

        def mid_copy(s):
            return (
                send(mid_out.at[s], mid_in.at[s], m_s.at[s], m_r.at[s], "gy", other_mid),
                send(mstat_out.at[s], mstat_in.at[s], ms_s.at[s], ms_r.at[s], "gy", other_mid),
            )

        def block_of(s):
            return steps - 1 - s

        def final_copy(s):
            place = attn.at[pl.ds(block_of(s) * part, part)]
            return send(place, place, f_s.at[s], f_r.at[s], "gy", end_of)

        def attend(s):
            b = block_of(s)
            for n in range(part // 2):
                k = b * (part // 2) + n
                source = lax.div(k, chunks)
                relayed = jnp.logical_and(relay, source == 0)

                @pl.when(jnp.logical_and(source != me, jnp.logical_not(relayed)))
                def _():
                    q_copy(k, 0, source).wait_recv()

            g = lax.div(b * part, group)
            query = qall[pl.ds(b * part, part)].reshape(rows, dim)
            score = lax.dot_general(query, kext[g], contract, preferred_element_type=jnp.float32)
            cached = score[:, :span] + bias[...]
            tree = score[:, span:] + jnp.concatenate([tree_bias[...]] * part, 0)
            top = jnp.maximum(jnp.max(cached, 1, keepdims=True), jnp.max(tree, 1, keepdims=True))
            top = jnp.maximum(top, 0.5 * NEG)
            prob = jnp.concatenate(
                [
                    jnp.exp2((cached - top) * factor).astype(jnp.bfloat16),
                    jnp.exp2((tree - top) * factor).astype(jnp.bfloat16),
                ],
                1,
            )
            out = jnp.dot(prob, vext[g], preferred_element_type=jnp.float32)
            for j in range(part):
                here = slice(j * tokens, (j + 1) * tokens)
                own_stat[s, j : j + 1, :] = as_row(top[here])
                own_stat[s, part + j : part + j + 1, :] = as_row(out[here, dim:])

            @pl.when(is_end)
            def _():
                end_out[s] = out[:, :dim].astype(jnp.bfloat16)
                for copy in end_copy(s):
                    copy.start()

            @pl.when(is_mid)
            def _():
                own_acc[s] = out[:, :dim]

        def join(s):
            for copy in end_copy(s):
                copy.wait_recv()
            a, b = own_stat[s, :part, :], stat_in[s, :part, :]
            top = jnp.maximum(a, b)
            fa, fb = jnp.exp2((a - top) * factor), jnp.exp2((b - top) * factor)
            mstat_out[s, :part, :] = top
            mstat_out[s, part:, :] = own_stat[s, part:, :] * fa + stat_in[s, part:, :] * fb
            for j in range(part):
                here = slice(j * tokens, (j + 1) * tokens)
                value = own_acc[s, here, :] * as_column(fa[j : j + 1])
                value = value + end_in[s, here, :].astype(jnp.float32) * as_column(fb[j : j + 1])
                own_acc[s, here, :] = value
                mid_out[s, here, :] = value.astype(jnp.bfloat16)
            for copy in mid_copy(s):
                copy.start()

        def project_out(s):
            b = block_of(s)
            value = jnp.concatenate([attn[b * part + j] for j in range(part)], 1)
            weight = wo[pl.ds(pl.multiple_of(b * part * dim, part * dim), part * dim), :]
            total[...] += jnp.dot(value, weight, preferred_element_type=jnp.float32)

        def settle(s):
            for copy in mid_copy(s):
                copy.wait_recv()
            a, b = mstat_out[s, :part, :], mstat_in[s, :part, :]
            top = jnp.maximum(a, b)
            fa, fb = jnp.exp2((a - top) * factor), jnp.exp2((b - top) * factor)
            denom = mstat_out[s, part:, :] * fa + mstat_in[s, part:, :] * fb
            fa, fb = fa / denom, fb / denom
            for j in range(part):
                here = slice(j * tokens, (j + 1) * tokens)
                value = own_acc[s, here, :] * as_column(fa[j : j + 1])
                value = value + mid_in[s, here, :].astype(jnp.float32) * as_column(fb[j : j + 1])
                attn[block_of(s) * part + j] = value.astype(jnp.bfloat16)
            final_copy(s).start()
            project_out(s)

        for g in range(kv_heads):
            load_k(g).wait()
            load_v(g).wait()

        def step(t, carry):
            @pl.when(t < steps)
            def _():
                attend(t)

            k = chunks + first_relay - 1 - t

            @pl.when(jnp.logical_and(relay, jnp.logical_and(k >= 0, k < chunks)))
            def _():
                q_copy(k, 0, 0).wait_recv()
                relay_copy(k).start()

            @pl.when(t == 2)
            def _():
                load_o.wait()

            @pl.when(jnp.logical_and(is_mid, jnp.logical_and(t >= lag, t < steps + lag)))
            def _():
                join(t - lag)

            @pl.when(jnp.logical_and(is_mid, jnp.logical_and(t >= 2 * lag, t < steps + 2 * lag)))
            def _():
                settle(t - 2 * lag)

            @pl.when(jnp.logical_and(is_end, t >= 3 * lag))
            def _():
                final_copy(t - 3 * lag).wait_recv()
                project_out(t - 3 * lag)

            return carry

        lax.fori_loop(0, steps + 3 * lag, step, 0)
        h_all[row] = total[...].astype(jnp.bfloat16)

        pair = row + 1 - 2 * lax.rem(row, 2)

        def block_from(start, d):
            return lax.rem(start + rows_gx - d, rows_gx)

        def h_copy(d):
            place = h_all.at[row]
            return send(place, place, h_s.at[d], h_r.at[d], "gx", lax.rem(row + d, rows_gx))

        def pair_copy(d):
            place = h_all.at[block_from(row, d)]
            return send(place, place, h_s.at[d + 1], h_r.at[d + 1], "gx", pair)

        pair_copy(0).start()
        for d in sorted(range(2, rows_gx, 2), key=lambda d: abs(2 * d - rows_gx)):
            h_copy(d).start()

        @pl.when(is_last)
        def _():
            for d in range(last):
                akv_copy(d, d).wait_send()

        @pl.when(jnp.logical_not(is_last))
        def _():
            akv_copy(0, last).wait_recv()

        akv_ref[...] = akv[0:accepted, :]

        def sent(c, carry):
            k = me * chunks + c
            for peer in range(count):

                @pl.when(direct(k, peer))
                def _():
                    q_copy(k, c, peer).wait_send()

            return carry

        def relayed(k, carry):
            @pl.when(relay)
            def _():
                relay_copy(k).wait_send()

            return carry

        def done(s, carry):
            @pl.when(is_end)
            def _():
                for copy in end_copy(s):
                    copy.wait_send()

            @pl.when(is_mid)
            def _():
                for copy in mid_copy(s):
                    copy.wait_send()
                final_copy(s).wait_send()

            return carry

        gain = fg_ref[...].reshape(1, cols).astype(jnp.float32)

        def scale(source):
            scaled[source] = (h_all[source].astype(jnp.float32) * gain).astype(jnp.bfloat16)

        scale(row)
        for d in range(2, rows_gx, 2):
            h_copy(d).wait_recv()
            pair_copy(d).start()
            scale(block_from(row, d))
        for d in range(0, rows_gx, 2):
            pair_copy(d).wait_recv()
            scale(block_from(pair, d))
        square_of = lax.broadcasted_iota(jnp.int32, (lane, lane), 0) == lax.broadcasted_iota(
            jnp.int32, (lane, lane), 1
        )

        def multiply(h, s):
            e = h * split + s
            load_in(e).wait()
            value = jnp.dot(
                jnp.concatenate([pick[0, e], pick[1, e]], 0),
                scaled[...].reshape(everyone, cols),
                preferred_element_type=jnp.float32,
            ).astype(jnp.bfloat16)
            value = jnp.dot(value, wbuf[e], preferred_element_type=jnp.float32)
            for j in range(sub):
                c = j // turn_sub * turn_strips + s * turn_sub + j % turn_sub
                part_sum[h, c] = value[j * grain : (j + 1) * grain].astype(jnp.bfloat16)

        prev = lax.rem(me + count - 1, count)
        nxt = lax.rem(me + 1, count)
        at_low = me == 0
        at_high = is_last

        def rs_copy(h, c):
            return send(
                part_sum.at[h, c], rbuf.at[h, c], rs_s.at[h, c], rs_r.at[h, c], "gy",
                jnp.where(h == 1, nxt, prev),
            )

        first_h = jnp.where(low, 1, 0)
        multiply(first_h, 0)

        @pl.when(is_end)
        def _():
            for c in range(turn_sub):
                rs_copy(first_h, c).start()

        multiply(1 - first_h, 0)
        sq_out[...] = jnp.zeros(sq_out.shape, jnp.float32)
        for i in range(everyone // lane):
            value = h_all[pl.ds(i * (lane // tokens), lane // tokens)].reshape(lane, cols)
            value = value.astype(jnp.float32)
            column = jnp.sum(value * value, 1, keepdims=True)
            line = jnp.sum(jnp.where(square_of, column, 0.0), 0, keepdims=True)
            sq_out[0:1, i * lane : (i + 1) * lane] = line

        def sq_copy(d):
            return send(
                sq_out, sq_in.at[d], sq_s.at[d], sq_r.at[d], "gy", lax.rem(me + d, count)
            )

        for d in range(1, count):
            sq_copy(d).start()

        def finish_squares():
            whole = sq_out[0:1, :]
            for d in range(1, count):
                sq_copy(d).wait()
                whole = whole + sq_in[d, 0:1, :]
            inv_row[...] = lax.rsqrt(whole / model + EPS)

        def hid_copy(h, c):
            return send(
                hid.at[h, c], hid.at[h, c], hid_s.at[h, c], hid_r.at[h, c], "gy",
                prev if h else nxt,
            )

        def straight_copy(h, c, d):
            peer = lax.rem(me + (count - d if h else d), count)
            return send(
                hid.at[h, c], hid.at[h, c], st_s.at[h, c - chained, d], hid_r.at[h, c], "gy", peer
            )

        def ends(h):
            return (at_low, at_high) if h else (at_high, at_low)

        def reduce_strip(h, c):
            first, final = ends(h)

            @pl.when(jnp.logical_not(first))
            def _():
                rs_copy(h, c).wait_recv()

            @pl.when(jnp.logical_not(jnp.logical_or(first, final)))
            def _():
                part_sum[h, c] = (
                    part_sum[h, c].astype(jnp.float32) + rbuf[h, c].astype(jnp.float32)
                ).astype(jnp.bfloat16)

            begun = jnp.logical_and(first, c < turn_sub)

            @pl.when(jnp.logical_not(jnp.logical_or(final, begun)))
            def _():
                rs_copy(h, c).start()

            @pl.when(final)
            def _():
                turn = lax.div(c, turn_strips)
                e = h * split + lax.div(lax.rem(c, turn_strips), turn_sub)
                at = pl.multiple_of(lax.rem(c, turn_sub) * grain, grain)
                chosen = pick[turn, e, pl.ds(at, grain), :].astype(jnp.float32)
                inverse = jnp.sum(chosen * inv_row[...], 1, keepdims=True)
                summed = part_sum[h, c].astype(jnp.float32) + rbuf[h, c].astype(jnp.float32)
                gate = summed[:, :units] * inverse
                up = summed[:, units:] * inverse
                hid[h, c] = (gate / (1.0 + jnp.exp(-gate)) * up).astype(jnp.bfloat16)

                @pl.when(c < chained)
                def _():
                    hid_copy(h, c).start()

                @pl.when(c >= chained)
                def _():
                    for d in range(last, 0, -1):
                        straight_copy(h, c, d).start()

        def return_strip(h, c):
            first, final = ends(h)

            @pl.when(jnp.logical_not(final))
            def _():
                hid_copy(h, c).wait_recv()

            passed = jnp.logical_not(jnp.logical_or(first, final))

            @pl.when(jnp.logical_and(passed, c < chained))
            def _():
                hid_copy(h, c).start()

        def project_down(h, b):
            turn = lax.div(b, turn_strips)
            e = h * split + lax.div(lax.rem(b, turn_strips), turn_sub)

            @pl.when(turn == 0)
            def _():
                load_down(e).wait()

            value = hid[h, pl.ds(b + 1 - turn_sub, turn_sub)].reshape(turn_slots, units)
            value = jnp.dot(value, dbuf[e], preferred_element_type=jnp.float32)
            obuf[turn, e] = (value * wcol[turn, e, :, 0:1]).astype(jnp.bfloat16)

        def back_copy(d):
            peer = lax.rem(row + d, rows_gx)
            return send(pbuf.at[peer], ret.at[d], g_s.at[d], g_r.at[d], "gx", peer)

        def send_back(turn):
            summed = lax.dot_general(
                pick[turn].reshape(experts * turn_slots, everyone),
                obuf[turn].reshape(experts * turn_slots, cols),
                (((0,), (0,)), ((), ())),
                preferred_element_type=jnp.float32,
            )
            for p in range(turn, rows_gx, 2):
                pbuf[p] = summed[p * tokens : (p + 1) * tokens].astype(jnp.bfloat16)
            for d in sorted(range(1, rows_gx), key=lambda d: abs(2 * d - rows_gx)):

                @pl.when(lax.rem(row + d, 2) == turn)
                def _():
                    back_copy(d).start()

        home = turn_strips - 1 + 2 * far - hop * jnp.minimum(me, last - me)

        def moe_step(t, carry):
            for h, place in ((1, turn_sub // 2), (0, turn_sub - 1)):

                ready = jnp.logical_and(t < turn_strips - turn_sub, lax.rem(t, turn_sub) == place)

                @pl.when(ready)
                def _():
                    multiply(h, lax.div(t, turn_sub) + 1)

            @pl.when(t == far - 1)
            def _():
                finish_squares()

            for h in (1, 0):
                way = hop * (me if h else last - me)
                c = t - way

                @pl.when(jnp.logical_and(c >= 0, c < strips))
                def _():
                    reduce_strip(h, c)

            for h in (1, 0):
                way = hop * (me if h else last - me)
                b = t - 2 * far + way

                @pl.when(jnp.logical_and(b >= 0, b < strips))
                def _():
                    return_strip(h, b)

                    @pl.when(lax.rem(b, turn_sub) == turn_sub - 1)
                    def _():
                        project_down(h, b)

            @pl.when(t == home)
            def _():
                send_back(0)

            return carry

        lax.fori_loop(0, strips + 2 * far, moe_step, 0)

        def finish(c, carry):
            for h in (1, 0):
                first, final = ends(h)

                @pl.when(jnp.logical_not(final))
                def _():
                    rs_copy(h, c).wait_send()

                @pl.when(jnp.logical_and(jnp.logical_not(first), c < chained))
                def _():
                    hid_copy(h, c).wait_send()

                @pl.when(jnp.logical_and(final, c >= chained))
                def _():
                    for d in range(1, count):
                        straight_copy(h, c, d).wait_send()

            return carry

        send_back(1)
        moe = pbuf[row].astype(jnp.float32)
        lax.fori_loop(0, chunks, sent, 0)
        lax.fori_loop(0, chunks, relayed, 0)
        lax.fori_loop(0, steps, done, 0)
        lax.fori_loop(0, strips, finish, 0)
        for d in range(0, rows_gx, 2):
            pair_copy(d).wait_send()
            if d:
                h_copy(d).wait_send()
        for d in range(1, rows_gx):
            back_copy(d).wait_recv()
            moe = moe + ret[d].astype(jnp.float32)
        out_ref[...] = (h_all[row].astype(jnp.float32) + moe).astype(jnp.bfloat16)
        for d in range(1, rows_gx):
            back_copy(d).wait_send()

    pad = -accepted % 16
    vmem = pl.BlockSpec(memory_space=pltpu.VMEM)
    hbm = pl.BlockSpec(memory_space=pl.ANY)
    dma = pltpu.SemaphoreType.DMA
    stat = pltpu.VMEM((steps, 2 * part, lane), jnp.float32)
    piece = pltpu.VMEM((steps, rows, dim), jnp.bfloat16)
    return pl.pallas_call(
        kernel,
        out_shape=[
            jax.ShapeDtypeStruct((tokens, cols), jnp.bfloat16),
            jax.ShapeDtypeStruct((accepted, 2 * kv_cols), jnp.bfloat16),
        ],
        in_specs=[pl.BlockSpec(memory_space=pltpu.SMEM)] + [vmem] * 9 + [hbm] * 6,
        out_specs=[vmem, vmem],
        scratch_shapes=[
            pltpu.VMEM((tokens, model), jnp.bfloat16),
            pltpu.VMEM((chunks, model, 2 * dim), jnp.bfloat16),
            pltpu.VMEM((own * count, tokens, dim), jnp.bfloat16),
            pltpu.VMEM((kv_heads, span + lane, dim), jnp.bfloat16),
            pltpu.VMEM((kv_heads, span + lane, 2 * dim), jnp.bfloat16),
            pltpu.VMEM(w_o.shape, jnp.bfloat16),
            pltpu.VMEM((1, span), jnp.float32),
            pltpu.VMEM((tokens, lane), jnp.float32),
            pltpu.VMEM((steps, rows, dim), jnp.float32),
            stat,
            piece,
            piece,
            stat,
            piece,
            piece,
            stat,
            stat,
            pltpu.VMEM((heads, tokens, dim), jnp.bfloat16),
            pltpu.VMEM((tokens, cols), jnp.float32),
            pltpu.VMEM((accepted + pad, 2 * kv_cols), jnp.bfloat16),
            dma((chunks,)),
            dma((kv_heads,)),
            dma((kv_heads,)),
            dma,
            dma((count, 2 * chunks)),
            dma((count * chunks,)),
        ]
        + [dma((steps,))] * 10
        + [dma((last,)), dma, dma((rows_gx,)), dma((rows_gx,))]
        + [
            pltpu.VMEM((rows_gx, tokens, cols), jnp.bfloat16),
            pltpu.VMEM((rows_gx, tokens, cols), jnp.bfloat16),
            pltpu.VMEM((2, experts, turn_slots, everyone), jnp.bfloat16),
            pltpu.VMEM((2, experts, turn_slots, lane), jnp.float32),
            pltpu.VMEM((8, everyone), jnp.float32),
            pltpu.VMEM((count, 8, everyone), jnp.float32),
            pltpu.VMEM((1, everyone), jnp.float32),
            pltpu.VMEM((2, strips, grain, units), jnp.bfloat16),
            pltpu.VMEM((experts, depth, wide), jnp.bfloat16),
            pltpu.VMEM((experts, units, cols), jnp.bfloat16),
            pltpu.VMEM((2, strips, grain, wide), jnp.bfloat16),
            pltpu.VMEM((2, strips, grain, wide), jnp.bfloat16),
            pltpu.VMEM((2, experts, turn_slots, cols), jnp.bfloat16),
            pltpu.VMEM((rows_gx, tokens, cols), jnp.bfloat16),
            pltpu.VMEM((rows_gx, tokens, cols), jnp.bfloat16),
            dma((experts,)),
            dma((experts,)),
            dma((count,)),
            dma((count,)),
            dma((2, strips)),
            dma((2, strips)),
            dma((2, strips)),
            dma((2, strips)),
            dma((2, straight, count)),
            dma((rows_gx,)),
            dma((rows_gx,)),
        ],
        compiler_params=pltpu.CompilerParams(
            collective_id=cid, has_side_effects=True, vmem_limit_bytes=62 * 1024 * 1024
        ),
        name="layer_line",
    )(
        cache_len, states, attn_gain, q_gain, k_gain, tree_mask,
        accept, ffn_gain, routing, route_weight, w_qkv, cache_k, cache_v, w_o, w_in, w_down,
    )


def hand_over(first, second):
    def kernel(a_ref, b_ref, c_ref, d_ref):
        c_ref[...] = a_ref[...]
        d_ref[...] = b_ref[...]

    vmem = pl.BlockSpec(memory_space=pltpu.VMEM)
    return pl.pallas_call(
        kernel,
        out_shape=[
            jax.ShapeDtypeStruct(first.shape, first.dtype),
            jax.ShapeDtypeStruct(second.shape, second.dtype),
        ],
        in_specs=[vmem, vmem],
        out_specs=[vmem, vmem],
        name="hand_over",
    )(first, second)


def rms_scale(values, gain):
    return values * lax.rsqrt(jnp.mean(values * values, -1, keepdims=True) + EPS) * gain


def angles_of(position, dim):
    freqs = jnp.exp(jnp.arange(dim // 2, dtype=jnp.float32) * (-2.0 * THETA_LOG / dim))
    angles = position.astype(jnp.float32)[..., None] * freqs
    cosine = jnp.cos(angles)
    sine = jnp.sin(angles)
    return jnp.concatenate([cosine, cosine], -1), jnp.concatenate([-sine, sine], -1)


def body(
    states,
    attn_gain,
    w_qkv,
    q_gain,
    k_gain,
    cache_k,
    cache_v,
    cache_len,
    tree_mask,
    w_o,
    ffn_gain,
    routing,
    route_weight,
    w_in,
    w_down,
    accept,
):
    tok_rows, model_width = states.shape
    head_dim = q_gain.shape[0]
    kv_cols = cache_k.shape[2]
    heads_all = w_o.shape[0] // head_dim
    cache_span = cache_k.shape[1]
    cols_here = w_o.shape[1]
    col_index = lax.axis_index("gy")
    row_index = lax.axis_index("gx")
    count_gx = lax.axis_size("gx")
    count_gy = lax.axis_size("gy")
    own_heads = w_qkv.shape[1] // head_dim
    kv_heads = kv_cols // head_dim
    on_line = (
        count_gy == 4
        and w_qkv.shape[1] % (2 * head_dim) == 0
        and own_heads >= 2 * kv_heads
        and (own_heads - 2 * kv_heads) % 2 == 0
        and heads_all % (4 * kv_heads) == 0
        and tok_rows % 16 == 0
        and 128 % tok_rows == 0
        and routing.shape[0] % 128 == 0
        and w_in.shape[1] == w_o.shape[1]
        and (3 * routing.shape[0] * routing.shape[1] // (2 * w_in.shape[0] * lax.axis_size("gx"))) % 32 == 0
        and lax.axis_size("gx") % 2 == 0
    )
    if on_line:
        layer_out, accepted_kv = layer_line(
            states,
            attn_gain,
            w_qkv,
            q_gain[None],
            k_gain[None],
            cache_k[0],
            cache_v[0],
            cache_len,
            tree_mask[0],
            w_o,
            accept[0],
            ffn_gain,
            routing.T,
            route_weight.T,
            w_in,
            w_down,
            0,
        )
        layer_out, accepted_kv = hand_over(layer_out, accepted_kv)
        return (layer_out, accepted_kv[None])
    normed = rms_scale(states.astype(jnp.float32), attn_gain.astype(jnp.float32)).astype(
        jnp.bfloat16
    )
    qkv_part = jnp.dot(normed, w_qkv, preferred_element_type=jnp.float32).astype(jnp.bfloat16)
    (qkv_blocks,) = exchange([qkv_part], "gy", False, 0)
    qkv_whole = jnp.swapaxes(qkv_blocks, 0, 1).reshape(tok_rows, -1)
    q_cols = heads_all * head_dim
    depth = jnp.sum(tree_mask, -1) - 1
    cosine, sine = angles_of((cache_len[:, None] + depth)[0], head_dim)
    states_here = lax.dynamic_slice_in_dim(states, col_index * cols_here, cols_here, 1)
    gathered, k_rot = attention_block(
        qkv_whole,
        q_gain[None],
        k_gain[None],
        cosine,
        sine,
        cache_k[0],
        cache_v[0],
        cache_len - col_index * cache_span,
        tree_mask[0],
        states_here,
        w_o,
        1,
    )
    kv_new = jnp.concatenate([k_rot, qkv_whole[:, q_cols + kv_cols :]], -1)[None]
    accepted_kv = jnp.einsum(
        "rat,rtc->rac", accept.astype(jnp.bfloat16), kv_new, preferred_element_type=jnp.float32
    ).astype(jnp.bfloat16)
    resid = lax.dynamic_index_in_dim(gathered, row_index, 0, False)
    exp_here = w_in.shape[0]
    expert_count = exp_here * count_gx
    top_k = routing.shape[1]
    most_rows = 3 * tok_rows * top_k // (2 * expert_count)
    hidden_units = w_down.shape[1]
    gain_float = ffn_gain.astype(jnp.float32)
    tokens = routing.shape[0]
    slots = count_gx * most_rows
    own_experts = row_index * exp_here + jnp.arange(exp_here, dtype=jnp.int32)
    matched = routing[:, None, :] == own_experts[None, :, None]
    hits = jnp.any(matched, -1)
    weights = jnp.sum(jnp.where(matched, route_weight[:, None, :], 0.0), -1)
    order = jnp.arange(tok_rows, dtype=jnp.int32)
    earlier = (order[:, None] > order[None, :]).astype(jnp.bfloat16)
    rank = jnp.einsum(
        "tu,bue->bte",
        earlier,
        hits.astype(jnp.bfloat16).reshape(count_gx, tok_rows, exp_here),
        preferred_element_type=jnp.float32,
    ).astype(jnp.int32)
    first_slot = jnp.arange(count_gx, dtype=jnp.int32)[:, None, None] * most_rows
    slot_of = jnp.where(hits, (rank + first_slot).reshape(tokens, exp_here), -1)
    pick = slot_of.T[:, None, :] == jnp.arange(slots, dtype=jnp.int32)[None, :, None]
    pick_matrix = pick.astype(jnp.bfloat16)
    slot_weight = jnp.sum(jnp.where(pick, weights.T[:, None, :], 0.0), -1)
    gathered = gathered.reshape(tokens, cols_here).astype(jnp.float32)
    token_squares = jnp.sum(gathered * gathered, -1)
    slot_squares = jnp.sum(jnp.where(pick, token_squares, 0.0), -1)
    piece = 16
    slot_squares = jnp.pad(slot_squares.reshape(-1, piece), ((0, 0), (0, 128 - piece)))
    scaled = (gathered * gain_float).astype(jnp.bfloat16)
    rows = jnp.einsum(
        "est,td->esd", pick_matrix, scaled, preferred_element_type=jnp.float32
    ).astype(jnp.bfloat16)
    layer_out = expert_layer(
        rows,
        slot_squares,
        w_in,
        w_down,
        slot_weight[..., None],
        pick_matrix.reshape(exp_here * slots, tokens),
        resid,
        model_width,
        4,
    )
    return (layer_out, accepted_kv)


def solution(mesh):
    in_specs = (
        P("gx", None),
        P(),
        P(None, "gy"),
        P(),
        P(),
        P("gx", "gy", None),
        P("gx", "gy", None),
        P("gx"),
        P("gx", None, None),
        P(None, "gy"),
        P("gy"),
        P(),
        P(),
        P("gx", "gy", None),
        P("gx", None, "gy"),
        P("gx", None, None),
    )
    out_specs = (P("gx", "gy"), P("gx", None, None))
    return jax.shard_map(body, mesh=mesh, in_specs=in_specs, out_specs=out_specs, check_vma=False)
```
